256 devices in a mesh: cfg: 2 (over core), tok: 8 (over z), mlp: 16 (over x, y).
Axes of the slice: x: 4, y: 4, z: 8, core: 2. Of those that a mesh axis runs over, the one named last changes fastest.
Arguments:
- hidden: bfloat16 [2, 1536, 4, 3072], P('cfg', ('tok', 'mlp')), may hold values from -6 to 6
- latents: float32 [1536, 4, 64], P(('tok', 'mlp'), None, 'cfg'), may hold values from -6 to 6
- vec: float32 [2, 4, 3072], P('cfg'), may hold values from -9 to 9
- slot_token: int32 [4, 1536], replicated, may hold values from 0 to 1535, each once within a row
- text_len: int32 [2, 4], P('cfg'), may hold values from 64 to 512, as said below
- step_index: int32 [1], replicated, may hold values from 0 to 27
- guidance: float32 [1], replicated, may hold values from 2 to 5
- w_mod: bfloat16 [3072, 15360], P(None, ('tok', 'mlp')), may hold values from -0.109375 to 0.109375
- w_qkv: bfloat16 [1, 3072, 3, 2048], P(None, 'cfg', None, 'mlp'), may hold values from -0.109375 to 0.109375
- w_mlp_in: bfloat16 [1, 3072, 12288], P(None, 'cfg', 'mlp'), may hold values from -0.109375 to 0.109375
- qk_gain: float32 [1, 2, 128], replicated, may hold values from 1.5 to 2.5
- w_attn_out: bfloat16 [1, 2048, 3072], P(None, 'mlp', 'cfg'), may hold values from -0.125 to 0.125
- w_mlp_out: bfloat16 [1, 12288, 3072], P(None, 'mlp', 'cfg'), may hold values from -0.0546875 to 0.0546875
- w_final: bfloat16 [3072, 64], replicated, may hold values from -0.109375 to 0.109375
Outputs:
- velocity: float32 [1536, 4, 64], P(('tok', 'mlp'), None, 'cfg')
- latents_next: float32 [1536, 4, 64], P(('tok', 'mlp'), None, 'cfg')
- stream_out: bfloat16 [2, 1536, 4, 3072], P('cfg', ('tok', 'mlp'))
The draws below stay inside these ranges and needn't reach their ends.
Inputs may be any that keep to these rules, and one draw needn't show every extreme that they name: `text_len`: real text tokens of each request; its other text slots are padding; exactly one request has all 512. `slot_token`: row p lists the token held by each slot of request p: text tokens are 0 to 511, image tokens follow row by row on the 32 x 32 grid.
All inputs are finite; a program needn't handle non-finite values.
Results may differ from the reference program's by a relative error of at most 0.018.
Values may be sent and summed in bfloat16 or wider, within the bound.
A program may use at most 128 MiB of HBM per device.

```python
import math
import jax
import jax.numpy as jnp
from jax import lax

D = 3072
FF = 12288
HEAD_DIM = 128
CH = 64
HEADS = 16
LAYERS = 1
SIDE = 32
TXT = 512
STEPS = 28
PROMPTS = 4
S = 1536
MODS = 5
N_MLP = 16


def draw_text_len(key, part):
    lengths = jax.random.randint(key, (2 * PROMPTS,), TXT // 8, TXT)
    chosen = jax.random.randint(jax.random.fold_in(key, 7), (), 0, 2 * PROMPTS)
    lengths = jnp.where(jnp.arange(2 * PROMPTS) == chosen, TXT, lengths)
    return lengths.reshape(2, PROMPTS).astype(jnp.int32)


def steps_of(rng, dims, cuts, low, top_value):
    level, own = 1.0, jax.random.fold_in(rng, 6)
    for dim, blocks in cuts:
        steps = jnp.exp(jax.random.uniform(jax.random.fold_in(own, dim), (blocks,), jnp.float32, low / len(cuts), top_value / len(cuts)))
        level = level * jnp.repeat(steps, dims[dim] // blocks).reshape([-1 if axis == dim else 1 for axis in range(len(dims))])
    return level


def noise(rng, shape, scale, limit, cuts=(), dtype=jnp.bfloat16):
    loudness = steps_of(rng, shape, cuts, -0.22, 0.18) if cuts else 1.0
    entries = jax.random.normal(rng, shape, jnp.float32) * scale * loudness
    return jnp.minimum(jnp.maximum(entries, -limit), limit).astype(dtype)


def setup_inputs(seed: int = 0) -> dict:
    streams_of = jax.random.split(jax.random.key(seed), 15)
    hidden = noise(streams_of[0], (2, S, PROMPTS, D), 1.0, 6.0, ((0, 2), (1, 128)))
    latents = noise(streams_of[1], (S, PROMPTS, CH), 1.0, 6.0, ((0, 128), (2, 2)), jnp.float32)
    vec = noise(streams_of[2], (2, PROMPTS, D), 1.5, 9.0, ((0, 2),), jnp.float32)
    slot_token = jax.vmap(lambda own: jax.random.permutation(own, S))(jax.random.split(streams_of[3], PROMPTS)).reshape((PROMPTS, S)).astype(jnp.int32)
    text_len = draw_text_len(jax.random.fold_in(streams_of[14], 71), 0)
    step_index = jax.random.randint(streams_of[5], (1,), 0, STEPS).astype(jnp.int32)
    guidance = jnp.clip(jax.random.uniform(streams_of[6], (1,), jnp.float32, 2.0, 5.0), 2.0, 5.0)
    w_mod = noise(streams_of[7], (D, MODS * D), D ** -0.5, 0.109375, ((1, 128),))
    w_qkv = noise(streams_of[8], (LAYERS, D, 3, HEADS * HEAD_DIM), D ** -0.5, 0.109375, ((1, 2), (3, 16)))
    w_mlp_in = noise(streams_of[9], (LAYERS, D, FF), D ** -0.5, 0.109375, ((1, 2), (2, 16)))
    qk_gain = jnp.clip(jax.random.uniform(streams_of[10], (LAYERS, 2, HEAD_DIM), jnp.float32, 1.5, 2.5), 1.5, 2.5)
    w_attn_out = noise(streams_of[11], (LAYERS, HEADS * HEAD_DIM, D), (HEADS * HEAD_DIM) ** -0.5, 0.125, ((1, 16), (2, 2)))
    w_mlp_out = noise(streams_of[12], (LAYERS, FF, D), FF ** -0.5, 0.0546875, ((1, 16), (2, 2)))
    w_final = noise(streams_of[13], (D, CH), D ** -0.5, 0.109375)
    return dict(hidden=hidden, latents=latents, vec=vec, slot_token=slot_token, text_len=text_len, step_index=step_index, guidance=guidance, w_mod=w_mod, w_qkv=w_qkv, w_mlp_in=w_mlp_in, qk_gain=qk_gain, w_attn_out=w_attn_out, w_mlp_out=w_mlp_out, w_final=w_final)


EPSILON = 1e-06
ROPE_BASE = 10000.0
TIME_SHIFT = 3.0

def layer_norm(values):
    average = lax.optimization_barrier(jnp.mean(values, axis=-1, keepdims=True))
    centred = values - average
    spread = lax.optimization_barrier(jnp.mean(centred * centred, axis=-1, keepdims=True))
    return centred * lax.rsqrt(spread + EPSILON)

def rms_norm(values, gains):
    return values * lax.rsqrt(lax.optimization_barrier(jnp.mean(values * values, axis=-1, keepdims=True)) + EPSILON) * gains

def rope_table(tokens, head_size, text_count, side_count):
    pair_count = head_size // 2
    first_pairs = head_size // 16
    axis_pairs = (head_size - head_size // 8) // 4
    pair_index = jnp.arange(pair_count).astype(jnp.float32)
    in_rows = (pair_index >= first_pairs) & (pair_index < first_pairs + axis_pairs)
    in_cols = pair_index >= first_pairs + axis_pairs
    log_base = math.log(ROPE_BASE)
    freq_rows = jnp.where(in_rows, jnp.exp(-log_base * (pair_index - first_pairs) / axis_pairs), 0.0)
    freq_cols = jnp.where(in_cols, jnp.exp(-log_base * (pair_index - first_pairs - axis_pairs) / axis_pairs), 0.0)
    is_image = tokens >= text_count
    image_pos = jnp.where(is_image, tokens - text_count, 0).astype(jnp.int32)
    row_pos = (image_pos // side_count).astype(jnp.float32)
    col_pos = (image_pos % side_count).astype(jnp.float32)
    angles = row_pos[..., None] * freq_rows + col_pos[..., None] * freq_cols
    return (jnp.cos(angles), jnp.sin(angles))

def apply_rope(values, cosine, sine_table):
    even_part = values[..., 0::2]
    odd_part = values[..., 1::2]
    return jnp.concatenate([even_part * cosine - odd_part * sine_table, even_part * sine_table + odd_part * cosine], axis=-1)

def sigma_at(position, steps_total):
    remain = 1.0 - position / steps_total
    return TIME_SHIFT * remain / (1.0 + (TIME_SHIFT - 1.0) * remain)

def reference(hidden, latents, vec, slot_token, text_len, step_index, guidance, w_mod, w_qkv, w_mlp_in, qk_gain, w_attn_out, w_mlp_out, w_final):
    head_total = HEADS * HEAD_DIM
    head_cols = head_total // N_MLP
    unit_cols = FF // N_MLP
    slot_tokens = slot_token.T
    cosine, sine_table = rope_table(slot_tokens, HEAD_DIM, TXT, SIDE)
    is_image = slot_tokens >= TXT
    halves = []
    streams = []
    for half_idx in range(2):
        stream = hidden[half_idx]
        modulation = jnp.dot(jax.nn.silu(vec[half_idx]).astype(jnp.bfloat16), w_mod, preferred_element_type=jnp.float32)
        key_valid = (slot_token >= TXT) | (slot_token < text_len[half_idx][:, None])
        for layer_idx in range(LAYERS):
            offset_cols = 3 * layer_idx * D
            shift_mod = modulation[:, offset_cols:offset_cols + D]
            scale_mod = modulation[:, offset_cols + D:offset_cols + 2 * D]
            gate_mod = modulation[:, offset_cols + 2 * D:offset_cols + 3 * D]
            normed = (layer_norm(stream.astype(jnp.float32)) * (1.0 + scale_mod[None]) + shift_mod[None]).astype(jnp.bfloat16)
            flattened = normed.reshape(S * PROMPTS, D)
            projected = jnp.dot(flattened, w_qkv[layer_idx].reshape(D, 3 * head_total), preferred_element_type=jnp.float32)
            projected = projected.reshape(S, PROMPTS, 3, HEADS, HEAD_DIM)
            unit_pre = jnp.dot(flattened, w_mlp_in[layer_idx], preferred_element_type=jnp.float32)
            queries = apply_rope(rms_norm(projected[:, :, 0], qk_gain[layer_idx, 0]), cosine[:, :, None], sine_table[:, :, None]).astype(jnp.bfloat16)
            keys_rot = apply_rope(rms_norm(projected[:, :, 1], qk_gain[layer_idx, 1]), cosine[:, :, None], sine_table[:, :, None]).astype(jnp.bfloat16)
            values = projected[:, :, 2].astype(jnp.bfloat16)
            queries = lax.optimization_barrier(queries).astype(jnp.float32)
            keys_rot = lax.optimization_barrier(keys_rot).astype(jnp.float32)
            values = lax.optimization_barrier(values).astype(jnp.float32)
            activation = jax.nn.gelu(unit_pre, approximate=True).astype(jnp.bfloat16)
            outputs = []
            for prompt_idx in range(PROMPTS):
                scores = jnp.einsum('she,the->hst', queries[:, prompt_idx], keys_rot[:, prompt_idx]) / math.sqrt(HEAD_DIM)
                softened = jnp.exp(scores) * key_valid[prompt_idx][None, None, :].astype(jnp.float32)
                rounded = lax.optimization_barrier(softened.astype(jnp.bfloat16)).astype(jnp.float32)
                numerator = jnp.einsum('hst,the->she', rounded, values[:, prompt_idx])
                denominator = lax.optimization_barrier(jnp.sum(softened, axis=-1))
                outputs.append((numerator / denominator.T[:, :, None]).astype(jnp.bfloat16))
            attended = jnp.stack(outputs, axis=1).reshape(S * PROMPTS, head_total)
            branch_out = jnp.zeros((S * PROMPTS, D), jnp.float32)
            for shard_idx in range(N_MLP):
                head_lo = shard_idx * head_cols
                unit_lo = shard_idx * unit_cols
                shard_term = jnp.dot(attended[:, head_lo:head_lo + head_cols], w_attn_out[layer_idx, head_lo:head_lo + head_cols], preferred_element_type=jnp.float32)
                shard_term = shard_term + jnp.dot(activation[:, unit_lo:unit_lo + unit_cols], w_mlp_out[layer_idx, unit_lo:unit_lo + unit_cols], preferred_element_type=jnp.float32)
                branch_out = branch_out + lax.optimization_barrier(shard_term.astype(jnp.bfloat16)).astype(jnp.float32)
            stream = (stream.astype(jnp.float32) + gate_mod[None] * branch_out.reshape(S, PROMPTS, D)).astype(jnp.bfloat16)
        streams.append(stream)
        final_lo = 3 * LAYERS * D
        final_shift = modulation[:, final_lo:final_lo + D]
        final_scale = modulation[:, final_lo + D:final_lo + 2 * D]
        final_normed = (layer_norm(stream.astype(jnp.float32)) * (1.0 + final_scale[None]) + final_shift[None]).astype(jnp.bfloat16)
        half_velocity = jnp.dot(final_normed.reshape(S * PROMPTS, D), w_final, preferred_element_type=jnp.float32).reshape(S, PROMPTS, CH)
        halves.append(jnp.where(is_image[:, :, None], half_velocity, 0.0))
    velocity = halves[1] + guidance[0] * (halves[0] - halves[1])
    current = step_index[0].astype(jnp.float32)
    step_size = sigma_at(current + 1.0, STEPS) - sigma_at(current, STEPS)
    return (velocity, latents + step_size * velocity, jnp.stack(streams, axis=0))
```

```python
import math

import jax
import jax.numpy as jnp
from jax import lax
from jax.experimental import pallas as pl
from jax.experimental.pallas import tpu as pltpu
from jax.sharding import PartitionSpec as P

SIDE = 32
TXT = 512
STEPS = 28
EPSILON = 1e-06
ROPE_BASE = 10000.0
TIME_SHIFT = 3.0

MESH = pl.DeviceIdType.MESH
F32 = jnp.float32
BF16 = jnp.bfloat16

D = 3072
HALF = D // 2
HEAD = 128
UNITS = 768
PROMPTS = 4
RING = 4
TOKS = 8
MLPS = 16
PIECE = 24
CHUNK = RING * PIECE
STAGE = 2 * CHUNK
SLOTS = 192
ROWS_OWN = 2 * PIECE
MOD_COLS = 120
CH_HALF = 32


def sigma_at(position, steps_total):
    remain = 1.0 - position / steps_total
    return TIME_SHIFT * remain / (1.0 + (TIME_SHIFT - 1.0) * remain)


def layer_norm(values):
    average = jnp.mean(values, axis=-1, keepdims=True)
    centred = values - average
    spread = jnp.mean(centred * centred, axis=-1, keepdims=True)
    return centred * lax.rsqrt(spread + EPSILON)


def dot_f32(a, b):
    return jnp.dot(a, b, preferred_element_type=F32)


def dot_t(a, b):
    return lax.dot_general(a, b, (((1,), (1,)), ((), ())), preferred_element_type=F32)


def kernel(
    hid_ref, lat_ref, vec_ref, cos_ref, sin_ref, mask_ref, image_ref, scal_ref, gain_ref,
    wmod_hbm, wqkv_hbm, wmi_hbm, wao_hbm, wmo_hbm, wfin_hbm,
    vel_ref, latn_ref, stream_ref,
    X, N, WMOD, WQKV, WMI, WAO, WMO, WFIN, G, MOD, QF, ST, R, OS, OR, ATT,
    ACT, ACC, PS, RB, RC, PS2, RB2, RC2, VS, VR,
    ag_s, ag_r, rs_s, rs_r, w_l, w_s, w_r, m_s, m_r, z_s, z_r, o_s, o_r, v_s, v_r,
):
    c = lax.axis_index("cfg")
    t = lax.axis_index("tok")
    m = lax.axis_index("mlp")
    x, y = m // RING, m % RING
    uv = ((x, y), (y, x))

    def at_uv(k, u, v):
        return u * RING + v if k == 0 else v * RING + u

    def remote(src, dst, ssem, rsem, **where):
        return pltpu.make_async_remote_copy(
            src_ref=src, dst_ref=dst, send_sem=ssem, recv_sem=rsem,
            device_id=where, device_id_type=MESH,
        )

    barrier = pltpu.get_barrier_semaphore()
    for d in range(1, MLPS):
        pl.semaphore_signal(barrier, inc=1, device_id={"mlp": (m + d) % MLPS}, device_id_type=MESH)
    for d in range(1, TOKS):
        pl.semaphore_signal(barrier, inc=1, device_id={"tok": (t + d) % TOKS}, device_id_type=MESH)
    pl.semaphore_signal(barrier, inc=1, device_id={"cfg": 1 - c}, device_id_type=MESH)

    wmod_copy = pltpu.make_async_copy(wmod_hbm, WMOD, w_l.at[0])
    wmod_copy.start()
    k_rows = pl.ds(pl.multiple_of(c * HALF, HALF), HALF)
    weights = (
        [(wqkv_hbm.at[j], WQKV.at[k_rows, pl.ds(j * HEAD, HEAD)]) for j in range(3)]
        + [(wmi_hbm, WMI.at[k_rows]), (wao_hbm, WAO.at[c]), (wmo_hbm, WMO.at[c])]
    )
    local_w = [pltpu.make_async_copy(s, d, w_l.at[1 + i]) for i, (s, d) in enumerate(weights)]
    remote_w = [remote(s, d, w_s.at[i], w_r.at[i], cfg=1 - c) for i, (s, d) in enumerate(weights)]
    fin_copy = pltpu.make_async_copy(wfin_hbm, WFIN, w_l.at[7])

    normed = layer_norm(hid_ref[...].astype(F32)).astype(BF16)
    X[0, y, x] = normed[:PIECE]
    X[1, x, y] = normed[PIECE:]
    pl.semaphore_wait(barrier, MLPS - 1 + TOKS - 1 + 1)

    lo, hi = pl.ds(0, HALF), pl.ds(HALF, HALF)

    def order_u(u, j):
        return (u, (u + 3) % RING, (u + 1) % RING, (u + 2) % RING)[j]

    def ag(k, i):
        u, v = uv[k]
        sems = (ag_s.at[k, i], ag_r.at[k, i])
        up, um = {"mlp": at_uv(k, (u + 1) % RING, v)}, {"mlp": at_uv(k, (u + 3) % RING, v)}
        vp, vm = {"mlp": at_uv(k, u, (v + 1) % RING)}, {"mlp": at_uv(k, u, (v + 3) % RING)}
        if i < 2:
            block = X.at[k, v, u]
            return remote(block, block, *sems, **(up if i == 0 else um))
        if i < 4:
            block = X.at[k, v, (u + (3 if i == 2 else 1)) % RING, :, lo if i == 2 else hi]
            return remote(block, block, *sems, **(up if i == 2 else um))
        if i < 12:
            j, d = (i - 4) // 2, (i - 4) % 2
            block = X.at[k, v, order_u(u, j)]
            return remote(block, block, *sems, **(vp if d == 0 else vm))
        j, d = (i - 12) // 2, (i - 12) % 2
        block = X.at[k, (v + (3 if d == 0 else 1)) % RING, order_u(u, j), :, lo if d == 0 else hi]
        return remote(block, block, *sems, **(vp if d == 0 else vm))

    def ag_start(ids):
        for i in ids:
            for k in range(2):
                ag(k, i).start()

    def ag_recv(ids):
        for i in ids:
            for k in range(2):
                ag(k, i).wait_recv()

    ag_start((0, 1))
    for copy in local_w[:3]:
        copy.start()
    for copy in remote_w[:3]:
        copy.start()
    for i in range(3, 6):
        local_w[i].start()
        remote_w[i].start()
    fin_copy.start()
    ag_start((4, 5))

    wmod_copy.wait()
    vec = vec_ref[...]
    silu_vec = (vec * (1.0 / (1.0 + jnp.exp(-vec)))).astype(BF16)
    G[t, m, :, 0:MOD_COLS] = dot_t(silu_vec, WMOD[...])
    mod1 = [
        remote(G.at[t, m], G.at[t, m], m_s.at[0], m_r.at[0], tok=(t + d) % TOKS) for d in range(1, TOKS)
    ]
    for copy in mod1:
        copy.start()

    ag_recv((0, 1))
    ag_start((2, 3, 6, 7, 8, 9))

    span1 = remote(G.at[pl.ds(0, TOKS - 1), m], G.at[pl.ds(0, TOKS - 1), m], m_s.at[0], m_r.at[0], tok=(t + 1) % TOKS)
    span1.wait_recv()
    mod2 = [
        remote(G.at[:, m], G.at[:, m], m_s.at[1], m_r.at[1], mlp=(m + d) % MLPS) for d in range(1, MLPS)
    ]
    for copy in mod2:
        copy.start()

    ag_recv((2, 3))
    ag_start((10, 11))

    for copy in local_w[:3]:
        copy.wait()
    for copy in remote_w[:3]:
        copy.wait_recv()
    src_col = lax.broadcasted_iota(jnp.int32, (HEAD, HEAD), 0)
    out_col = lax.broadcasted_iota(jnp.int32, (HEAD, HEAD), 1)
    wanted = jnp.where(out_col < HEAD // 2, 2 * out_col, 2 * out_col - HEAD + 1)
    permute = jnp.where(src_col == wanted, 1.0, 0.0).astype(BF16)

    def permute_step(i, carry):
        rows = pl.ds(pl.multiple_of(i * 512, 512), 512)
        for j in range(2):
            cols = pl.ds(j * HEAD, HEAD)
            WQKV[rows, cols] = dot_f32(WQKV[rows, cols], permute).astype(BF16)
        return carry

    lax.fori_loop(0, D // 512, permute_step, 0)

    span2 = remote(
        G.at[:, pl.ds(0, MLPS - 1)], G.at[:, pl.ds(0, MLPS - 1)], m_s.at[1], m_r.at[1], mlp=(m + 1) % MLPS
    )
    span2.wait_recv()
    lane = lax.broadcasted_iota(jnp.int32, (PROMPTS, 128), 1)

    def mod_step(i, carry):
        base = pl.multiple_of(i * (MLPS * MOD_COLS), 128)
        for j in range(15):
            shift = (8 * j) % MOD_COLS
            first = G[i, j]
            if shift:
                first = pltpu.roll(first, 128 - shift, 1)
            second = pltpu.roll(G[i, j + 1], MOD_COLS - shift, 1)
            both = jnp.where(lane < MOD_COLS - shift, first, second)
            MOD[:, pl.ds(base + j * 128, 128)] = jnp.concatenate([both, both], axis=0)
        return carry

    lax.fori_loop(0, TOKS, mod_step, 0)

    for i in range(3, 4):
        local_w[i].wait()
        remote_w[i].wait_recv()

    offsets = (0, 1, 3, 2)

    def chunk_of(s, k):
        return (uv[k][1] + offsets[s]) % RING

    def modulate(s):
        def step(i, carry):
            cols = pl.ds(pl.multiple_of(i * 256, 256), 256)
            scale = 1.0 + MOD[:, pl.ds(pl.multiple_of(D + i * 256, 256), 256)]
            shift = MOD[:, cols]
            for k in range(2):
                ch = chunk_of(s, k)
                for half in range(2):
                    pieces = [X[k, ch, half * 2 + q, :, cols].astype(F32).reshape(3, 8, 256) for q in range(2)]
                    both = jnp.concatenate(pieces, axis=0) * scale[None] + shift[None]
                    N[k * CHUNK + half * 48 : k * CHUNK + half * 48 + 48, cols] = both.reshape(48, 256).astype(BF16)
            return carry

        lax.fori_loop(0, D // 256, step, 0)

    soft_scale = math.log2(math.e) / math.sqrt(HEAD)

    def qkv(s):
        pre = dot_f32(N[...], WQKV[...])
        for j in range(3):
            QF[j] = pre[:, j * HEAD : (j + 1) * HEAD]
        cha, chb = chunk_of(s, 0), chunk_of(s, 1) + RING
        for p in range(PROMPTS):
            rows = pl.ds(p, 2 * PIECE, stride=PROMPTS)
            cosine = jnp.concatenate([cos_ref[p, cha], cos_ref[p, chb]], axis=0)
            sine = jnp.concatenate([sin_ref[p, cha], sin_ref[p, chb]], axis=0)
            outs = []
            for j in range(2):
                val = QF.at[j][rows, :]
                val = val * lax.rsqrt(jnp.mean(val * val, axis=-1, keepdims=True) + EPSILON) * gain_ref[j : j + 1, :]
                outs.append((val * cosine + pltpu.roll(val, HEAD // 2, 1) * sine).astype(BF16))
            outs.append(QF.at[2][rows, :].astype(BF16))
            for place, val in ((0, outs[1]), (1, outs[2]), (2, outs[0])):
                ST[p, cha, place] = val[:PIECE]
                ST[p, chb, place] = val[PIECE:]

    def job(i):
        p = (t // 2 + i) % PROMPTS
        rel = (t - 2 * p + TOKS) % TOKS
        half = 1 - ((rel + 7) % TOKS) // RING
        return p, 2 * p + half, 2 * p + 1 - half

    kv = pl.ds(0, 2)

    def send_stage(s):
        for ch in (chunk_of(s, 0), chunk_of(s, 1) + RING):
            for i in range(PROMPTS):
                p, z_query, z_other = job(i)
                if i == 0:
                    pltpu.make_async_copy(ST.at[p, ch], R.at[t, ch], z_r.at[t]).start()
                else:
                    remote(ST.at[p, ch], R.at[t, ch], z_s.at[i, 0], z_r.at[t], tok=z_query).start()
                remote(ST.at[p, ch, kv], R.at[t, ch, kv], z_s.at[i, 1], z_r.at[t], tok=z_other).start()

    def units(s):
        def step(i, carry):
            cols = pl.ds(pl.multiple_of(i * 256, 256), 256)
            ACT[s, :, cols] = jax.nn.gelu(dot_f32(N[...], WMI[:, cols]), approximate=True).astype(BF16)
            return carry

        lax.fori_loop(0, UNITS // 256, step, 0)

    def units_out(s):
        def step(i, carry):
            cols = pl.ds(pl.multiple_of(i * 256, 256), 256)
            for h in range(2):
                ACC[s, h, :, cols] = dot_f32(ACT[s], WMO[h, :, cols])
            return carry

        lax.fori_loop(0, HALF // 256, step, 0)

    modulate(0)
    qkv(0)
    send_stage(0)
    ag_recv((4, 5))
    ag_start((12, 13))
    units(0)
    ag_recv((6, 7))
    ag_start((14, 15))
    for i in range(4, 6):
        local_w[i].wait()
        remote_w[i].wait_recv()
    ag_recv((8, 9))
    ag_start((16, 17))
    ag_recv((10, 11))
    ag_start((18, 19))
    for s in (1, 2):
        modulate(s)
        qkv(s)
        send_stage(s)
        units(s)
    ag_recv(range(12, 20))
    modulate(3)
    qkv(3)
    send_stage(3)
    units(3)
    for s in range(4):
        units_out(s)

    sign = 1 - 2 * (t % 2)

    def tile(o):
        return (t + TOKS - sign * o) % TOKS

    pltpu.make_async_copy(ST.at[0], R.at[t], z_r.at[t]).wait()
    for o in range(1, TOKS):
        src = tile(o)
        if o < RING:
            remote(R.at[src], R.at[src], z_s.at[0, 0], z_r.at[src], tok=(t + 1) % TOKS).wait_recv()
        else:
            part = R.at[src, :, kv]
            remote(part, part, z_s.at[0, 0], z_r.at[src], tok=(t + 1) % TOKS).wait_recv()
    own_p = t // 2

    def attend(o):
        keys = R[:, :, 0].reshape(TOKS * SLOTS, HEAD)
        vals = R[:, :, 1].reshape(TOKS * SLOTS, HEAD)
        query = R[tile(o), :, 2].reshape(SLOTS, HEAD)
        soft = jnp.exp2(dot_t(query, keys) * soft_scale) * mask_ref[...]
        total = jnp.sum(soft, axis=-1, keepdims=True)
        return (dot_f32(soft.astype(BF16), vals) / total).astype(BF16)

    for o in range(1, RING):
        OS[o] = attend(o)
        remote(OS.at[o], OR.at[own_p], o_s.at[o], o_r.at[own_p], tok=tile(o)).start()
    OR[own_p] = attend(0)

    for i in range(1, PROMPTS):
        p, z_query, _ = job(i)
        remote(OS.at[0], OR.at[p], o_s.at[0], o_r.at[p], tok=z_query).wait_recv()
    for p in range(PROMPTS):
        ATT[pl.ds(p, SLOTS, stride=PROMPTS), :] = OR[p].astype(F32)

    def out_stage(s):
        rows = [
            ATT[pl.ds(pl.multiple_of((k * RING + chunk_of(s, k)) * CHUNK, CHUNK), CHUNK), :] for k in range(2)
        ]
        att = jnp.concatenate(rows, axis=0).astype(BF16)
        for h in range(2):
            for n in range(HALF // 512):
                cols = slice(n * 512, (n + 1) * 512)
                part = dot_f32(att, WAO[h, :, cols]) + ACC[s, h, :, cols]
                for k in range(2):
                    for u in range(RING):
                        first = k * CHUNK + u * PIECE
                        PS[k, chunk_of(s, k), u, :, h * HALF + n * 512 : h * HALF + (n + 1) * 512] = part[
                            first : first + PIECE
                        ].astype(BF16)

    def back_u(u, j):
        return (u + (2, 1, 3, 0)[j]) % RING

    def rs(k, i):
        u, v = uv[k]
        sems = (rs_s.at[k, i], rs_r.at[k, i])
        up, um = {"mlp": at_uv(k, (u + 1) % RING, v)}, {"mlp": at_uv(k, (u + 3) % RING, v)}
        vp, vm = {"mlp": at_uv(k, u, (v + 1) % RING)}, {"mlp": at_uv(k, u, (v + 3) % RING)}
        if i < 16:
            j, d = (i % 8) // 2, i % 2
            where = vp if d == 0 else vm
            if i < 8:
                block = PS.at[k, (v + 2) % RING, back_u(u, j), :, lo if d == 0 else hi]
                return remote(block, RB.at[k, d, j], *sems, **where)
            block = PS.at[k, (v + (1 if d == 0 else 3)) % RING, back_u(u, j)]
            return remote(block, RC.at[k, d, j], *sems, **where)
        d = i % 2
        where = up if d == 0 else um
        if i < 18:
            return remote(PS2.at[k, 0, :, lo if d == 0 else hi], RB2.at[k, d], *sems, **where)
        return remote(PS2.at[k, 1 + d], RC2.at[k, d], *sems, **where)

    out_stage(3)
    for i in range(8):
        for k in range(2):
            rs(k, i).start()
    out_stage(1)
    out_stage(2)
    for j in range(RING):
        for d in range(2):
            for k in range(2):
                u, v = uv[k]
                rs(k, 2 * j + d).wait_recv()
                cols = slice(0, HALF) if d == 0 else slice(HALF, D)
                ch = (v + (1 if d == 0 else 3)) % RING
                PS[k, ch, back_u(u, j), :, cols] = (
                    PS[k, ch, back_u(u, j), :, cols].astype(F32) + RB[k, d, j].astype(F32)
                ).astype(BF16)
                rs(k, 8 + 2 * j + d).start()
    out_stage(0)

    def own_sum(k, j):
        u, v = uv[k]
        for d in range(2):
            rs(k, 8 + 2 * j + d).wait_recv()
        return PS[k, v, back_u(u, j)].astype(F32) + RC[k, 0, j].astype(F32) + RC[k, 1, j].astype(F32)

    for k in range(2):
        PS2[k, 0] = own_sum(k, 0).astype(BF16)
        rs(k, 16).start()
        rs(k, 17).start()
    for d in range(2):
        for k in range(2):
            total = own_sum(k, 1 + d)
            rs(k, 16 + d).wait_recv()
            cols = slice(0, HALF) if d == 0 else slice(HALF, D)
            PS2[k, 1 + d] = total.astype(BF16)
            PS2[k, 1 + d, :, cols] = (total[:, cols] + RB2[k, d].astype(F32)).astype(BF16)
            rs(k, 18 + d).start()
    fin_copy.wait()
    finals = []
    for k in range(2):
        branch = own_sum(k, 3)
        for d in range(2):
            rs(k, 18 + d).wait_recv()
        branch = branch + RC2[k, 0].astype(F32) + RC2[k, 1].astype(F32)
        rows = slice(k * PIECE, (k + 1) * PIECE)
        gated = branch.reshape(3, 8, D) * MOD[:, 2 * D : 3 * D][None]
        stream = (hid_ref[rows, :].astype(F32) + gated.reshape(PIECE, D)).astype(BF16)
        stream_ref[rows, :] = stream
        shaped = layer_norm(stream.astype(F32)).reshape(3, 8, D)
        shaped = shaped * (1.0 + MOD[:, 4 * D : 5 * D])[None] + MOD[:, 3 * D : 4 * D][None]
        finals.append(shaped.reshape(PIECE, D).astype(BF16).astype(F32))
    final_normed = jnp.concatenate(finals, axis=0).astype(BF16)
    half_velocity = dot_t(final_normed, WFIN[...])
    parts = (half_velocity[:, :CH_HALF] * image_ref[...], half_velocity[:, CH_HALF:] * image_ref[...])
    first = c == 0
    VS[...] = jnp.where(first, parts[1], parts[0])
    swap = remote(VS, VR, v_s, v_r, cfg=1 - c)
    swap.start()
    own = jnp.where(first, parts[0], parts[1])
    swap.wait_recv()
    other = VR[...]
    cond = jnp.where(first, own, other)
    uncond = jnp.where(first, other, own)
    velocity = uncond + scal_ref[0:1, :] * (cond - uncond)
    vel_ref[...] = velocity
    latn_ref[...] = lat_ref[...] + scal_ref[1:2, :] * velocity

    swap.wait_send()
    for copy in remote_w:
        copy.wait_send()
    span1.wait_send()
    span2.wait_send()
    for k in range(2):
        for i in range(20):
            ag(k, i).wait_send()
            rs(k, i).wait_send()
    for i in range(PROMPTS):
        p, z_query, z_other = job(i)
        if i:
            remote(ST.at[p], R.at[t], z_s.at[i, 0], z_r.at[t], tok=z_query).wait_send()
        remote(ST.at[p, :, kv], R.at[t, :, kv], z_s.at[i, 1], z_r.at[t], tok=z_other).wait_send()
    for o in range(1, RING):
        remote(OS.at[o], OR.at[own_p], o_s.at[o], o_r.at[own_p], tok=tile(o)).wait_send()


def call_kernel(*operands):
    vmem = pl.BlockSpec(memory_space=pltpu.VMEM)
    hbm = pl.BlockSpec(memory_space=pl.ANY)
    dma = pltpu.SemaphoreType.DMA
    scratch = [
        pltpu.VMEM((2, RING, RING, PIECE, D), BF16),
        pltpu.VMEM((STAGE, D), BF16),
        pltpu.VMEM((MOD_COLS, D), BF16),
        pltpu.VMEM((D, 3 * HEAD), BF16),
        pltpu.VMEM((D, UNITS), BF16),
        pltpu.VMEM((2, HEAD, HALF), BF16),
        pltpu.VMEM((2, UNITS, HALF), BF16),
        pltpu.VMEM((2 * CH_HALF, D), BF16),
        pltpu.VMEM((TOKS, MLPS, PROMPTS, 128), F32),
        pltpu.VMEM((8, 5 * D), F32),
        pltpu.VMEM((3, STAGE, HEAD), F32),
        pltpu.VMEM((PROMPTS, 2 * RING, 3, PIECE, HEAD), BF16),
        pltpu.VMEM((TOKS, 2 * RING, 3, PIECE, HEAD), BF16),
        pltpu.VMEM((RING, SLOTS, HEAD), BF16),
        pltpu.VMEM((PROMPTS, SLOTS, HEAD), BF16),
        pltpu.VMEM((PROMPTS * SLOTS, HEAD), F32),
        pltpu.VMEM((RING, STAGE, UNITS), BF16),
        pltpu.VMEM((RING, 2, STAGE, HALF), F32),
        pltpu.VMEM((2, RING, RING, PIECE, D), BF16),
        pltpu.VMEM((2, 2, RING, PIECE, HALF), BF16),
        pltpu.VMEM((2, 2, RING, PIECE, D), BF16),
        pltpu.VMEM((2, 3, PIECE, D), BF16),
        pltpu.VMEM((2, 2, PIECE, HALF), BF16),
        pltpu.VMEM((2, 2, PIECE, D), BF16),
        pltpu.VMEM((ROWS_OWN, CH_HALF), F32),
        pltpu.VMEM((ROWS_OWN, CH_HALF), F32),
        dma((2, 20)), dma((2, 20)), dma((2, 20)), dma((2, 20)),
        dma((8,)), dma((6,)), dma((6,)), dma((2,)), dma((2,)),
        dma((PROMPTS, 2)), dma((TOKS,)), dma((RING,)), dma((PROMPTS,)), dma, dma,
    ]
    return pl.pallas_call(
        kernel,
        out_shape=(
            jax.ShapeDtypeStruct((ROWS_OWN, CH_HALF), F32),
            jax.ShapeDtypeStruct((ROWS_OWN, CH_HALF), F32),
            jax.ShapeDtypeStruct((ROWS_OWN, D), BF16),
        ),
        in_specs=[vmem] * 9 + [hbm] * 6,
        out_specs=(vmem, vmem, vmem),
        scratch_shapes=scratch,
        compiler_params=pltpu.CompilerParams(
            collective_id=0, has_side_effects=True, vmem_limit_bytes=67043328
        ),
    )(*operands)


def rope_tables(tokens):
    pair_count = HEAD // 2
    first_pairs = HEAD // 16
    axis_pairs = (HEAD - HEAD // 8) // 4
    pair_index = (jnp.arange(HEAD) % pair_count).astype(F32)
    in_rows = (pair_index >= first_pairs) & (pair_index < first_pairs + axis_pairs)
    in_cols = pair_index >= first_pairs + axis_pairs
    log_base = math.log(ROPE_BASE)
    freq_rows = jnp.where(in_rows, jnp.exp(-log_base * (pair_index - first_pairs) / axis_pairs), 0.0)
    freq_cols = jnp.where(in_cols, jnp.exp(-log_base * (pair_index - first_pairs - axis_pairs) / axis_pairs), 0.0)
    is_image = tokens >= TXT
    image_pos = jnp.where(is_image, tokens - TXT, 0)
    row_pos = (image_pos // SIDE).astype(F32)
    col_pos = (image_pos % SIDE).astype(F32)
    angles = row_pos[..., None] * freq_rows + col_pos[..., None] * freq_cols
    side = jnp.where(jnp.arange(HEAD) < pair_count, -1.0, 1.0)
    return jnp.cos(angles), jnp.sin(angles) * side


def on_device(
    hidden, latents, vec, slot_token, text_len, step_index, guidance,
    w_mod, w_qkv, w_mlp_in, qk_gain, w_attn_out, w_mlp_out, w_final,
):
    tok = lax.axis_index("tok")
    mlp = lax.axis_index("mlp")
    rows_dev, prompts = hidden.shape[1], hidden.shape[2]
    split = slot_token.reshape(prompts, TOKS, RING, RING, 2, rows_dev // 2)
    first = split[:, :, :, :, 0].transpose(0, 1, 3, 2, 4).reshape(prompts, TOKS, SLOTS // 2)
    second = split[:, :, :, :, 1].reshape(prompts, TOKS, SLOTS // 2)
    ordered = jnp.concatenate([first, second], axis=2)
    tile_tokens = lax.dynamic_index_in_dim(ordered, tok, 1, keepdims=False)
    cosine, sine = rope_tables(tile_tokens.reshape(prompts, 2 * RING, PIECE))
    own_prompt = tok // 2
    job_tokens = lax.dynamic_index_in_dim(ordered, own_prompt, 0, keepdims=False).reshape(1, TOKS * SLOTS)
    job_len = lax.dynamic_index_in_dim(text_len[0], own_prompt, 0, keepdims=False)
    mask = ((job_tokens >= TXT) | (job_tokens < job_len)).astype(F32)
    own_first = (tok * MLPS + mlp) * rows_dev
    own_tokens = lax.dynamic_slice_in_dim(slot_token, own_first, rows_dev, 1).T.reshape(ROWS_OWN, 1)
    image = jnp.broadcast_to((own_tokens >= TXT).astype(F32), (ROWS_OWN, CH_HALF))
    current = step_index[0].astype(F32)
    step_size = sigma_at(current + 1.0, STEPS) - sigma_at(current, STEPS)
    scalars = jnp.broadcast_to(jnp.stack([guidance[0], step_size])[:, None], (2, CH_HALF))
    gains = qk_gain[0].reshape(2, HEAD // 2, 2).transpose(0, 2, 1).reshape(2, HEAD)
    velocity, latents_next, stream = call_kernel(
        hidden[0].reshape(ROWS_OWN, D), latents.reshape(ROWS_OWN, CH_HALF), vec[0],
        cosine, sine, mask, image, scalars, gains,
        w_mod.T, w_qkv[0].transpose(1, 0, 2), w_mlp_in[0], w_attn_out[0], w_mlp_out[0], w_final.T,
    )
    return (
        velocity.reshape(latents.shape),
        latents_next.reshape(latents.shape),
        stream.reshape(hidden.shape),
    )


def solution(mesh):
    return jax.shard_map(
        on_device,
        mesh=mesh,
        in_specs=(
            P("cfg", ("tok", "mlp"), None, None),
            P(("tok", "mlp"), None, "cfg"),
            P("cfg", None, None),
            P(),
            P("cfg", None),
            P(),
            P(),
            P(None, ("tok", "mlp")),
            P(None, "cfg", None, "mlp"),
            P(None, "cfg", "mlp"),
            P(),
            P(None, "mlp", "cfg"),
            P(None, "mlp", "cfg"),
            P(),
        ),
        out_specs=(
            P(("tok", "mlp"), None, "cfg"),
            P(("tok", "mlp"), None, "cfg"),
            P("cfg", ("tok", "mlp"), None, None),
        ),
        check_vma=False,
    )
```

```python
import math

import jax
import jax.numpy as jnp
import numpy as np
from jax import lax
from jax.experimental import pallas as pl
from jax.experimental.pallas import tpu as pltpu
from jax.sharding import PartitionSpec as P

SIDE = 32
TXT = 512
STEPS = 28
EPSILON = 1e-06
ROPE_BASE = 10000.0
TIME_SHIFT = 3.0

MESH = pl.DeviceIdType.MESH
F32 = jnp.float32
BF16 = jnp.bfloat16

D = 3072
HALF = D // 2
HEAD = 128
UNITS = 768
PROMPTS = 4
RING = 4
TOKS = 8
MLPS = 16
PIECE = 24
CHUNK = RING * PIECE
STAGE = 2 * CHUNK
SLOTS = 192
ROWS_OWN = 2 * PIECE
MOD_COLS = 120
CH_HALF = 32


def sigma_at(position, steps_total):
    remain = 1.0 - position / steps_total
    return TIME_SHIFT * remain / (1.0 + (TIME_SHIFT - 1.0) * remain)


def layer_norm(values):
    average = jnp.mean(values, axis=-1, keepdims=True)
    centred = values - average
    spread = jnp.mean(centred * centred, axis=-1, keepdims=True)
    return centred * lax.rsqrt(spread + EPSILON)


def dot_f32(a, b):
    return jnp.dot(a, b, preferred_element_type=F32)


def dot_t(a, b):
    return lax.dot_general(a, b, (((1,), (1,)), ((), ())), preferred_element_type=F32)


def kernel(
    hid_ref, lat_ref, vec_ref, token_ref, len_ref, step_ref, guide_ref, gain_ref, place_ref, tab_ref,
    wmod_hbm, wqkv_hbm, wmi_hbm, wao_hbm, wmo_hbm, wfin_hbm,
    vel_ref, latn_ref, stream_ref,
    HID, TT, COS, SIN, MASK, IMAGE, GAIN, X, N, WMOD, WQKV, WMI, WAO, WMO, WFIN, G, MOD, QF, ST, R, OS, OR, ATT,
    ACT, ACC, PS, RB, RC, PS2, RB2, RC2, VS, VR,
    ag_s, ag_r, rs_s, rs_r, w_l, w_s, w_r, m_s, m_r, z_l, z_s, z_r, f_s, f_r, o_s, o_r, v_s, v_r,
):
    c = lax.axis_index("cfg")
    t = lax.axis_index("tok")
    m = lax.axis_index("mlp")
    x, y = m // RING, m % RING
    uv = ((x, y), (y, x))

    def at_uv(k, u, v):
        return u * RING + v if k == 0 else v * RING + u

    def remote(src, dst, ssem, rsem, **where):
        return pltpu.make_async_remote_copy(
            src_ref=src, dst_ref=dst, send_sem=ssem, recv_sem=rsem,
            device_id=where, device_id_type=MESH,
        )

    barrier = pltpu.get_barrier_semaphore()
    for d in range(1, MLPS):
        pl.semaphore_signal(barrier, inc=1, device_id={"mlp": (m + d) % MLPS}, device_id_type=MESH)
    for d in range(1, TOKS):
        pl.semaphore_signal(barrier, inc=1, device_id={"tok": (t + d) % TOKS}, device_id_type=MESH)
    pl.semaphore_signal(barrier, inc=1, device_id={"cfg": 1 - c}, device_id_type=MESH)

    wmod_copy = pltpu.make_async_copy(wmod_hbm, WMOD, w_l.at[0])
    wmod_copy.start()
    k_rows = pl.ds(pl.multiple_of(c * HALF, HALF), HALF)
    weights = (
        [(wqkv_hbm.at[j], WQKV.at[k_rows, pl.ds(j * HEAD, HEAD)]) for j in range(3)]
        + [(wmi_hbm, WMI.at[k_rows]), (wao_hbm, WAO.at[c]), (wmo_hbm, WMO.at[c])]
    )
    local_w = [pltpu.make_async_copy(s, d, w_l.at[1 + i]) for i, (s, d) in enumerate(weights)]
    remote_w = [remote(s, d, w_s.at[i], w_r.at[i], cfg=1 - c) for i, (s, d) in enumerate(weights)]
    fin_copy = pltpu.make_async_copy(wfin_hbm, WFIN, w_l.at[7])

    for i in range(ROWS_OWN // PROMPTS):
        HID[i * PROMPTS : (i + 1) * PROMPTS, :] = hid_ref[i].astype(F32)
    normed = layer_norm(HID[...]).astype(BF16)
    X[0, y, x] = normed[:PIECE]
    X[1, x, y] = normed[PIECE:]

    vec = vec_ref[...]
    silu_vec = (vec * (1.0 / (1.0 + jnp.exp(-vec)))).astype(BF16)
    wmod_copy.wait()
    G[t, m, :, 0:MOD_COLS] = dot_t(silu_vec, WMOD[...])
    pl.semaphore_wait(barrier, MLPS - 1 + TOKS - 1 + 1)
    mod1 = [
        remote(G.at[t, m], G.at[t, m], m_s.at[0], m_r.at[0], mlp=(m + d) % MLPS) for d in range(1, MLPS)
    ]
    for copy in mod1:
        copy.start()

    lo, hi = pl.ds(0, HALF), pl.ds(HALF, HALF)

    def order_u(u, j):
        return (u, (u + 3) % RING, (u + 1) % RING, (u + 2) % RING)[j]

    def ag(k, i):
        u, v = uv[k]
        sems = (ag_s.at[k, i], ag_r.at[k, i])
        up, um = {"mlp": at_uv(k, (u + 1) % RING, v)}, {"mlp": at_uv(k, (u + 3) % RING, v)}
        vp, vm = {"mlp": at_uv(k, u, (v + 1) % RING)}, {"mlp": at_uv(k, u, (v + 3) % RING)}
        if i < 2:
            block = X.at[k, v, u]
            return remote(block, block, *sems, **(up if i == 0 else um))
        if i < 4:
            block = X.at[k, v, (u + (3 if i == 2 else 1)) % RING, :, lo if i == 2 else hi]
            return remote(block, block, *sems, **(up if i == 2 else um))
        if i < 12:
            j, d = (i - 4) // 2, (i - 4) % 2
            block = X.at[k, v, order_u(u, j)]
            return remote(block, block, *sems, **(vp if d == 0 else vm))
        j, d = (i - 12) // 2, (i - 12) % 2
        block = X.at[k, (v + (3 if d == 0 else 1)) % RING, order_u(u, j), :, lo if d == 0 else hi]
        return remote(block, block, *sems, **(vp if d == 0 else vm))

    def ag_start(ids):
        for i in ids:
            for k in range(2):
                ag(k, i).start()

    def ag_recv(ids):
        for i in ids:
            for k in range(2):
                ag(k, i).wait_recv()

    ag_start((0, 1))
    for copy in local_w[:3]:
        copy.start()
    for copy in remote_w[:3]:
        copy.start()
    for i in range(3, 6):
        local_w[i].start()
        remote_w[i].start()
    fin_copy.start()
    ag_start((4, 5))

    tokens = token_ref[...]
    is_image = tokens >= TXT
    place = jnp.where(is_image, tokens - TXT, 0)
    TT[0:4, :] = (place // SIDE).astype(F32)
    TT[4:8, :] = (place % SIDE).astype(F32)
    TT[8:12, :] = jnp.where(is_image, 1.0, 0.0)
    TT[12:16, :] = jnp.zeros((4, TOKS * SLOTS), F32)
    kinds = TT[...].astype(BF16)

    def lanes(shape):
        return lax.broadcasted_iota(jnp.int32, shape, 1)

    place_x = (place_ref[:, 0:1] + x) % RING
    place_y = (place_ref[:, 1:2] + y) % RING
    natural = (RING * place_x + place_y) * (ROWS_OWN // PROMPTS) + place_ref[:, 2:3]
    chosen = jnp.where(lanes((SLOTS, TOKS * SLOTS)) == natural + t * SLOTS, 1.0, 0.0).astype(BF16)
    picked = dot_t(chosen, kinds)
    lane192 = lanes((SLOTS, SLOTS))
    for p in range(PROMPTS):
        wanted_pos = jnp.where(lane192 % 64 < 32, picked[:, p : p + 1], picked[:, 4 + p : 5 + p])
        hot = jnp.where((lane192 % 32).astype(F32) == wanted_pos, 1.0, 0.0).astype(BF16)
        both = dot_f32(hot, tab_ref[...])
        COS[p] = both[:, :HEAD].reshape(2 * RING, PIECE, HEAD)
        SIN[p] = both[:, HEAD:].reshape(2 * RING, PIECE, HEAD)
    sub = lax.broadcasted_iota(jnp.int32, (ROWS_OWN, TOKS * SLOTS), 0)
    chosen = jnp.where(
        lanes((ROWS_OWN, TOKS * SLOTS)) == sub // PROMPTS + (t * MLPS + m) * (ROWS_OWN // PROMPTS), 1.0, 0.0
    ).astype(BF16)
    sub16 = lax.broadcasted_iota(jnp.int32, (ROWS_OWN, 16), 0)
    own_image = jnp.where(lanes((ROWS_OWN, 16)) == 8 + sub16 % PROMPTS, dot_t(chosen, kinds), 0.0)
    IMAGE[...] = jnp.broadcast_to(jnp.sum(own_image, axis=-1, keepdims=True), (ROWS_OWN, CH_HALF))
    this = lax.broadcasted_iota(jnp.int32, (PROMPTS, TOKS * SLOTS), 0) == t // 2
    job_tokens = jnp.sum(jnp.where(this, tokens.astype(F32), 0.0), axis=0, keepdims=True)
    job_len = jnp.sum(
        jnp.where(lanes((1, PROMPTS)) == t // 2, len_ref[...].astype(F32), 0.0), axis=-1, keepdims=True
    )
    valid = jnp.where((job_tokens >= TXT) | (job_tokens < job_len), 1.0, 0.0)
    valid = jnp.concatenate([valid[:, i * SLOTS : (i + 1) * SLOTS] for i in range(TOKS)], axis=0)
    valid = dot_t(valid.astype(BF16), jnp.where(lane192 == natural, 1.0, 0.0).astype(BF16))
    MASK[...] = jnp.concatenate([valid[i : i + 1, :] for i in range(TOKS)], axis=1)

    ag_recv((0, 1))
    ag_start((2, 3, 6, 7, 8, 9))

    span1 = remote(G.at[t, pl.ds(0, MLPS - 1)], G.at[t, pl.ds(0, MLPS - 1)], m_s.at[0], m_r.at[0], mlp=(m + 1) % MLPS)
    span1.wait_recv()
    mod2 = [remote(G.at[t], G.at[t], m_s.at[1], m_r.at[1], tok=(t + d) % TOKS) for d in range(1, TOKS)]
    for copy in mod2:
        copy.start()

    ag_recv((2, 3))
    ag_start((10, 11))

    for copy in local_w[:3]:
        copy.wait()
    for copy in remote_w[:3]:
        copy.wait_recv()
    src_col = lax.broadcasted_iota(jnp.int32, (HEAD, HEAD), 0)
    out_col = lax.broadcasted_iota(jnp.int32, (HEAD, HEAD), 1)
    wanted = jnp.where(out_col < HEAD // 2, 2 * out_col, 2 * out_col - HEAD + 1)
    permute = jnp.where(src_col == wanted, 1.0, 0.0).astype(BF16)

    gain = gain_ref[...]
    gain_sum = jnp.zeros((2, HEAD), F32)
    for _ in range(3):
        part = gain.astype(BF16)
        gain_sum = gain_sum + dot_f32(part, permute)
        gain = gain - part.astype(F32)
    GAIN[...] = gain_sum

    def permute_step(i, carry):
        rows = pl.ds(pl.multiple_of(i * 512, 512), 512)
        for j in range(2):
            cols = pl.ds(j * HEAD, HEAD)
            WQKV[rows, cols] = dot_f32(WQKV[rows, cols], permute).astype(BF16)
        return carry

    lax.fori_loop(0, D // 512, permute_step, 0)

    span2 = remote(
        G.at[pl.ds(0, TOKS - 1)], G.at[pl.ds(0, TOKS - 1)], m_s.at[1], m_r.at[1], tok=(t + 1) % TOKS
    )
    span2.wait_recv()
    lane = lax.broadcasted_iota(jnp.int32, (PROMPTS, 128), 1)

    def mod_step(i, carry):
        base = pl.multiple_of(i * (MLPS * MOD_COLS), 128)
        for j in range(15):
            shift = (8 * j) % MOD_COLS
            first = G[i, j]
            if shift:
                first = pltpu.roll(first, 128 - shift, 1)
            second = pltpu.roll(G[i, j + 1], MOD_COLS - shift, 1)
            both = jnp.where(lane < MOD_COLS - shift, first, second)
            MOD[:, pl.ds(base + j * 128, 128)] = jnp.concatenate([both, both], axis=0)
        return carry

    lax.fori_loop(0, TOKS, mod_step, 0)

    for i in range(3, 4):
        local_w[i].wait()
        remote_w[i].wait_recv()

    batches = [[(k, 0, j) for k in range(2) for j in range(RING)]]
    batches += [[(k, dv, j) for k in range(2) for dv in (1, 3)] for j in range(RING)]
    batches += [[(k, 2, j) for half in range(2) for k in range(2) for j in (2 * half, 2 * half + 1)]]
    starts = (0, 192, 288, 384, 480, 576)

    def modulate(b):
        blocks = batches[b]

        def step(i, carry):
            cols = pl.ds(pl.multiple_of(i * 256, 256), 256)
            scale = 1.0 + MOD[:, pl.ds(pl.multiple_of(D + i * 256, 256), 256)]
            shift = MOD[:, cols]
            for pair in range(0, len(blocks), 2):
                pieces = [
                    X[k, (uv[k][1] + dv) % RING, order_u(uv[k][0], j), :, cols].astype(F32).reshape(3, 8, 256)
                    for k, dv, j in blocks[pair : pair + 2]
                ]
                both = jnp.concatenate(pieces, axis=0) * scale[None] + shift[None]
                first = starts[b] + pair * PIECE
                N[first : first + 48, cols] = both.reshape(48, 256).astype(BF16)
            return carry

        lax.fori_loop(0, D // 256, step, 0)

    soft_scale = math.log2(math.e) / math.sqrt(HEAD)

    def groups_of(b):
        return len(batches[b]) // RING, starts[b] // CHUNK

    def qkv(b):
        count, g0 = groups_of(b)
        rows_b = count * CHUNK
        pre = dot_f32(N[starts[b] : starts[b] + rows_b, :], WQKV[...])
        for j in range(3):
            QF[j, 0:rows_b] = pre[:, j * HEAD : (j + 1) * HEAD]
        for p in range(PROMPTS):
            rows = pl.ds(p, count * PIECE, stride=PROMPTS)
            cosine = COS[p, g0 : g0 + count].reshape(count * PIECE, HEAD)
            sine = SIN[p, g0 : g0 + count].reshape(count * PIECE, HEAD)
            outs = []
            for j in range(2):
                val = QF.at[j][rows, :]
                val = val * lax.rsqrt(jnp.mean(val * val, axis=-1, keepdims=True) + EPSILON) * GAIN[j : j + 1, :]
                outs.append((val * cosine + pltpu.roll(val, HEAD // 2, 1) * sine).astype(BF16))
            outs.append(QF.at[2][rows, :].astype(BF16))
            for place, val in ((0, outs[1]), (1, outs[2]), (2, outs[0])):
                for g in range(count):
                    ST[p, g0 + g, place] = val[g * PIECE : (g + 1) * PIECE]

    def job(i):
        p = (t // 2 + i) % PROMPTS
        rel = (t - 2 * p + TOKS) % TOKS
        half = 1 - ((rel + 7) % TOKS) // RING
        return p, 2 * p + half

    sign = 1 - 2 * (t % 2)
    partner = t + sign
    kv = pl.ds(0, 2)

    def tile(o):
        return (t + TOKS - sign * o) % TOKS

    def z_local(b):
        count, g0 = groups_of(b)
        gs = pl.ds(g0, count)
        return pltpu.make_async_copy(ST.at[t // 2, gs], R.at[t, gs], z_l.at[b])

    def z_send(b, i):
        count, g0 = groups_of(b)
        gs = pl.ds(g0, count)
        p, z_query = job(i)
        return remote(ST.at[p, gs], R.at[t, gs], z_s.at[i, b], z_r.at[t, b], tok=z_query)

    def z_near(b, o):
        count, g0 = groups_of(b)
        block = R.at[tile(o), pl.ds(g0, count)]
        return remote(block, block, z_s.at[0, b], z_r.at[tile(o), b], tok=partner)

    def z_hand(b, o):
        count, g0 = groups_of(b)
        gs = pl.ds(g0, count)
        src = ST.at[t // 2, gs, kv] if o == 0 else R.at[tile(o), gs, kv]
        return remote(src, R.at[tile(o), gs, kv], f_s.at[o, b], f_r.at[tile(o), b], tok=partner)

    def z_far(b, o):
        count, g0 = groups_of(b)
        block = R.at[tile(o), pl.ds(g0, count), kv]
        return remote(block, block, f_s.at[0, b], f_r.at[tile(o), b], tok=partner)

    def send_batch(b):
        for i in (2, 1, 3):
            z_send(b, i).start()
        z_local(b).start()
        z_hand(b, 0).start()

    def hand_on(b):
        for o in range(1, RING):
            z_near(b, o).wait_recv()
            z_hand(b, o).start()

    def units(first, count):
        def step(i, carry):
            cols = pl.ds(pl.multiple_of(i * 256, 256), 256)
            ACT[first : first + count, cols] = jax.nn.gelu(
                dot_f32(N[first : first + count, :], WMI[:, cols]), approximate=True
            ).astype(BF16)
            return carry

        lax.fori_loop(0, UNITS // 256, step, 0)

    def units_out(first, count):
        def step(i, carry):
            cols = pl.ds(pl.multiple_of(i * 256, 256), 256)
            for h in range(2):
                ACC[h, first : first + count, cols] = dot_f32(ACT[first : first + count, :], WMO[h, :, cols])
            return carry

        lax.fori_loop(0, HALF // 256, step, 0)

    def take(b):
        modulate(b)
        qkv(b)
        send_batch(b)

    take(0)
    ag_recv((4, 5))
    ag_start((12, 13))
    take(1)
    units(0, 192)
    ag_recv((6, 7))
    ag_start((14, 15))
    take(2)
    hand_on(0)
    hand_on(1)
    ag_recv((8, 9))
    ag_start((16, 17))
    take(3)
    hand_on(2)
    for i in range(4, 6):
        local_w[i].wait()
        remote_w[i].wait_recv()
    ag_recv((10, 11))
    ag_start((18, 19))
    take(4)
    hand_on(3)
    units(192, 192)
    hand_on(4)
    units_out(0, 192)
    ag_recv(range(12, 20))
    take(5)
    units(384, 192)
    hand_on(5)
    units(576, 192)
    units_out(192, 192)
    units_out(384, 192)
    units_out(576, 192)

    for b in range(len(batches)):
        z_local(b).wait()
        for o in range(RING, TOKS):
            z_far(b, o).wait_recv()
    own_p = t // 2

    def attend(o):
        keys = R[:, :, 0].reshape(TOKS * SLOTS, HEAD)
        vals = R[:, :, 1].reshape(TOKS * SLOTS, HEAD)
        query = R[tile(o), :, 2].reshape(SLOTS, HEAD)
        soft = jnp.exp2(dot_t(query, keys) * soft_scale) * MASK[...]
        total = jnp.sum(soft, axis=-1, keepdims=True)
        return (dot_f32(soft.astype(BF16), vals) / total).astype(BF16)

    for o in range(1, RING):
        OS[o] = attend(o)
        remote(OS.at[o], OR.at[own_p], o_s.at[o], o_r.at[own_p], tok=tile(o)).start()
    OR[own_p] = attend(0)

    for i in range(1, PROMPTS):
        p, z_query = job(i)
        remote(OS.at[0], OR.at[p], o_s.at[0], o_r.at[p], tok=z_query).wait_recv()
    for p in range(PROMPTS):
        ATT[pl.ds(p, SLOTS, stride=PROMPTS), :] = OR[p].astype(F32)

    rel_v = {0: 0, 1: 1, 3: 2, 2: 3}

    def out_rows(first, blocks):
        count = len(blocks) * PIECE
        att = ATT[first : first + count, :].astype(BF16)
        for h in range(2):
            for n in range(HALF // 512):
                cols = slice(n * 512, (n + 1) * 512)
                part = dot_f32(att, WAO[h, :, cols]) + ACC[h, first : first + count, cols]
                for i, (k, dv, j) in enumerate(blocks):
                    PS[k, rel_v[dv], j, :, h * HALF + n * 512 : h * HALF + (n + 1) * 512] = part[
                        i * PIECE : (i + 1) * PIECE
                    ].astype(BF16)

    def rs(k, i):
        u, v = uv[k]
        sems = (rs_s.at[k, i], rs_r.at[k, i])
        up, um = {"mlp": at_uv(k, (u + 1) % RING, v)}, {"mlp": at_uv(k, (u + 3) % RING, v)}
        vp, vm = {"mlp": at_uv(k, u, (v + 1) % RING)}, {"mlp": at_uv(k, u, (v + 3) % RING)}
        if i < 16:
            j, d = 3 - (i % 8) // 2, i % 2
            where = vp if d == 0 else vm
            if i < 8:
                block = PS.at[k, 3, j, :, lo if d == 0 else hi]
                return remote(block, RB.at[k, d, j], *sems, **where)
            block = PS.at[k, 1 + d, j]
            return remote(block, RC.at[k, d, j], *sems, **where)
        d = i % 2
        where = up if d == 0 else um
        if i < 18:
            return remote(PS2.at[k, 0, :, lo if d == 0 else hi], RB2.at[k, d], *sems, **where)
        return remote(PS2.at[k, 1 + d], RC2.at[k, d], *sems, **where)

    last = batches[5]
    for half in (1, 0):
        out_rows(576 + half * 96, last[half * 4 : half * 4 + 4])
        for i in range(4 * (1 - half), 4 * (1 - half) + 4):
            for k in range(2):
                rs(k, i).start()
    for step in range(RING):
        j = 3 - step
        out_rows(starts[1 + j], batches[1 + j])
        for d in range(2):
            for k in range(2):
                rs(k, 2 * step + d).wait_recv()
                cols = slice(0, HALF) if d == 0 else slice(HALF, D)
                PS[k, 1 + d, j, :, cols] = (
                    PS[k, 1 + d, j, :, cols].astype(F32) + RB[k, d, j].astype(F32)
                ).astype(BF16)
                rs(k, 8 + 2 * step + d).start()
    out_rows(0, batches[0])

    def own_sum(k, j):
        for d in range(2):
            rs(k, 8 + 2 * (3 - j) + d).wait_recv()
        return PS[k, 0, j].astype(F32) + RC[k, 0, j].astype(F32) + RC[k, 1, j].astype(F32)

    for k in range(2):
        PS2[k, 0] = own_sum(k, 3).astype(BF16)
        rs(k, 16).start()
        rs(k, 17).start()
    for d in range(2):
        for k in range(2):
            total = own_sum(k, 2 - d)
            rs(k, 16 + d).wait_recv()
            cols = slice(0, HALF) if d == 0 else slice(HALF, D)
            PS2[k, 1 + d] = total.astype(BF16)
            PS2[k, 1 + d, :, cols] = (total[:, cols] + RB2[k, d].astype(F32)).astype(BF16)
            rs(k, 18 + d).start()
    fin_copy.wait()
    finals = []
    for k in range(2):
        branch = own_sum(k, 0)
        for d in range(2):
            rs(k, 18 + d).wait_recv()
        branch = branch + RC2[k, 0].astype(F32) + RC2[k, 1].astype(F32)
        rows = slice(k * PIECE, (k + 1) * PIECE)
        gated = branch.reshape(3, 8, D) * MOD[:, 2 * D : 3 * D][None]
        stream = (HID[rows, :] + gated.reshape(PIECE, D)).astype(BF16)
        stream32 = stream.astype(F32)
        for i in range(PIECE // PROMPTS):
            stream_ref[k * (PIECE // PROMPTS) + i] = stream32[i * PROMPTS : (i + 1) * PROMPTS].astype(BF16)
        shaped = layer_norm(stream32).reshape(3, 8, D)
        shaped = shaped * (1.0 + MOD[:, 4 * D : 5 * D])[None] + MOD[:, 3 * D : 4 * D][None]
        finals.append(shaped.reshape(PIECE, D).astype(BF16).astype(F32))
    final_normed = jnp.concatenate(finals, axis=0).astype(BF16)
    half_velocity = dot_t(final_normed, WFIN[...])
    parts = (half_velocity[:, :CH_HALF] * IMAGE[...], half_velocity[:, CH_HALF:] * IMAGE[...])
    first = c == 0
    VS[...] = jnp.where(first, parts[1], parts[0])
    swap = remote(VS, VR, v_s, v_r, cfg=1 - c)
    swap.start()
    own = jnp.where(first, parts[0], parts[1])
    swap.wait_recv()
    other = VR[...]
    cond = jnp.where(first, own, other)
    uncond = jnp.where(first, other, own)
    velocity = uncond + guide_ref[...] * (cond - uncond)
    current = step_ref[...].astype(F32)
    step_size = sigma_at(current + 1.0, STEPS) - sigma_at(current, STEPS)
    moved = step_size * velocity
    for i in range(ROWS_OWN // PROMPTS):
        rows = slice(i * PROMPTS, (i + 1) * PROMPTS)
        vel_ref[i] = velocity[rows]
        latn_ref[i] = lat_ref[i] + moved[rows]

    swap.wait_send()
    for copy in remote_w:
        copy.wait_send()
    span1.wait_send()
    span2.wait_send()
    for k in range(2):
        for i in range(20):
            ag(k, i).wait_send()
            rs(k, i).wait_send()
    for b in range(len(batches)):
        for i in range(1, PROMPTS):
            z_send(b, i).wait_send()
        for o in range(RING):
            z_hand(b, o).wait_send()
    for o in range(1, RING):
        remote(OS.at[o], OR.at[own_p], o_s.at[o], o_r.at[own_p], tok=tile(o)).wait_send()


def call_kernel(*operands):
    vmem = pl.BlockSpec(memory_space=pltpu.VMEM)
    hbm = pl.BlockSpec(memory_space=pl.ANY)
    dma = pltpu.SemaphoreType.DMA
    scratch = [
        pltpu.VMEM((ROWS_OWN, D), F32),
        pltpu.VMEM((16, TOKS * SLOTS), F32),
        pltpu.VMEM((PROMPTS, 2 * RING, PIECE, HEAD), F32),
        pltpu.VMEM((PROMPTS, 2 * RING, PIECE, HEAD), F32),
        pltpu.VMEM((1, TOKS * SLOTS), F32),
        pltpu.VMEM((ROWS_OWN, CH_HALF), F32),
        pltpu.VMEM((2, HEAD), F32),
        pltpu.VMEM((2, RING, RING, PIECE, D), BF16),
        pltpu.VMEM((PROMPTS * SLOTS, D), BF16),
        pltpu.VMEM((MOD_COLS, D), BF16),
        pltpu.VMEM((D, 3 * HEAD), BF16),
        pltpu.VMEM((D, UNITS), BF16),
        pltpu.VMEM((2, HEAD, HALF), BF16),
        pltpu.VMEM((2, UNITS, HALF), BF16),
        pltpu.VMEM((2 * CH_HALF, D), BF16),
        pltpu.VMEM((TOKS, MLPS, PROMPTS, 128), F32),
        pltpu.VMEM((8, 5 * D), F32),
        pltpu.VMEM((3, STAGE, HEAD), F32),
        pltpu.VMEM((PROMPTS, 2 * RING, 3, PIECE, HEAD), BF16),
        pltpu.VMEM((TOKS, 2 * RING, 3, PIECE, HEAD), BF16),
        pltpu.VMEM((RING, SLOTS, HEAD), BF16),
        pltpu.VMEM((PROMPTS, SLOTS, HEAD), BF16),
        pltpu.VMEM((PROMPTS * SLOTS, HEAD), F32),
        pltpu.VMEM((PROMPTS * SLOTS, UNITS), BF16),
        pltpu.VMEM((2, PROMPTS * SLOTS, HALF), F32),
        pltpu.VMEM((2, RING, RING, PIECE, D), BF16),
        pltpu.VMEM((2, 2, RING, PIECE, HALF), BF16),
        pltpu.VMEM((2, 2, RING, PIECE, D), BF16),
        pltpu.VMEM((2, 3, PIECE, D), BF16),
        pltpu.VMEM((2, 2, PIECE, HALF), BF16),
        pltpu.VMEM((2, 2, PIECE, D), BF16),
        pltpu.VMEM((ROWS_OWN, CH_HALF), F32),
        pltpu.VMEM((ROWS_OWN, CH_HALF), F32),
        dma((2, 20)), dma((2, 20)), dma((2, 20)), dma((2, 20)),
        dma((8,)), dma((6,)), dma((6,)), dma((2,)), dma((2,)),
        dma((6,)), dma((PROMPTS, 6)), dma((TOKS, 6)), dma((RING, 6)), dma((TOKS, 6)),
        dma((RING,)), dma((PROMPTS,)), dma, dma,
    ]
    return pl.pallas_call(
        kernel,
        out_shape=(
            jax.ShapeDtypeStruct((ROWS_OWN // PROMPTS, PROMPTS, CH_HALF), F32),
            jax.ShapeDtypeStruct((ROWS_OWN // PROMPTS, PROMPTS, CH_HALF), F32),
            jax.ShapeDtypeStruct((ROWS_OWN // PROMPTS, PROMPTS, D), BF16),
        ),
        in_specs=[vmem] * 10 + [hbm] * 6,
        out_specs=(vmem, vmem, vmem),
        scratch_shapes=scratch,
        compiler_params=pltpu.CompilerParams(
            collective_id=0, has_side_effects=True, vmem_limit_bytes=67043328
        ),
    )(*operands)


def slot_places():
    blocks = [(k, 0, j) for k in range(2) for j in range(RING)]
    blocks += [(k, dv, j) for j in range(RING) for k in range(2) for dv in (1, 3)]
    blocks += [(k, 2, j) for half in range(2) for k in range(2) for j in (2 * half, 2 * half + 1)]
    rows = []
    for k, dv, j in blocks:
        du = (0, 3, 1, 2)[j]
        dx, dy = (du, dv) if k == 0 else (dv, du)
        rows += [(dx, dy, 6 * k + i) for i in range(6)]
    return np.array(rows, np.int32)


def rope_table():
    pairs = HEAD // 2
    first_pairs = HEAD // 16
    axis_pairs = (HEAD - HEAD // 8) // 4
    index = np.arange(pairs, dtype=np.float32)
    in_rows = (index >= first_pairs) & (index < first_pairs + axis_pairs)
    in_cols = index >= first_pairs + axis_pairs
    log_base = np.float32(math.log(ROPE_BASE))
    table = np.zeros((2 * SIDE, 2 * HEAD), np.float32)
    for pos in range(SIDE):
        for base, inside, start in ((0, in_rows, first_pairs), (SIDE, in_cols, first_pairs + axis_pairs)):
            freq = np.exp(-log_base * (index - np.float32(start)) / np.float32(axis_pairs)).astype(np.float32)
            angle = np.where(inside, np.float32(pos) * freq, 0.0).astype(np.float32)
            still = ~(in_rows | in_cols) if base == 0 else np.zeros_like(inside)
            cosine = np.where(inside, np.cos(angle), np.where(still, 1.0, 0.0))
            sine = np.where(inside, np.sin(angle), 0.0)
            table[base + pos] = np.concatenate([cosine, cosine, -sine, sine])
    parts, left = [], table
    for _ in range(3):
        part = left.astype(jnp.bfloat16)
        parts.append(part)
        left = left - part.astype(np.float32)
    return np.concatenate(parts, axis=0)


def on_device(
    hidden, latents, vec, slot_token, text_len, step_index, guidance,
    w_mod, w_qkv, w_mlp_in, qk_gain, w_attn_out, w_mlp_out, w_final,
):
    velocity, latents_next, stream = call_kernel(
        hidden[0], latents, vec[0], slot_token, text_len, step_index[None], guidance[None], qk_gain[0],
        jnp.asarray(slot_places()), jnp.asarray(rope_table()),
        w_mod.T, w_qkv[0].transpose(1, 0, 2), w_mlp_in[0], w_attn_out[0], w_mlp_out[0], w_final.T,
    )
    return velocity, latents_next, stream[None]


def solution(mesh):
    return jax.shard_map(
        on_device,
        mesh=mesh,
        in_specs=(
            P("cfg", ("tok", "mlp"), None, None),
            P(("tok", "mlp"), None, "cfg"),
            P("cfg", None, None),
            P(),
            P("cfg", None),
            P(),
            P(),
            P(None, ("tok", "mlp")),
            P(None, "cfg", None, "mlp"),
            P(None, "cfg", "mlp"),
            P(),
            P(None, "mlp", "cfg"),
            P(None, "mlp", "cfg"),
            P(),
        ),
        out_specs=(
            P(("tok", "mlp"), None, "cfg"),
            P(("tok", "mlp"), None, "cfg"),
            P("cfg", ("tok", "mlp"), None, None),
        ),
        check_vma=False,
    )
```

```python
import math

import jax
import jax.numpy as jnp
import numpy as np
from jax import lax
from jax.experimental import pallas as pl
from jax.experimental.pallas import tpu as pltpu
from jax.sharding import PartitionSpec as P

SIDE = 32
TXT = 512
STEPS = 28
EPSILON = 1e-06
ROPE_BASE = 10000.0
TIME_SHIFT = 3.0

MESH = pl.DeviceIdType.MESH
F32 = jnp.float32
BF16 = jnp.bfloat16

D = 3072
HALF = D // 2
HEAD = 128
UNITS = 768
PROMPTS = 4
RING = 4
TOKS = 8
MLPS = 16
PIECE = 24
CHUNK = RING * PIECE
STAGE = 2 * CHUNK
SLOTS = 192
ROWS_OWN = 2 * PIECE
MOD_COLS = 120
CH_HALF = 32


def sigma_at(position, steps_total):
    remain = 1.0 - position / steps_total
    return TIME_SHIFT * remain / (1.0 + (TIME_SHIFT - 1.0) * remain)


def layer_norm(values):
    average = jnp.mean(values, axis=-1, keepdims=True)
    centred = values - average
    spread = jnp.mean(centred * centred, axis=-1, keepdims=True)
    return centred * lax.rsqrt(spread + EPSILON)


def dot_f32(a, b):
    return jnp.dot(a, b, preferred_element_type=F32)


def dot_t(a, b):
    return lax.dot_general(a, b, (((1,), (1,)), ((), ())), preferred_element_type=F32)


def kernel(
    hid_ref, vec_ref, token_ref, len_ref, gain_ref, place_ref, tab_ref,
    wmod_hbm, wqkv_hbm, wmi_hbm, wao_hbm, wmo_hbm, wfin_hbm,
    cond_ref, uncond_ref, stream_ref,
    HID, TT, COS, SIN, MASK, IMAGE, GAIN, X, N, WMOD, WQKV, WMI, WAO, WMO, WFIN, G, MOD, QF, ST, R, OS, OR, ATT,
    ACT, ACC, PS, RB, RC, PS2, RB2, RC2, VS, VR,
    ag_s, ag_r, rs_s, rs_r, w_l, w_s, w_r, m_s, m_r, z_l, z_s, z_r, f_s, f_r, o_s, o_r, v_s, v_r,
):
    c = lax.axis_index("cfg")
    t = lax.axis_index("tok")
    m = lax.axis_index("mlp")
    x, y = m // RING, m % RING
    uv = ((x, y), (y, x))

    def at_uv(k, u, v):
        return u * RING + v if k == 0 else v * RING + u

    def remote(src, dst, ssem, rsem, **where):
        return pltpu.make_async_remote_copy(
            src_ref=src, dst_ref=dst, send_sem=ssem, recv_sem=rsem,
            device_id=where, device_id_type=MESH,
        )

    barrier = pltpu.get_barrier_semaphore()
    for d in range(1, MLPS):
        pl.semaphore_signal(barrier, inc=1, device_id={"mlp": (m + d) % MLPS}, device_id_type=MESH)
    for d in range(1, TOKS):
        pl.semaphore_signal(barrier, inc=1, device_id={"tok": (t + d) % TOKS}, device_id_type=MESH)
    pl.semaphore_signal(barrier, inc=1, device_id={"cfg": 1 - c}, device_id_type=MESH)

    wmod_copy = pltpu.make_async_copy(wmod_hbm, WMOD, w_l.at[0])
    wmod_copy.start()
    k_rows = pl.ds(pl.multiple_of(c * HALF, HALF), HALF)
    weights = (
        [(wqkv_hbm.at[j], WQKV.at[k_rows, pl.ds(j * HEAD, HEAD)]) for j in range(3)]
        + [(wmi_hbm, WMI.at[k_rows]), (wao_hbm, WAO.at[c]), (wmo_hbm, WMO.at[c])]
    )
    local_w = [pltpu.make_async_copy(s, d, w_l.at[1 + i]) for i, (s, d) in enumerate(weights)]
    remote_w = [remote(s, d, w_s.at[i], w_r.at[i], cfg=1 - c) for i, (s, d) in enumerate(weights)]
    fin_copy = pltpu.make_async_copy(wfin_hbm, WFIN, w_l.at[7])

    for i in range(ROWS_OWN // PROMPTS):
        HID[i * PROMPTS : (i + 1) * PROMPTS, :] = hid_ref[i].astype(F32)
    normed = layer_norm(HID[...]).astype(BF16)
    X[0, y, x] = normed[:PIECE]
    X[1, x, y] = normed[PIECE:]

    vec = vec_ref[...]
    silu_vec = (vec * (1.0 / (1.0 + jnp.exp(-vec)))).astype(BF16)
    wmod_copy.wait()
    G[t, m, :, 0:MOD_COLS] = dot_t(silu_vec, WMOD[...])
    pl.semaphore_wait(barrier, MLPS - 1 + TOKS - 1 + 1)
    mod1 = [
        remote(G.at[t, m], G.at[t, m], m_s.at[0], m_r.at[0], mlp=(m + d) % MLPS) for d in range(1, MLPS)
    ]
    for copy in mod1:
        copy.start()

    lo, hi = pl.ds(0, HALF), pl.ds(HALF, HALF)

    def order_u(u, j):
        return (u, (u + 3) % RING, (u + 1) % RING, (u + 2) % RING)[j]

    def ag(k, i):
        u, v = uv[k]
        sems = (ag_s.at[k, i], ag_r.at[k, i])
        up, um = {"mlp": at_uv(k, (u + 1) % RING, v)}, {"mlp": at_uv(k, (u + 3) % RING, v)}
        vp, vm = {"mlp": at_uv(k, u, (v + 1) % RING)}, {"mlp": at_uv(k, u, (v + 3) % RING)}
        if i < 2:
            block = X.at[k, v, u]
            return remote(block, block, *sems, **(up if i == 0 else um))
        if i < 4:
            block = X.at[k, v, (u + (3 if i == 2 else 1)) % RING, :, lo if i == 2 else hi]
            return remote(block, block, *sems, **(up if i == 2 else um))
        if i < 12:
            j, d = (i - 4) // 2, (i - 4) % 2
            block = X.at[k, v, order_u(u, j)]
            return remote(block, block, *sems, **(vp if d == 0 else vm))
        j, d = (i - 12) // 2, (i - 12) % 2
        block = X.at[k, (v + (3 if d == 0 else 1)) % RING, order_u(u, j), :, lo if d == 0 else hi]
        return remote(block, block, *sems, **(vp if d == 0 else vm))

    def ag_start(ids):
        for i in ids:
            for k in range(2):
                ag(k, i).start()

    def ag_recv(ids):
        for i in ids:
            for k in range(2):
                ag(k, i).wait_recv()

    ag_start((0, 1, 4, 5))

    for copy in local_w[:3]:
        copy.start()
    for copy in remote_w[:3]:
        copy.start()
    for i in range(3, 6):
        local_w[i].start()
        remote_w[i].start()
    fin_copy.start()

    tokens = token_ref[...]
    is_image = tokens >= TXT
    place = jnp.where(is_image, tokens - TXT, 0)
    TT[0:4, :] = (place // SIDE).astype(F32)
    TT[4:8, :] = (place % SIDE).astype(F32)
    TT[8:12, :] = jnp.where(is_image, 1.0, 0.0)
    TT[12:16, :] = jnp.zeros((4, TOKS * SLOTS), F32)
    kinds = TT[...].astype(BF16)

    def lanes(shape):
        return lax.broadcasted_iota(jnp.int32, shape, 1)

    place_x = (place_ref[:, 0:1] + x) % RING
    place_y = (place_ref[:, 1:2] + y) % RING
    natural = (RING * place_x + place_y) * (ROWS_OWN // PROMPTS) + place_ref[:, 2:3]
    chosen = jnp.where(lanes((SLOTS, TOKS * SLOTS)) == natural + t * SLOTS, 1.0, 0.0).astype(BF16)
    picked = dot_t(chosen, kinds)
    lane192 = lanes((SLOTS, SLOTS))
    for p in range(PROMPTS):
        wanted_pos = jnp.where(lane192 % 64 < 32, picked[:, p : p + 1], picked[:, 4 + p : 5 + p])
        hot = jnp.where((lane192 % 32).astype(F32) == wanted_pos, 1.0, 0.0).astype(BF16)
        both = dot_f32(hot, tab_ref[...])
        COS[p] = both[:, :HEAD].reshape(2 * RING, PIECE, HEAD)
        SIN[p] = both[:, HEAD:].reshape(2 * RING, PIECE, HEAD)
    sub = lax.broadcasted_iota(jnp.int32, (ROWS_OWN, TOKS * SLOTS), 0)
    chosen = jnp.where(
        lanes((ROWS_OWN, TOKS * SLOTS)) == sub // PROMPTS + (t * MLPS + m) * (ROWS_OWN // PROMPTS), 1.0, 0.0
    ).astype(BF16)
    sub16 = lax.broadcasted_iota(jnp.int32, (ROWS_OWN, 16), 0)
    own_image = jnp.where(lanes((ROWS_OWN, 16)) == 8 + sub16 % PROMPTS, dot_t(chosen, kinds), 0.0)
    IMAGE[...] = jnp.broadcast_to(jnp.sum(own_image, axis=-1, keepdims=True), (ROWS_OWN, CH_HALF))
    this = lax.broadcasted_iota(jnp.int32, (PROMPTS, TOKS * SLOTS), 0) == t // 2
    job_tokens = jnp.sum(jnp.where(this, tokens.astype(F32), 0.0), axis=0, keepdims=True)
    job_len = jnp.sum(
        jnp.where(lanes((1, PROMPTS)) == t // 2, len_ref[...].astype(F32), 0.0), axis=-1, keepdims=True
    )
    valid = jnp.where((job_tokens >= TXT) | (job_tokens < job_len), 1.0, 0.0)
    valid = jnp.concatenate([valid[:, i * SLOTS : (i + 1) * SLOTS] for i in range(TOKS)], axis=0)
    valid = dot_t(valid.astype(BF16), jnp.where(lane192 == natural, 1.0, 0.0).astype(BF16))
    MASK[...] = jnp.concatenate([valid[i : i + 1, :] for i in range(TOKS)], axis=1)

    ag_recv((0, 1))
    ag_start((2, 3, 6, 7, 8, 9))

    span1 = remote(G.at[t, pl.ds(0, MLPS - 1)], G.at[t, pl.ds(0, MLPS - 1)], m_s.at[0], m_r.at[0], mlp=(m + 1) % MLPS)
    span1.wait_recv()
    mod2 = [remote(G.at[t], G.at[t], m_s.at[1], m_r.at[1], tok=(t + d) % TOKS) for d in range(1, TOKS)]
    for copy in mod2:
        copy.start()

    ag_recv((2, 3))
    ag_start((10, 11))

    for copy in local_w[:3]:
        copy.wait()
    for copy in remote_w[:3]:
        copy.wait_recv()
    src_col = lax.broadcasted_iota(jnp.int32, (HEAD, HEAD), 0)
    out_col = lax.broadcasted_iota(jnp.int32, (HEAD, HEAD), 1)
    wanted = jnp.where(out_col < HEAD // 2, 2 * out_col, 2 * out_col - HEAD + 1)
    permute = jnp.where(src_col == wanted, 1.0, 0.0).astype(BF16)

    gain = gain_ref[...]
    gain_sum = jnp.zeros((2, HEAD), F32)
    for _ in range(3):
        part = gain.astype(BF16)
        gain_sum = gain_sum + dot_f32(part, permute)
        gain = gain - part.astype(F32)
    GAIN[...] = gain_sum

    def permute_step(i, carry):
        rows = pl.ds(pl.multiple_of(i * 512, 512), 512)
        for j in range(2):
            cols = pl.ds(j * HEAD, HEAD)
            WQKV[rows, cols] = dot_f32(WQKV[rows, cols], permute).astype(BF16)
        return carry

    lax.fori_loop(0, D // 512, permute_step, 0)

    span2 = remote(
        G.at[pl.ds(0, TOKS - 1)], G.at[pl.ds(0, TOKS - 1)], m_s.at[1], m_r.at[1], tok=(t + 1) % TOKS
    )
    span2.wait_recv()
    lane = lax.broadcasted_iota(jnp.int32, (PROMPTS, 128), 1)

    def mod_step(i, carry):
        base = pl.multiple_of(i * (MLPS * MOD_COLS), 128)
        for j in range(15):
            shift = (8 * j) % MOD_COLS
            first = G[i, j]
            if shift:
                first = pltpu.roll(first, 128 - shift, 1)
            second = pltpu.roll(G[i, j + 1], MOD_COLS - shift, 1)
            index = i * 15 + j
            is_scale = jnp.where(((index >= 24) & (index < 48)) | (index >= 96), 1.0, 0.0)
            both = jnp.where(lane < MOD_COLS - shift, first, second) + is_scale
            MOD[:, pl.ds(base + j * 128, 128)] = jnp.concatenate([both, both], axis=0)
        return carry

    lax.fori_loop(0, TOKS, mod_step, 0)

    for i in range(3, 4):
        local_w[i].wait()
        remote_w[i].wait_recv()

    batches = [[(k, 0, j) for k in range(2) for j in range(RING)]]
    batches += [[(k, dv, j) for k in range(2) for dv in (1, 3)] for j in range(RING)]
    batches += [[(k, 2, j) for k in range(2) for j in (2 * half, 2 * half + 1)] for half in range(2)]
    starts = (0, 192, 288, 384, 480, 576, 672)
    width = 768

    def modulate(b):
        blocks = batches[b]

        def step(i, carry):
            cols = pl.ds(pl.multiple_of(i * width, width), width)
            scale = MOD[:, pl.ds(pl.multiple_of(D + i * width, width), width)]
            shift = MOD[:, cols]
            for pair in range(0, len(blocks), 2):
                pieces = [
                    X[k, (uv[k][1] + dv) % RING, order_u(uv[k][0], j), :, cols].astype(F32).reshape(3, 8, width)
                    for k, dv, j in blocks[pair : pair + 2]
                ]
                both = jnp.concatenate(pieces, axis=0) * scale[None] + shift[None]
                first = starts[b] + pair * PIECE
                N[first : first + 48, cols] = both.reshape(48, width).astype(BF16)
            return carry

        lax.fori_loop(0, D // width, step, 0)

    soft_scale = math.log2(math.e) / math.sqrt(HEAD)

    def groups_of(b):
        return len(batches[b]) // RING, starts[b] // CHUNK

    def qkv(b):
        count, g0 = groups_of(b)
        rows_b = count * CHUNK
        pre = dot_f32(N[starts[b] : starts[b] + rows_b, :], WQKV[...])
        for j in range(3):
            QF[j, 0:rows_b] = pre[:, j * HEAD : (j + 1) * HEAD]
        for p in range(PROMPTS):
            rows = pl.ds(p, count * PIECE, stride=PROMPTS)
            cosine = COS[p, g0 : g0 + count].reshape(count * PIECE, HEAD)
            sine = SIN[p, g0 : g0 + count].reshape(count * PIECE, HEAD)
            outs = []
            for j in range(2):
                val = QF.at[j][rows, :]
                val = val * lax.rsqrt(jnp.mean(val * val, axis=-1, keepdims=True) + EPSILON) * GAIN[j : j + 1, :]
                outs.append((val * cosine + pltpu.roll(val, HEAD // 2, 1) * sine).astype(BF16))
            outs.append(QF.at[2][rows, :].astype(BF16))
            for place, val in ((0, outs[1]), (1, outs[2]), (2, outs[0])):
                for g in range(count):
                    ST[p, g0 + g, place] = val[g * PIECE : (g + 1) * PIECE]

    def job(i):
        p = (t // 2 + i) % PROMPTS
        rel = (t - 2 * p + TOKS) % TOKS
        half = 1 - ((rel + 7) % TOKS) // RING
        return p, 2 * p + half

    sign = 1 - 2 * (t % 2)
    partner = t + sign
    kv = pl.ds(0, 2)

    def tile(o):
        return (t + TOKS - sign * o) % TOKS

    def z_local(b):
        count, g0 = groups_of(b)
        gs = pl.ds(g0, count)
        return pltpu.make_async_copy(ST.at[t // 2, gs], R.at[t, gs], z_l.at[b])

    def z_send(b, i):
        count, g0 = groups_of(b)
        gs = pl.ds(g0, count)
        p, z_query = job(i)
        return remote(ST.at[p, gs], R.at[t, gs], z_s.at[i, b], z_r.at[t, b], tok=z_query)

    def z_near(b, o):
        count, g0 = groups_of(b)
        block = R.at[tile(o), pl.ds(g0, count)]
        return remote(block, block, z_s.at[0, b], z_r.at[tile(o), b], tok=partner)

    def z_hand(b, o):
        count, g0 = groups_of(b)
        gs = pl.ds(g0, count)
        src = ST.at[t // 2, gs, kv] if o == 0 else R.at[tile(o), gs, kv]
        return remote(src, R.at[tile(o), gs, kv], f_s.at[o, b], f_r.at[tile(o), b], tok=partner)

    def z_far(b, o):
        count, g0 = groups_of(b)
        block = R.at[tile(o), pl.ds(g0, count), kv]
        return remote(block, block, f_s.at[0, b], f_r.at[tile(o), b], tok=partner)

    def send_batch(b):
        for i in (2, 1, 3):
            z_send(b, i).start()
        z_local(b).start()
        z_hand(b, 0).start()

    def z_both(b, i):
        count, g0 = groups_of(b)
        gs = pl.ds(g0, count)
        p, z_query = job(i)
        other = 4 * p + 1 - z_query
        return remote(ST.at[p, gs, kv], R.at[t, gs, kv], f_s.at[i, b], f_r.at[t, b], tok=other)

    def hand_on(b):
        for o in range(1, RING):
            z_near(b, o).wait_recv()
            z_hand(b, o).start()

    def units(first, count):
        def step(i, carry):
            cols = pl.ds(pl.multiple_of(i * 256, 256), 256)
            ACT[first : first + count, cols] = jax.nn.gelu(
                dot_f32(N[first : first + count, :], WMI[:, cols]), approximate=True
            ).astype(BF16)
            return carry

        lax.fori_loop(0, UNITS // 256, step, 0)

    def units_out(first, count):
        def step(i, carry):
            cols = pl.ds(pl.multiple_of(i * 256, 256), 256)
            for h in range(2):
                ACC[h, first : first + count, cols] = dot_f32(ACT[first : first + count, :], WMO[h, :, cols])
            return carry

        lax.fori_loop(0, HALF // 256, step, 0)

    def take(b):
        modulate(b)
        qkv(b)
        send_batch(b)

    take(0)
    ag_recv((4, 5))
    ag_start((12, 13))
    ag_recv((6, 7))
    ag_start((14, 15))
    take(1)
    take(2)
    units(0, 192)
    ag_recv((8, 9))
    ag_start((16, 17))
    take(3)
    for b in range(3):
        hand_on(b)
    for i in range(4, 6):
        local_w[i].wait()
        remote_w[i].wait_recv()
    units_out(0, 192)
    ag_recv((10, 11))
    ag_start((18, 19))
    take(4)
    hand_on(3)
    units(192, 192)
    ag_recv(range(12, 16))
    take(5)
    hand_on(4)
    ag_recv(range(16, 20))
    take(6)
    for i in (2, 1, 3):
        z_both(6, i).start()
    hand_on(5)
    units(384, 192)
    units(576, 192)
    units_out(192, 384)
    units_out(576, 192)
    for o in range(1, RING):
        z_near(6, o).wait_recv()

    for b in range(len(batches)):
        z_local(b).wait()
        for o in range(RING, TOKS):
            z_far(b, o).wait_recv()
    own_p = t // 2

    def attend(o):
        keys = R[:, :, 0].reshape(TOKS * SLOTS, HEAD)
        vals = R[:, :, 1].reshape(TOKS * SLOTS, HEAD)
        query = R[tile(o), :, 2].reshape(SLOTS, HEAD)
        soft = jnp.exp2(dot_t(query, keys) * soft_scale) * MASK[...]
        total = jnp.sum(soft, axis=-1, keepdims=True)
        return (dot_f32(soft.astype(BF16), vals) / total).astype(BF16)

    for o in range(1, RING):
        OS[o] = attend(o)
        remote(OS.at[o], OR.at[own_p], o_s.at[o], o_r.at[own_p], tok=tile(o)).start()
    OR[own_p] = attend(0)

    for i in range(1, PROMPTS):
        p, z_query = job(i)
        remote(OS.at[0], OR.at[p], o_s.at[0], o_r.at[p], tok=z_query).wait_recv()
    for p in range(PROMPTS):
        ATT[pl.ds(p, SLOTS, stride=PROMPTS), :] = OR[p].astype(F32)

    rel_v = {0: 0, 1: 1, 3: 2, 2: 3}

    def out_rows(first, blocks):
        count = len(blocks) * PIECE
        att = ATT[first : first + count, :].astype(BF16)
        for h in range(2):
            for n in range(HALF // 512):
                cols = slice(n * 512, (n + 1) * 512)
                part = dot_f32(att, WAO[h, :, cols]) + ACC[h, first : first + count, cols]
                for i, (k, dv, j) in enumerate(blocks):
                    PS[k, rel_v[dv], j, :, h * HALF + n * 512 : h * HALF + (n + 1) * 512] = part[
                        i * PIECE : (i + 1) * PIECE
                    ].astype(BF16)

    def rs(k, i):
        u, v = uv[k]
        sems = (rs_s.at[k, i], rs_r.at[k, i])
        up, um = {"mlp": at_uv(k, (u + 1) % RING, v)}, {"mlp": at_uv(k, (u + 3) % RING, v)}
        vp, vm = {"mlp": at_uv(k, u, (v + 1) % RING)}, {"mlp": at_uv(k, u, (v + 3) % RING)}
        if i < 16:
            j, d = 3 - (i % 8) // 2, i % 2
            where = vp if d == 0 else vm
            if i < 8:
                block = PS.at[k, 3, j, :, lo if d == 0 else hi]
                return remote(block, RB.at[k, d, j], *sems, **where)
            block = PS.at[k, 1 + d, j]
            return remote(block, RC.at[k, d, j], *sems, **where)
        d = i % 2
        where = up if d == 0 else um
        if i < 18:
            return remote(PS2.at[k, 0, :, lo if d == 0 else hi], RB2.at[k, d], *sems, **where)
        return remote(PS2.at[k, 1 + d], RC2.at[k, d], *sems, **where)

    for half in (1, 0):
        out_rows(starts[5 + half], batches[5 + half])
        for i in range(4 * (1 - half), 4 * (1 - half) + 4):
            for k in range(2):
                rs(k, i).start()
    for step in range(RING):
        j = 3 - step
        out_rows(starts[1 + j], batches[1 + j])
        for d in range(2):
            for k in range(2):
                rs(k, 2 * step + d).wait_recv()
                cols = slice(0, HALF) if d == 0 else slice(HALF, D)
                PS[k, 1 + d, j, :, cols] = (
                    PS[k, 1 + d, j, :, cols].astype(F32) + RB[k, d, j].astype(F32)
                ).astype(BF16)
                rs(k, 8 + 2 * step + d).start()
    out_rows(0, batches[0])

    def own_sum(k, j):
        for d in range(2):
            rs(k, 8 + 2 * (3 - j) + d).wait_recv()
        return PS[k, 0, j].astype(F32) + RC[k, 0, j].astype(F32) + RC[k, 1, j].astype(F32)

    for k in range(2):
        PS2[k, 0] = own_sum(k, 3).astype(BF16)
        rs(k, 16).start()
        rs(k, 17).start()
    for d in range(2):
        for k in range(2):
            total = own_sum(k, 2 - d)
            rs(k, 16 + d).wait_recv()
            cols = slice(0, HALF) if d == 0 else slice(HALF, D)
            PS2[k, 1 + d] = total.astype(BF16)
            PS2[k, 1 + d, :, cols] = (total[:, cols] + RB2[k, d].astype(F32)).astype(BF16)
            rs(k, 18 + d).start()
    fin_copy.wait()
    finals = []
    for k in range(2):
        branch = own_sum(k, 0)
        for d in range(2):
            rs(k, 18 + d).wait_recv()
        branch = branch + RC2[k, 0].astype(F32) + RC2[k, 1].astype(F32)
        rows = slice(k * PIECE, (k + 1) * PIECE)
        gated = branch.reshape(3, 8, D) * MOD[:, 2 * D : 3 * D][None]
        stream = (HID[rows, :] + gated.reshape(PIECE, D)).astype(BF16)
        stream32 = stream.astype(F32)
        for i in range(PIECE // PROMPTS):
            stream_ref[k * (PIECE // PROMPTS) + i] = stream32[i * PROMPTS : (i + 1) * PROMPTS].astype(BF16)
        shaped = layer_norm(stream32).reshape(3, 8, D)
        shaped = shaped * MOD[:, 4 * D : 5 * D][None] + MOD[:, 3 * D : 4 * D][None]
        finals.append(shaped.reshape(PIECE, D).astype(BF16).astype(F32))
    final_normed = jnp.concatenate(finals, axis=0).astype(BF16)
    half_velocity = dot_t(final_normed, WFIN[...])
    parts = (half_velocity[:, :CH_HALF] * IMAGE[...], half_velocity[:, CH_HALF:] * IMAGE[...])
    first = c == 0
    VS[...] = jnp.where(first, parts[1], parts[0])
    swap = remote(VS, VR, v_s, v_r, cfg=1 - c)
    swap.start()
    own = jnp.where(first, parts[0], parts[1])
    swap.wait_recv()
    other = VR[...]
    cond = jnp.where(first, own, other)
    uncond = jnp.where(first, other, own)
    for i in range(ROWS_OWN // PROMPTS):
        rows = slice(i * PROMPTS, (i + 1) * PROMPTS)
        cond_ref[i] = cond[rows]
        uncond_ref[i] = uncond[rows]

    swap.wait_send()
    for copy in remote_w:
        copy.wait_send()
    span1.wait_send()
    span2.wait_send()
    for k in range(2):
        for i in range(20):
            ag(k, i).wait_send()
            rs(k, i).wait_send()
    for b in range(len(batches)):
        for i in range(1, PROMPTS):
            z_send(b, i).wait_send()
        for o in range(RING):
            (z_both(b, o) if b == 6 and o else z_hand(b, o)).wait_send()
    for o in range(1, RING):
        remote(OS.at[o], OR.at[own_p], o_s.at[o], o_r.at[own_p], tok=tile(o)).wait_send()


def call_kernel(*operands):
    vmem = pl.BlockSpec(memory_space=pltpu.VMEM)
    hbm = pl.BlockSpec(memory_space=pl.ANY)
    dma = pltpu.SemaphoreType.DMA
    scratch = [
        pltpu.VMEM((ROWS_OWN, D), F32),
        pltpu.VMEM((16, TOKS * SLOTS), F32),
        pltpu.VMEM((PROMPTS, 2 * RING, PIECE, HEAD), F32),
        pltpu.VMEM((PROMPTS, 2 * RING, PIECE, HEAD), F32),
        pltpu.VMEM((1, TOKS * SLOTS), F32),
        pltpu.VMEM((ROWS_OWN, CH_HALF), F32),
        pltpu.VMEM((2, HEAD), F32),
        pltpu.VMEM((2, RING, RING, PIECE, D), BF16),
        pltpu.VMEM((PROMPTS * SLOTS, D), BF16),
        pltpu.VMEM((MOD_COLS, D), BF16),
        pltpu.VMEM((D, 3 * HEAD), BF16),
        pltpu.VMEM((D, UNITS), BF16),
        pltpu.VMEM((2, HEAD, HALF), BF16),
        pltpu.VMEM((2, UNITS, HALF), BF16),
        pltpu.VMEM((2 * CH_HALF, D), BF16),
        pltpu.VMEM((TOKS, MLPS, PROMPTS, 128), F32),
        pltpu.VMEM((8, 5 * D), F32),
        pltpu.VMEM((3, STAGE, HEAD), F32),
        pltpu.VMEM((PROMPTS, 2 * RING, 3, PIECE, HEAD), BF16),
        pltpu.VMEM((TOKS, 2 * RING, 3, PIECE, HEAD), BF16),
        pltpu.VMEM((RING, SLOTS, HEAD), BF16),
        pltpu.VMEM((PROMPTS, SLOTS, HEAD), BF16),
        pltpu.VMEM((PROMPTS * SLOTS, HEAD), F32),
        pltpu.VMEM((PROMPTS * SLOTS, UNITS), BF16),
        pltpu.VMEM((2, PROMPTS * SLOTS, HALF), F32),
        pltpu.VMEM((2, RING, RING, PIECE, D), BF16),
        pltpu.VMEM((2, 2, RING, PIECE, HALF), BF16),
        pltpu.VMEM((2, 2, RING, PIECE, D), BF16),
        pltpu.VMEM((2, 3, PIECE, D), BF16),
        pltpu.VMEM((2, 2, PIECE, HALF), BF16),
        pltpu.VMEM((2, 2, PIECE, D), BF16),
        pltpu.VMEM((ROWS_OWN, CH_HALF), F32),
        pltpu.VMEM((ROWS_OWN, CH_HALF), F32),
        dma((2, 20)), dma((2, 20)), dma((2, 20)), dma((2, 20)),
        dma((8,)), dma((6,)), dma((6,)), dma((2,)), dma((2,)),
        dma((7,)), dma((PROMPTS, 7)), dma((TOKS, 7)), dma((RING, 7)), dma((TOKS, 7)),
        dma((RING,)), dma((PROMPTS,)), dma, dma,
    ]
    return pl.pallas_call(
        kernel,
        out_shape=(
            jax.ShapeDtypeStruct((ROWS_OWN // PROMPTS, PROMPTS, CH_HALF), F32),
            jax.ShapeDtypeStruct((ROWS_OWN // PROMPTS, PROMPTS, CH_HALF), F32),
            jax.ShapeDtypeStruct((ROWS_OWN // PROMPTS, PROMPTS, D), BF16),
        ),
        in_specs=[vmem] * 7 + [hbm] * 6,
        out_specs=(vmem, vmem, vmem),
        scratch_shapes=scratch,
        compiler_params=pltpu.CompilerParams(
            collective_id=0, has_side_effects=True, vmem_limit_bytes=67043328
        ),
    )(*operands)


def slot_places():
    blocks = [(k, 0, j) for k in range(2) for j in range(RING)]
    blocks += [(k, dv, j) for j in range(RING) for k in range(2) for dv in (1, 3)]
    blocks += [(k, 2, j) for half in range(2) for k in range(2) for j in (2 * half, 2 * half + 1)]
    rows = []
    for k, dv, j in blocks:
        du = (0, 3, 1, 2)[j]
        dx, dy = (du, dv) if k == 0 else (dv, du)
        rows += [(dx, dy, 6 * k + i) for i in range(6)]
    return np.array(rows, np.int32)


def rope_table():
    pairs = HEAD // 2
    first_pairs = HEAD // 16
    axis_pairs = (HEAD - HEAD // 8) // 4
    index = np.arange(pairs, dtype=np.float32)
    in_rows = (index >= first_pairs) & (index < first_pairs + axis_pairs)
    in_cols = index >= first_pairs + axis_pairs
    log_base = np.float32(math.log(ROPE_BASE))
    table = np.zeros((2 * SIDE, 2 * HEAD), np.float32)
    for pos in range(SIDE):
        for base, inside, start in ((0, in_rows, first_pairs), (SIDE, in_cols, first_pairs + axis_pairs)):
            freq = np.exp(-log_base * (index - np.float32(start)) / np.float32(axis_pairs)).astype(np.float32)
            angle = np.where(inside, np.float32(pos) * freq, 0.0).astype(np.float32)
            still = ~(in_rows | in_cols) if base == 0 else np.zeros_like(inside)
            cosine = np.where(inside, np.cos(angle), np.where(still, 1.0, 0.0))
            sine = np.where(inside, np.sin(angle), 0.0)
            table[base + pos] = np.concatenate([cosine, cosine, -sine, sine])
    parts, left = [], table
    for _ in range(3):
        part = left.astype(jnp.bfloat16)
        parts.append(part)
        left = left - part.astype(np.float32)
    return np.concatenate(parts, axis=0)


def on_device(
    hidden, latents, vec, slot_token, text_len, step_index, guidance,
    w_mod, w_qkv, w_mlp_in, qk_gain, w_attn_out, w_mlp_out, w_final,
):
    cond, uncond, stream = call_kernel(
        hidden[0], vec[0], slot_token, text_len, qk_gain[0], jnp.asarray(slot_places()), jnp.asarray(rope_table()),
        w_mod.T, w_qkv[0].transpose(1, 0, 2), w_mlp_in[0], w_attn_out[0], w_mlp_out[0], w_final.T,
    )
    velocity = uncond + guidance[0] * (cond - uncond)
    current = step_index[0].astype(F32)
    step_size = sigma_at(current + 1.0, STEPS) - sigma_at(current, STEPS)
    return velocity, latents + step_size * velocity, stream[None]


def solution(mesh):
    return jax.shard_map(
        on_device,
        mesh=mesh,
        in_specs=(
            P("cfg", ("tok", "mlp"), None, None),
            P(("tok", "mlp"), None, "cfg"),
            P("cfg", None, None),
            P(),
            P("cfg", None),
            P(),
            P(),
            P(None, ("tok", "mlp")),
            P(None, "cfg", None, "mlp"),
            P(None, "cfg", "mlp"),
            P(),
            P(None, "mlp", "cfg"),
            P(None, "mlp", "cfg"),
            P(),
        ),
        out_specs=(
            P(("tok", "mlp"), None, "cfg"),
            P(("tok", "mlp"), None, "cfg"),
            P("cfg", ("tok", "mlp"), None, None),
        ),
        check_vma=False,
    )
```

```python
import math

import jax
import jax.numpy as jnp
import numpy as np
from jax import lax
from jax.experimental import pallas as pl
from jax.experimental.pallas import tpu as pltpu
from jax.sharding import PartitionSpec as P

SIDE = 32
TXT = 512
STEPS = 28
EPSILON = 1e-06
ROPE_BASE = 10000.0
TIME_SHIFT = 3.0

MESH = pl.DeviceIdType.MESH
F32 = jnp.float32
BF16 = jnp.bfloat16

D = 3072
HALF = D // 2
HEAD = 128
UNITS = 768
PROMPTS = 4
RING = 4
TOKS = 8
MLPS = 16
PIECE = 24
CHUNK = RING * PIECE
STAGE = 2 * CHUNK
SLOTS = 192
ROWS_OWN = 2 * PIECE
MOD_COLS = 120
CH_HALF = 32


def sigma_at(position, steps_total):
    remain = 1.0 - position / steps_total
    return TIME_SHIFT * remain / (1.0 + (TIME_SHIFT - 1.0) * remain)


def layer_norm(values):
    average = jnp.mean(values, axis=-1, keepdims=True)
    centred = values - average
    spread = jnp.mean(centred * centred, axis=-1, keepdims=True)
    return centred * lax.rsqrt(spread + EPSILON)


def dot_f32(a, b):
    return jnp.dot(a, b, preferred_element_type=F32)


def dot_t(a, b):
    return lax.dot_general(a, b, (((1,), (1,)), ((), ())), preferred_element_type=F32)


def kernel(
    hid_hbm, vec_hbm, token_hbm, len_hbm, gain_hbm, place_hbm, tab_hbm,
    wmod_hbm, wqkv_hbm, wmi_hbm, wao_hbm, wmo_hbm, wfin_hbm,
    cond_ref, uncond_ref, stream_hbm,
    hid_ref, vec_ref, token_ref, len_ref, gain_ref, place_ref, tab_ref, stream_ref, HID, TT, COS, SIN, MASK, IMAGE, GAIN, X, N, WMOD, WQKV, WMI, WAO, WMO, WFIN, G, MOD, QF, ST, R, OS, OR, ATT,
    ACT, ACC, PS, RB, RC, PS2, RB2, RC2, VS, VR,
    ag_s, ag_r, rs_s, rs_r, w_l, w_s, w_r, m_s, m_r, z_l, z_s, z_r, f_s, f_r, o_s, o_r, v_s, v_r, in_l, out_l,
):
    c = lax.axis_index("cfg")
    t = lax.axis_index("tok")
    m = lax.axis_index("mlp")
    x, y = m // RING, m % RING
    uv = ((x, y), (y, x))

    def at_uv(k, u, v):
        return u * RING + v if k == 0 else v * RING + u

    def remote(src, dst, ssem, rsem, **where):
        return pltpu.make_async_remote_copy(
            src_ref=src, dst_ref=dst, send_sem=ssem, recv_sem=rsem,
            device_id=where, device_id_type=MESH,
        )

    barrier = pltpu.get_barrier_semaphore()
    for d in range(1, MLPS):
        pl.semaphore_signal(barrier, inc=1, device_id={"mlp": (m + d) % MLPS}, device_id_type=MESH)
    for d in range(1, TOKS):
        pl.semaphore_signal(barrier, inc=1, device_id={"tok": (t + d) % TOKS}, device_id_type=MESH)
    pl.semaphore_signal(barrier, inc=1, device_id={"cfg": 1 - c}, device_id_type=MESH)

    inputs = [
        pltpu.make_async_copy(src, dst, in_l.at[i])
        for i, (src, dst) in enumerate((
            (hid_hbm, hid_ref), (vec_hbm, vec_ref), (token_hbm, token_ref), (len_hbm, len_ref),
            (gain_hbm, gain_ref), (place_hbm, place_ref), (tab_hbm, tab_ref),
        ))
    ]
    for copy in inputs:
        copy.start()

    wmod_copy = pltpu.make_async_copy(wmod_hbm, WMOD, w_l.at[0])
    wmod_copy.start()
    k_rows = pl.ds(pl.multiple_of(c * HALF, HALF), HALF)
    weights = (
        [(wqkv_hbm.at[j], WQKV.at[k_rows, pl.ds(j * HEAD, HEAD)]) for j in range(3)]
        + [(wmi_hbm, WMI.at[k_rows]), (wao_hbm, WAO.at[c]), (wmo_hbm, WMO.at[c])]
    )
    local_w = [pltpu.make_async_copy(s, d, w_l.at[1 + i]) for i, (s, d) in enumerate(weights)]
    remote_w = [remote(s, d, w_s.at[i], w_r.at[i], cfg=1 - c) for i, (s, d) in enumerate(weights)]
    fin_copy = pltpu.make_async_copy(wfin_hbm, WFIN, w_l.at[7])

    inputs[0].wait()
    for i in range(ROWS_OWN // PROMPTS):
        HID[i * PROMPTS : (i + 1) * PROMPTS, :] = hid_ref[i].astype(F32)
    normed = layer_norm(HID[...]).astype(BF16)
    X[0, y, x] = normed[:PIECE]
    X[1, x, y] = normed[PIECE:]

    inputs[1].wait()
    vec = vec_ref[...]
    silu_vec = (vec * (1.0 / (1.0 + jnp.exp(-vec)))).astype(BF16)
    wmod_copy.wait()
    G[t, m, :, 0:MOD_COLS] = dot_t(silu_vec, WMOD[...]).astype(BF16)
    pl.semaphore_wait(barrier, MLPS - 1 + TOKS - 1 + 1)
    mod1 = [
        remote(G.at[t, m], G.at[t, m], m_s.at[0], m_r.at[0], mlp=(m + d) % MLPS) for d in range(1, MLPS)
    ]
    for copy in mod1:
        copy.start()

    lo, hi = pl.ds(0, HALF), pl.ds(HALF, HALF)

    def order_u(u, j):
        return (u, (u + 3) % RING, (u + 1) % RING, (u + 2) % RING)[j]

    def ag(k, i):
        u, v = uv[k]
        sems = (ag_s.at[k, i], ag_r.at[k, i])
        up, um = {"mlp": at_uv(k, (u + 1) % RING, v)}, {"mlp": at_uv(k, (u + 3) % RING, v)}
        vp, vm = {"mlp": at_uv(k, u, (v + 1) % RING)}, {"mlp": at_uv(k, u, (v + 3) % RING)}
        if i < 2:
            block = X.at[k, v, u]
            return remote(block, block, *sems, **(up if i == 0 else um))
        if i < 4:
            block = X.at[k, v, (u + (3 if i == 2 else 1)) % RING, :, lo if i == 2 else hi]
            return remote(block, block, *sems, **(up if i == 2 else um))
        if i < 12:
            j, d = (i - 4) // 2, (i - 4) % 2
            block = X.at[k, v, order_u(u, j)]
            return remote(block, block, *sems, **(vp if d == 0 else vm))
        j, d = (i - 12) // 2, (i - 12) % 2
        block = X.at[k, (v + (3 if d == 0 else 1)) % RING, order_u(u, j), :, lo if d == 0 else hi]
        return remote(block, block, *sems, **(vp if d == 0 else vm))

    def ag_start(ids):
        for i in ids:
            for k in range(2):
                ag(k, i).start()

    def ag_recv(ids):
        for i in ids:
            for k in range(2):
                ag(k, i).wait_recv()

    ag_start((0, 1, 4, 5))

    for copy in local_w[:3]:
        copy.start()
    for copy in remote_w[:3]:
        copy.start()
    for i in range(3, 6):
        local_w[i].start()
        remote_w[i].start()
    fin_copy.start()

    for copy in inputs[2:]:
        copy.wait()
    tokens = token_ref[...]
    is_image = tokens >= TXT
    place = jnp.where(is_image, tokens - TXT, 0)
    TT[0:4, :] = (place // SIDE).astype(F32)
    TT[4:8, :] = (place % SIDE).astype(F32)
    TT[8:12, :] = jnp.where(is_image, 1.0, 0.0)
    TT[12:16, :] = jnp.zeros((4, TOKS * SLOTS), F32)
    kinds = TT[...].astype(BF16)

    def lanes(shape):
        return lax.broadcasted_iota(jnp.int32, shape, 1)

    place_x = (place_ref[:, 0:1] + x) % RING
    place_y = (place_ref[:, 1:2] + y) % RING
    natural = (RING * place_x + place_y) * (ROWS_OWN // PROMPTS) + place_ref[:, 2:3]
    chosen = jnp.where(lanes((SLOTS, TOKS * SLOTS)) == natural + t * SLOTS, 1.0, 0.0).astype(BF16)
    picked = dot_t(chosen, kinds)
    lane192 = lanes((SLOTS, SLOTS))
    for p in range(PROMPTS):
        wanted_pos = jnp.where(lane192 % 64 < 32, picked[:, p : p + 1], picked[:, 4 + p : 5 + p])
        hot = jnp.where((lane192 % 32).astype(F32) == wanted_pos, 1.0, 0.0).astype(BF16)
        both = dot_f32(hot, tab_ref[...])
        COS[p] = both[:, :HEAD].reshape(2 * RING, PIECE, HEAD)
        SIN[p] = both[:, HEAD:].reshape(2 * RING, PIECE, HEAD)
    sub = lax.broadcasted_iota(jnp.int32, (ROWS_OWN, TOKS * SLOTS), 0)
    chosen = jnp.where(
        lanes((ROWS_OWN, TOKS * SLOTS)) == sub // PROMPTS + (t * MLPS + m) * (ROWS_OWN // PROMPTS), 1.0, 0.0
    ).astype(BF16)
    sub16 = lax.broadcasted_iota(jnp.int32, (ROWS_OWN, 16), 0)
    own_image = jnp.where(lanes((ROWS_OWN, 16)) == 8 + sub16 % PROMPTS, dot_t(chosen, kinds), 0.0)
    IMAGE[...] = jnp.broadcast_to(jnp.sum(own_image, axis=-1, keepdims=True), (ROWS_OWN, CH_HALF))
    this = lax.broadcasted_iota(jnp.int32, (PROMPTS, TOKS * SLOTS), 0) == t // 2
    job_tokens = jnp.sum(jnp.where(this, tokens.astype(F32), 0.0), axis=0, keepdims=True)
    job_len = jnp.sum(
        jnp.where(lanes((1, PROMPTS)) == t // 2, len_ref[...].astype(F32), 0.0), axis=-1, keepdims=True
    )
    valid = jnp.where((job_tokens >= TXT) | (job_tokens < job_len), 1.0, 0.0)
    valid = jnp.concatenate([valid[:, i * SLOTS : (i + 1) * SLOTS] for i in range(TOKS)], axis=0)
    valid = dot_t(valid.astype(BF16), jnp.where(lane192 == natural, 1.0, 0.0).astype(BF16))
    MASK[...] = jnp.concatenate([valid[i : i + 1, :] for i in range(TOKS)], axis=1)

    ag_recv((0, 1))
    ag_start((2, 3, 6, 7, 8, 9))

    span1 = remote(G.at[t, pl.ds(0, MLPS - 1)], G.at[t, pl.ds(0, MLPS - 1)], m_s.at[0], m_r.at[0], mlp=(m + 1) % MLPS)
    span1.wait_recv()
    mod2 = [remote(G.at[t], G.at[t], m_s.at[1], m_r.at[1], tok=(t + d) % TOKS) for d in range(1, TOKS)]
    for copy in mod2:
        copy.start()

    ag_recv((2, 3))
    ag_start((10, 11))

    for copy in local_w[:3]:
        copy.wait()
    for copy in remote_w[:3]:
        copy.wait_recv()
    src_col = lax.broadcasted_iota(jnp.int32, (HEAD, HEAD), 0)
    out_col = lax.broadcasted_iota(jnp.int32, (HEAD, HEAD), 1)
    wanted = jnp.where(out_col < HEAD // 2, 2 * out_col, 2 * out_col - HEAD + 1)
    permute = jnp.where(src_col == wanted, 1.0, 0.0).astype(BF16)

    gain = gain_ref[...]
    gain_sum = jnp.zeros((2, HEAD), F32)
    for _ in range(3):
        part = gain.astype(BF16)
        gain_sum = gain_sum + dot_f32(part, permute)
        gain = gain - part.astype(F32)
    GAIN[...] = gain_sum

    def permute_step(i, carry):
        rows = pl.ds(pl.multiple_of(i * 512, 512), 512)
        for j in range(2):
            cols = pl.ds(j * HEAD, HEAD)
            WQKV[rows, cols] = dot_f32(WQKV[rows, cols], permute).astype(BF16)
        return carry

    lax.fori_loop(0, D // 512, permute_step, 0)

    span2 = remote(
        G.at[pl.ds(0, TOKS - 1)], G.at[pl.ds(0, TOKS - 1)], m_s.at[1], m_r.at[1], tok=(t + 1) % TOKS
    )
    span2.wait_recv()
    lane = lax.broadcasted_iota(jnp.int32, (PROMPTS, 128), 1)

    def mod_step(i, carry):
        base = pl.multiple_of(i * (MLPS * MOD_COLS), 128)
        for j in range(15):
            shift = (8 * j) % MOD_COLS
            first = G[i, j].astype(F32)
            if shift:
                first = pltpu.roll(first, 128 - shift, 1)
            second = pltpu.roll(G[i, j + 1].astype(F32), MOD_COLS - shift, 1)
            index = i * 15 + j
            is_scale = jnp.where(((index >= 24) & (index < 48)) | (index >= 96), 1.0, 0.0)
            both = jnp.where(lane < MOD_COLS - shift, first, second) + is_scale
            MOD[:, pl.ds(base + j * 128, 128)] = jnp.concatenate([both, both], axis=0)
        return carry

    lax.fori_loop(0, TOKS, mod_step, 0)

    for i in range(3, 4):
        local_w[i].wait()
        remote_w[i].wait_recv()

    batches = [[(k, 0, j) for k in range(2) for j in range(RING)]]
    batches += [[(k, dv, j) for k in range(2) for dv in (1, 3)] for j in range(RING)]
    batches += [[(k, 2, j) for k in range(2) for j in (2 * half, 2 * half + 1)] for half in range(2)]
    starts = (0, 192, 288, 384, 480, 576, 672)
    width = 768

    def modulate(b):
        blocks = batches[b]

        def step(i, carry):
            cols = pl.ds(pl.multiple_of(i * width, width), width)
            scale = MOD[:, pl.ds(pl.multiple_of(D + i * width, width), width)]
            shift = MOD[:, cols]
            for pair in range(0, len(blocks), 2):
                pieces = [
                    X[k, (uv[k][1] + dv) % RING, order_u(uv[k][0], j), :, cols].astype(F32).reshape(3, 8, width)
                    for k, dv, j in blocks[pair : pair + 2]
                ]
                both = jnp.concatenate(pieces, axis=0) * scale[None] + shift[None]
                first = starts[b] + pair * PIECE
                N[first : first + 48, cols] = both.reshape(48, width).astype(BF16)
            return carry

        lax.fori_loop(0, D // width, step, 0)

    soft_scale = math.log2(math.e) / math.sqrt(HEAD)

    def groups_of(b):
        return len(batches[b]) // RING, starts[b] // CHUNK

    def qkv(b):
        count, g0 = groups_of(b)
        rows_b = count * CHUNK
        pre = dot_f32(N[starts[b] : starts[b] + rows_b, :], WQKV[...])
        for j in range(3):
            QF[j, 0:rows_b] = pre[:, j * HEAD : (j + 1) * HEAD]
        for p in range(PROMPTS):
            rows = pl.ds(p, count * PIECE, stride=PROMPTS)
            cosine = COS[p, g0 : g0 + count].reshape(count * PIECE, HEAD)
            sine = SIN[p, g0 : g0 + count].reshape(count * PIECE, HEAD)
            outs = []
            for j in range(2):
                val = QF.at[j][rows, :]
                val = val * lax.rsqrt(jnp.mean(val * val, axis=-1, keepdims=True) + EPSILON) * GAIN[j : j + 1, :]
                outs.append((val * cosine + pltpu.roll(val, HEAD // 2, 1) * sine).astype(BF16))
            outs.append(QF.at[2][rows, :].astype(BF16))
            for place, val in ((0, outs[1]), (1, outs[2]), (2, outs[0])):
                for g in range(count):
                    ST[p, g0 + g, place] = val[g * PIECE : (g + 1) * PIECE]

    def job(i):
        p = (t // 2 + i) % PROMPTS
        rel = (t - 2 * p + TOKS) % TOKS
        half = 1 - ((rel + 7) % TOKS) // RING
        return p, 2 * p + half

    sign = 1 - 2 * (t % 2)
    partner = t + sign
    kv = pl.ds(0, 2)

    def tile(o):
        return (t + TOKS - sign * o) % TOKS

    def z_local(b):
        count, g0 = groups_of(b)
        gs = pl.ds(g0, count)
        return pltpu.make_async_copy(ST.at[t // 2, gs], R.at[t, gs], z_l.at[b])

    def z_send(b, i):
        count, g0 = groups_of(b)
        gs = pl.ds(g0, count)
        p, z_query = job(i)
        return remote(ST.at[p, gs], R.at[t, gs], z_s.at[i, b], z_r.at[t, b], tok=z_query)

    def z_near(b, o):
        count, g0 = groups_of(b)
        block = R.at[tile(o), pl.ds(g0, count)]
        return remote(block, block, z_s.at[0, b], z_r.at[tile(o), b], tok=partner)

    def z_hand(b, o):
        count, g0 = groups_of(b)
        gs = pl.ds(g0, count)
        src = ST.at[t // 2, gs, kv] if o == 0 else R.at[tile(o), gs, kv]
        return remote(src, R.at[tile(o), gs, kv], f_s.at[o, b], f_r.at[tile(o), b], tok=partner)

    def z_far(b, o):
        count, g0 = groups_of(b)
        block = R.at[tile(o), pl.ds(g0, count), kv]
        return remote(block, block, f_s.at[0, b], f_r.at[tile(o), b], tok=partner)

    def send_batch(b):
        for i in (2, 1, 3):
            z_send(b, i).start()
        z_local(b).start()
        z_hand(b, 0).start()

    def z_both(b, i):
        count, g0 = groups_of(b)
        gs = pl.ds(g0, count)
        p, z_query = job(i)
        other = 4 * p + 1 - z_query
        return remote(ST.at[p, gs, kv], R.at[t, gs, kv], f_s.at[i, b], f_r.at[t, b], tok=other)

    def hand_on(b):
        for o in range(1, RING):
            z_near(b, o).wait_recv()
            z_hand(b, o).start()

    def units(first, count):
        ACT[first : first + count, :] = jax.nn.gelu(
            dot_f32(N[first : first + count, :], WMI[...]), approximate=True
        ).astype(BF16)

    def units_out(first, count):
        def step(i, carry):
            cols = pl.ds(pl.multiple_of(i * 512, 512), 512)
            for h in range(2):
                ACC[h, first : first + count, cols] = dot_f32(ACT[first : first + count, :], WMO[h, :, cols])
            return carry

        lax.fori_loop(0, HALF // 512, step, 0)

    def take(b):
        modulate(b)
        qkv(b)
        send_batch(b)

    take(0)
    ag_recv((4, 5))
    ag_start((12, 13))
    ag_recv((6, 7))
    ag_start((14, 15))
    take(1)
    take(2)
    units(0, 192)
    ag_recv((8, 9))
    ag_start((16, 17))
    take(3)
    for b in range(3):
        hand_on(b)
    for i in range(4, 6):
        local_w[i].wait()
        remote_w[i].wait_recv()
    units_out(0, 192)
    ag_recv((10, 11))
    ag_start((18, 19))
    take(4)
    hand_on(3)
    units(192, 192)
    ag_recv(range(12, 16))
    take(5)
    hand_on(4)
    ag_recv(range(16, 20))
    take(6)
    for i in (2, 1, 3):
        z_both(6, i).start()
    hand_on(5)
    units(384, 192)
    units(576, 192)
    units_out(192, 384)
    units_out(576, 192)
    for o in range(1, RING):
        z_near(6, o).wait_recv()

    for b in range(len(batches)):
        z_local(b).wait()
        for o in range(RING, TOKS):
            z_far(b, o).wait_recv()
    own_p = t // 2

    def attend(o):
        keys = R[:, :, 0].reshape(TOKS * SLOTS, HEAD)
        vals = R[:, :, 1].reshape(TOKS * SLOTS, HEAD)
        query = R[tile(o), :, 2].reshape(SLOTS, HEAD)
        soft = jnp.exp2(dot_t(query, keys) * soft_scale) * MASK[...]
        total = jnp.sum(soft, axis=-1, keepdims=True)
        return (dot_f32(soft.astype(BF16), vals) / total).astype(BF16)

    for o in range(1, RING):
        OS[o] = attend(o)
        remote(OS.at[o], OR.at[own_p], o_s.at[o], o_r.at[own_p], tok=tile(o)).start()
    OR[own_p] = attend(0)

    for i in range(1, PROMPTS):
        p, z_query = job(i)
        remote(OS.at[0], OR.at[p], o_s.at[0], o_r.at[p], tok=z_query).wait_recv()
    for p in range(PROMPTS):
        ATT[pl.ds(p, SLOTS, stride=PROMPTS), :] = OR[p].astype(F32)

    rel_v = {0: 0, 1: 1, 3: 2, 2: 3}

    def out_rows(first, blocks):
        count = len(blocks) * PIECE
        att = ATT[first : first + count, :].astype(BF16)
        for h in range(2):
            for n in range(HALF // 512):
                cols = slice(n * 512, (n + 1) * 512)
                part = dot_f32(att, WAO[h, :, cols]) + ACC[h, first : first + count, cols]
                for i, (k, dv, j) in enumerate(blocks):
                    PS[k, rel_v[dv], j, :, h * HALF + n * 512 : h * HALF + (n + 1) * 512] = part[
                        i * PIECE : (i + 1) * PIECE
                    ].astype(BF16)

    def rs(k, i):
        u, v = uv[k]
        sems = (rs_s.at[k, i], rs_r.at[k, i])
        up, um = {"mlp": at_uv(k, (u + 1) % RING, v)}, {"mlp": at_uv(k, (u + 3) % RING, v)}
        vp, vm = {"mlp": at_uv(k, u, (v + 1) % RING)}, {"mlp": at_uv(k, u, (v + 3) % RING)}
        if i < 16:
            j, d = 3 - (i % 8) // 2, i % 2
            where = vp if d == 0 else vm
            if i < 8:
                block = PS.at[k, 3, j, :, lo if d == 0 else hi]
                return remote(block, RB.at[k, d, j], *sems, **where)
            block = PS.at[k, 1 + d, j]
            return remote(block, RC.at[k, d, j], *sems, **where)
        d = i % 2
        where = up if d == 0 else um
        if i < 18:
            return remote(PS2.at[k, 0, :, lo if d == 0 else hi], RB2.at[k, d], *sems, **where)
        return remote(PS2.at[k, 1 + d], RC2.at[k, d], *sems, **where)

    for half in (1, 0):
        out_rows(starts[5 + half], batches[5 + half])
        for i in range(4 * (1 - half), 4 * (1 - half) + 4):
            for k in range(2):
                rs(k, i).start()
    for step in range(RING):
        j = 3 - step
        out_rows(starts[1 + j], batches[1 + j])
        for d in range(2):
            for k in range(2):
                rs(k, 2 * step + d).wait_recv()
                cols = slice(0, HALF) if d == 0 else slice(HALF, D)
                PS[k, 1 + d, j, :, cols] = (
                    PS[k, 1 + d, j, :, cols].astype(F32) + RB[k, d, j].astype(F32)
                ).astype(BF16)
                rs(k, 8 + 2 * step + d).start()
    out_rows(0, batches[0])

    def own_sum(k, j):
        for d in range(2):
            rs(k, 8 + 2 * (3 - j) + d).wait_recv()
        return PS[k, 0, j].astype(F32) + RC[k, 0, j].astype(F32) + RC[k, 1, j].astype(F32)

    for k in range(2):
        PS2[k, 0] = own_sum(k, 3).astype(BF16)
        rs(k, 16).start()
        rs(k, 17).start()
    for d in range(2):
        for k in range(2):
            total = own_sum(k, 2 - d)
            rs(k, 16 + d).wait_recv()
            cols = slice(0, HALF) if d == 0 else slice(HALF, D)
            PS2[k, 1 + d] = total.astype(BF16)
            PS2[k, 1 + d, :, cols] = (total[:, cols] + RB2[k, d].astype(F32)).astype(BF16)
            rs(k, 18 + d).start()
    fin_copy.wait()
    finals = []
    stream_copy = pltpu.make_async_copy(stream_ref, stream_hbm, out_l)
    for k in range(2):
        branch = own_sum(k, 0)
        for d in range(2):
            rs(k, 18 + d).wait_recv()
        branch = branch + RC2[k, 0].astype(F32) + RC2[k, 1].astype(F32)
        rows = slice(k * PIECE, (k + 1) * PIECE)
        gated = branch.reshape(3, 8, D) * MOD[:, 2 * D : 3 * D][None]
        stream = (HID[rows, :] + gated.reshape(PIECE, D)).astype(BF16)
        stream32 = stream.astype(F32)
        for i in range(PIECE // PROMPTS):
            stream_ref[k * (PIECE // PROMPTS) + i] = stream32[i * PROMPTS : (i + 1) * PROMPTS].astype(BF16)
        shaped = layer_norm(stream32).reshape(3, 8, D)
        shaped = shaped * MOD[:, 4 * D : 5 * D][None] + MOD[:, 3 * D : 4 * D][None]
        finals.append(shaped.reshape(PIECE, D).astype(BF16).astype(F32))
    stream_copy.start()
    final_normed = jnp.concatenate(finals, axis=0).astype(BF16)
    half_velocity = dot_t(final_normed, WFIN[...])
    parts = (half_velocity[:, :CH_HALF] * IMAGE[...], half_velocity[:, CH_HALF:] * IMAGE[...])
    first = c == 0
    VS[...] = jnp.where(first, parts[1], parts[0])
    swap = remote(VS, VR, v_s, v_r, cfg=1 - c)
    swap.start()
    own = jnp.where(first, parts[0], parts[1])
    swap.wait_recv()
    other = VR[...]
    cond = jnp.where(first, own, other)
    uncond = jnp.where(first, other, own)
    for i in range(ROWS_OWN // PROMPTS):
        rows = slice(i * PROMPTS, (i + 1) * PROMPTS)
        cond_ref[i] = cond[rows]
        uncond_ref[i] = uncond[rows]

    stream_copy.wait()
    swap.wait_send()
    for copy in remote_w:
        copy.wait_send()
    span1.wait_send()
    span2.wait_send()
    for k in range(2):
        for i in range(20):
            ag(k, i).wait_send()
            rs(k, i).wait_send()
    for b in range(len(batches)):
        for i in range(1, PROMPTS):
            z_send(b, i).wait_send()
        for o in range(RING):
            (z_both(b, o) if b == 6 and o else z_hand(b, o)).wait_send()
    for o in range(1, RING):
        remote(OS.at[o], OR.at[own_p], o_s.at[o], o_r.at[own_p], tok=tile(o)).wait_send()


def call_kernel(*operands):
    vmem = pl.BlockSpec(memory_space=pltpu.VMEM)
    hbm = pl.BlockSpec(memory_space=pl.ANY)
    dma = pltpu.SemaphoreType.DMA
    scratch = [
        pltpu.VMEM((ROWS_OWN // PROMPTS, PROMPTS, D), BF16),
        pltpu.VMEM((PROMPTS, D), F32),
        pltpu.VMEM((PROMPTS, TOKS * SLOTS), jnp.int32),
        pltpu.VMEM((1, PROMPTS), jnp.int32),
        pltpu.VMEM((2, HEAD), F32),
        pltpu.VMEM((SLOTS, 3), jnp.int32),
        pltpu.VMEM((SLOTS, 2 * HEAD), BF16),
        pltpu.VMEM((ROWS_OWN // PROMPTS, PROMPTS, D), BF16),
        pltpu.VMEM((ROWS_OWN, D), F32),
        pltpu.VMEM((16, TOKS * SLOTS), F32),
        pltpu.VMEM((PROMPTS, 2 * RING, PIECE, HEAD), F32),
        pltpu.VMEM((PROMPTS, 2 * RING, PIECE, HEAD), F32),
        pltpu.VMEM((1, TOKS * SLOTS), F32),
        pltpu.VMEM((ROWS_OWN, CH_HALF), F32),
        pltpu.VMEM((2, HEAD), F32),
        pltpu.VMEM((2, RING, RING, PIECE, D), BF16),
        pltpu.VMEM((PROMPTS * SLOTS, D), BF16),
        pltpu.VMEM((MOD_COLS, D), BF16),
        pltpu.VMEM((D, 3 * HEAD), BF16),
        pltpu.VMEM((D, UNITS), BF16),
        pltpu.VMEM((2, HEAD, HALF), BF16),
        pltpu.VMEM((2, UNITS, HALF), BF16),
        pltpu.VMEM((2 * CH_HALF, D), BF16),
        pltpu.VMEM((TOKS, MLPS, PROMPTS, 128), BF16),
        pltpu.VMEM((8, 5 * D), F32),
        pltpu.VMEM((3, STAGE, HEAD), F32),
        pltpu.VMEM((PROMPTS, 2 * RING, 3, PIECE, HEAD), BF16),
        pltpu.VMEM((TOKS, 2 * RING, 3, PIECE, HEAD), BF16),
        pltpu.VMEM((RING, SLOTS, HEAD), BF16),
        pltpu.VMEM((PROMPTS, SLOTS, HEAD), BF16),
        pltpu.VMEM((PROMPTS * SLOTS, HEAD), F32),
        pltpu.VMEM((PROMPTS * SLOTS, UNITS), BF16),
        pltpu.VMEM((2, PROMPTS * SLOTS, HALF), F32),
        pltpu.VMEM((2, RING, RING, PIECE, D), BF16),
        pltpu.VMEM((2, 2, RING, PIECE, HALF), BF16),
        pltpu.VMEM((2, 2, RING, PIECE, D), BF16),
        pltpu.VMEM((2, 3, PIECE, D), BF16),
        pltpu.VMEM((2, 2, PIECE, HALF), BF16),
        pltpu.VMEM((2, 2, PIECE, D), BF16),
        pltpu.VMEM((ROWS_OWN, CH_HALF), F32),
        pltpu.VMEM((ROWS_OWN, CH_HALF), F32),
        dma((2, 20)), dma((2, 20)), dma((2, 20)), dma((2, 20)),
        dma((8,)), dma((6,)), dma((6,)), dma((2,)), dma((2,)),
        dma((7,)), dma((PROMPTS, 7)), dma((TOKS, 7)), dma((RING, 7)), dma((TOKS, 7)),
        dma((RING,)), dma((PROMPTS,)), dma, dma, dma((7,)), dma,
    ]
    return pl.pallas_call(
        kernel,
        out_shape=(
            jax.ShapeDtypeStruct((ROWS_OWN // PROMPTS, PROMPTS, CH_HALF), F32),
            jax.ShapeDtypeStruct((ROWS_OWN // PROMPTS, PROMPTS, CH_HALF), F32),
            jax.ShapeDtypeStruct((ROWS_OWN // PROMPTS, PROMPTS, D), BF16),
        ),
        in_specs=[hbm] * 13,
        out_specs=(vmem, vmem, hbm),
        scratch_shapes=scratch,
        compiler_params=pltpu.CompilerParams(
            collective_id=0, has_side_effects=True, vmem_limit_bytes=67043328
        ),
    )(*operands)


def slot_places():
    blocks = [(k, 0, j) for k in range(2) for j in range(RING)]
    blocks += [(k, dv, j) for j in range(RING) for k in range(2) for dv in (1, 3)]
    blocks += [(k, 2, j) for half in range(2) for k in range(2) for j in (2 * half, 2 * half + 1)]
    rows = []
    for k, dv, j in blocks:
        du = (0, 3, 1, 2)[j]
        dx, dy = (du, dv) if k == 0 else (dv, du)
        rows += [(dx, dy, 6 * k + i) for i in range(6)]
    return np.array(rows, np.int32)


def rope_table():
    pairs = HEAD // 2
    first_pairs = HEAD // 16
    axis_pairs = (HEAD - HEAD // 8) // 4
    index = np.arange(pairs, dtype=np.float32)
    in_rows = (index >= first_pairs) & (index < first_pairs + axis_pairs)
    in_cols = index >= first_pairs + axis_pairs
    log_base = np.float32(math.log(ROPE_BASE))
    table = np.zeros((2 * SIDE, 2 * HEAD), np.float32)
    for pos in range(SIDE):
        for base, inside, start in ((0, in_rows, first_pairs), (SIDE, in_cols, first_pairs + axis_pairs)):
            freq = np.exp(-log_base * (index - np.float32(start)) / np.float32(axis_pairs)).astype(np.float32)
            angle = np.where(inside, np.float32(pos) * freq, 0.0).astype(np.float32)
            still = ~(in_rows | in_cols) if base == 0 else np.zeros_like(inside)
            cosine = np.where(inside, np.cos(angle), np.where(still, 1.0, 0.0))
            sine = np.where(inside, np.sin(angle), 0.0)
            table[base + pos] = np.concatenate([cosine, cosine, -sine, sine])
    parts, left = [], table
    for _ in range(3):
        part = left.astype(jnp.bfloat16)
        parts.append(part)
        left = left - part.astype(np.float32)
    return np.concatenate(parts, axis=0)


def on_device(
    hidden, latents, vec, slot_token, text_len, step_index, guidance,
    w_mod, w_qkv, w_mlp_in, qk_gain, w_attn_out, w_mlp_out, w_final,
):
    cond, uncond, stream = call_kernel(
        hidden[0], vec[0], slot_token, text_len, qk_gain[0], jnp.asarray(slot_places()), jnp.asarray(rope_table()),
        w_mod.T, w_qkv[0].transpose(1, 0, 2), w_mlp_in[0], w_attn_out[0], w_mlp_out[0], w_final.T,
    )
    velocity = uncond + guidance[0] * (cond - uncond)
    current = step_index[0].astype(F32)
    step_size = sigma_at(current + 1.0, STEPS) - sigma_at(current, STEPS)
    return velocity, latents + step_size * velocity, stream[None]


def solution(mesh):
    return jax.shard_map(
        on_device,
        mesh=mesh,
        in_specs=(
            P("cfg", ("tok", "mlp"), None, None),
            P(("tok", "mlp"), None, "cfg"),
            P("cfg", None, None),
            P(),
            P("cfg", None),
            P(),
            P(),
            P(None, ("tok", "mlp")),
            P(None, "cfg", None, "mlp"),
            P(None, "cfg", "mlp"),
            P(),
            P(None, "mlp", "cfg"),
            P(None, "mlp", "cfg"),
            P(),
        ),
        out_specs=(
            P(("tok", "mlp"), None, "cfg"),
            P(("tok", "mlp"), None, "cfg"),
            P("cfg", ("tok", "mlp"), None, None),
        ),
        check_vma=False,
    )
```

```python
import math

import jax
import jax.numpy as jnp
import numpy as np
from jax import lax
from jax.experimental import pallas as pl
from jax.experimental.pallas import tpu as pltpu
from jax.sharding import PartitionSpec as P

SIDE = 32
TXT = 512
STEPS = 28
EPSILON = 1e-06
ROPE_BASE = 10000.0
TIME_SHIFT = 3.0

MESH = pl.DeviceIdType.MESH
F32 = jnp.float32
BF16 = jnp.bfloat16

D = 3072
HALF = D // 2
HEAD = 128
UNITS = 768
PROMPTS = 4
RING = 4
TOKS = 8
MLPS = 16
PIECE = 24
CHUNK = RING * PIECE
STAGE = 2 * CHUNK
SLOTS = 192
ROWS_OWN = 2 * PIECE
MOD_COLS = 120
CH_HALF = 32


def sigma_at(position, steps_total):
    remain = 1.0 - position / steps_total
    return TIME_SHIFT * remain / (1.0 + (TIME_SHIFT - 1.0) * remain)


def layer_norm(values):
    average = jnp.mean(values, axis=-1, keepdims=True)
    centred = values - average
    spread = jnp.mean(centred * centred, axis=-1, keepdims=True)
    return centred * lax.rsqrt(spread + EPSILON)


def dot_f32(a, b):
    return jnp.dot(a, b, preferred_element_type=F32)


def dot_t(a, b):
    return lax.dot_general(a, b, (((1,), (1,)), ((), ())), preferred_element_type=F32)


def kernel(
    hid_hbm, vec_hbm, token_hbm, len_hbm, gain_hbm, place_hbm, tab_hbm,
    wmod_hbm, wqkv_hbm, wmi_hbm, wao_hbm, wmo_hbm, wfin_hbm,
    cond_ref, uncond_ref, stream_hbm,
    hid_ref, vec_ref, token_ref, len_ref, gain_ref, place_ref, tab_ref, stream_ref, HID, TT, COS, SIN, MASK, IMAGE, GAIN, X, N, WMOD, WQKV, WMI, WAO, WMO, WFIN, G, MOD, QF, ST, R, OS, OR, ATT,
    ACT, ACC, PS, RB, RC, PS2, RB2, RC2, VS, VR,
    ag_s, ag_r, rs_s, rs_r, w_l, w_s, w_r, m_s, m_r, z_l, z_s, z_r, f_s, f_r, o_s, o_r, v_s, v_r, in_l, out_l,
):
    c = lax.axis_index("cfg")
    t = lax.axis_index("tok")
    m = lax.axis_index("mlp")
    x, y = m // RING, m % RING
    uv = ((x, y), (y, x))

    def at_uv(k, u, v):
        return u * RING + v if k == 0 else v * RING + u

    def remote(src, dst, ssem, rsem, **where):
        return pltpu.make_async_remote_copy(
            src_ref=src, dst_ref=dst, send_sem=ssem, recv_sem=rsem,
            device_id=where, device_id_type=MESH,
        )

    barrier = pltpu.get_barrier_semaphore()
    for d in range(1, MLPS):
        pl.semaphore_signal(barrier, inc=1, device_id={"mlp": (m + d) % MLPS}, device_id_type=MESH)
    for d in range(1, TOKS):
        pl.semaphore_signal(barrier, inc=1, device_id={"tok": (t + d) % TOKS}, device_id_type=MESH)
    pl.semaphore_signal(barrier, inc=1, device_id={"cfg": 1 - c}, device_id_type=MESH)

    inputs = [
        pltpu.make_async_copy(src, dst, in_l.at[i])
        for i, (src, dst) in enumerate((
            (hid_hbm, hid_ref), (vec_hbm, vec_ref), (token_hbm, token_ref), (len_hbm, len_ref),
            (gain_hbm, gain_ref), (place_hbm, place_ref), (tab_hbm, tab_ref),
        ))
    ]
    for copy in inputs:
        copy.start()

    wmod_copy = pltpu.make_async_copy(wmod_hbm, WMOD, w_l.at[0])
    wmod_copy.start()
    k_rows = pl.ds(pl.multiple_of(c * HALF, HALF), HALF)
    weights = (
        [(wqkv_hbm.at[j], WQKV.at[k_rows, pl.ds(j * HEAD, HEAD)]) for j in range(3)]
        + [(wmi_hbm, WMI.at[k_rows]), (wao_hbm, WAO.at[c]), (wmo_hbm, WMO.at[c])]
    )
    local_w = [pltpu.make_async_copy(s, d, w_l.at[1 + i]) for i, (s, d) in enumerate(weights)]
    remote_w = [remote(s, d, w_s.at[i], w_r.at[i], cfg=1 - c) for i, (s, d) in enumerate(weights)]
    fin_copy = pltpu.make_async_copy(wfin_hbm, WFIN, w_l.at[7])

    inputs[0].wait()
    for i in range(ROWS_OWN // PROMPTS):
        HID[i * PROMPTS : (i + 1) * PROMPTS, :] = hid_ref[i].astype(F32)
    normed = layer_norm(HID[...]).astype(BF16)
    X[0, y, x] = normed[:PIECE]
    X[1, x, y] = normed[PIECE:]

    inputs[1].wait()
    vec = vec_ref[...]
    silu_vec = (vec * (1.0 / (1.0 + jnp.exp(-vec)))).astype(BF16)
    wmod_copy.wait()
    G[t, m, :, 0:MOD_COLS] = dot_t(silu_vec, WMOD[...]).astype(BF16)
    pl.semaphore_wait(barrier, MLPS - 1 + TOKS - 1 + 1)
    mod1 = [
        remote(G.at[t, m], G.at[t, m], m_s.at[0], m_r.at[0], mlp=(m + d) % MLPS) for d in range(1, MLPS)
    ]
    for copy in mod1:
        copy.start()

    lo, hi = pl.ds(0, HALF), pl.ds(HALF, HALF)

    def order_u(u, j):
        return (u, (u + 3) % RING, (u + 1) % RING, (u + 2) % RING)[j]

    def ag(k, i):
        u, v = uv[k]
        sems = (ag_s.at[k, i], ag_r.at[k, i])
        up, um = {"mlp": at_uv(k, (u + 1) % RING, v)}, {"mlp": at_uv(k, (u + 3) % RING, v)}
        vp, vm = {"mlp": at_uv(k, u, (v + 1) % RING)}, {"mlp": at_uv(k, u, (v + 3) % RING)}
        if i < 2:
            block = X.at[k, v, u]
            return remote(block, block, *sems, **(up if i == 0 else um))
        if i < 4:
            block = X.at[k, v, (u + (3 if i == 2 else 1)) % RING, :, lo if i == 2 else hi]
            return remote(block, block, *sems, **(up if i == 2 else um))
        if i < 12:
            j, d = (i - 4) // 2, (i - 4) % 2
            block = X.at[k, v, order_u(u, j)]
            return remote(block, block, *sems, **(vp if d == 0 else vm))
        j, d = (i - 12) // 2, (i - 12) % 2
        block = X.at[k, (v + (3 if d == 0 else 1)) % RING, order_u(u, j), :, lo if d == 0 else hi]
        return remote(block, block, *sems, **(vp if d == 0 else vm))

    def ag_start(ids):
        for i in ids:
            for k in range(2):
                ag(k, i).start()

    def ag_recv(ids):
        for i in ids:
            for k in range(2):
                ag(k, i).wait_recv()

    ag_start((0, 1, 4, 5))

    for copy in local_w[:3]:
        copy.start()
    for copy in remote_w[:3]:
        copy.start()
    for i in range(3, 6):
        local_w[i].start()
        remote_w[i].start()
    fin_copy.start()

    for copy in inputs[2:]:
        copy.wait()
    tokens = token_ref[...]
    is_image = tokens >= TXT
    place = jnp.where(is_image, tokens - TXT, 0)
    TT[0:4, :] = (place // SIDE).astype(F32)
    TT[4:8, :] = (place % SIDE).astype(F32)
    TT[8:12, :] = jnp.where(is_image, 1.0, 0.0)
    TT[12:16, :] = jnp.zeros((4, TOKS * SLOTS), F32)
    kinds = TT[...].astype(BF16)

    def lanes(shape):
        return lax.broadcasted_iota(jnp.int32, shape, 1)

    place_x = (place_ref[:, 0:1] + x) % RING
    place_y = (place_ref[:, 1:2] + y) % RING
    natural = (RING * place_x + place_y) * (ROWS_OWN // PROMPTS) + place_ref[:, 2:3]
    chosen = jnp.where(lanes((SLOTS, TOKS * SLOTS)) == natural + t * SLOTS, 1.0, 0.0).astype(BF16)
    picked = dot_t(chosen, kinds)
    lane192 = lanes((SLOTS, SLOTS))
    for p in range(PROMPTS):
        wanted_pos = jnp.where(lane192 % 64 < 32, picked[:, p : p + 1], picked[:, 4 + p : 5 + p])
        hot = jnp.where((lane192 % 32).astype(F32) == wanted_pos, 1.0, 0.0).astype(BF16)
        both = dot_f32(hot, tab_ref[...])
        COS[p] = both[:, :HEAD].reshape(2 * RING, PIECE, HEAD)
        SIN[p] = both[:, HEAD:].reshape(2 * RING, PIECE, HEAD)
    sub = lax.broadcasted_iota(jnp.int32, (ROWS_OWN, TOKS * SLOTS), 0)
    chosen = jnp.where(
        lanes((ROWS_OWN, TOKS * SLOTS)) == sub // PROMPTS + (t * MLPS + m) * (ROWS_OWN // PROMPTS), 1.0, 0.0
    ).astype(BF16)
    sub16 = lax.broadcasted_iota(jnp.int32, (ROWS_OWN, 16), 0)
    own_image = jnp.where(lanes((ROWS_OWN, 16)) == 8 + sub16 % PROMPTS, dot_t(chosen, kinds), 0.0)
    IMAGE[...] = jnp.broadcast_to(jnp.sum(own_image, axis=-1, keepdims=True), (ROWS_OWN, CH_HALF))
    this = lax.broadcasted_iota(jnp.int32, (PROMPTS, TOKS * SLOTS), 0) == t // 2
    job_tokens = jnp.sum(jnp.where(this, tokens.astype(F32), 0.0), axis=0, keepdims=True)
    job_len = jnp.sum(
        jnp.where(lanes((1, PROMPTS)) == t // 2, len_ref[...].astype(F32), 0.0), axis=-1, keepdims=True
    )
    valid = jnp.where((job_tokens >= TXT) | (job_tokens < job_len), 1.0, 0.0)
    valid = jnp.concatenate([valid[:, i * SLOTS : (i + 1) * SLOTS] for i in range(TOKS)], axis=0)
    valid = dot_t(valid.astype(BF16), jnp.where(lane192 == natural, 1.0, 0.0).astype(BF16))
    MASK[...] = jnp.concatenate([valid[i : i + 1, :] for i in range(TOKS)], axis=1)

    ag_recv((0, 1))
    ag_start((2, 3, 6, 7, 8, 9))

    span1 = remote(G.at[t, pl.ds(0, MLPS - 1)], G.at[t, pl.ds(0, MLPS - 1)], m_s.at[0], m_r.at[0], mlp=(m + 1) % MLPS)
    span1.wait_recv()
    mod2 = [remote(G.at[t], G.at[t], m_s.at[1], m_r.at[1], tok=(t + d) % TOKS) for d in range(1, TOKS)]
    for copy in mod2:
        copy.start()

    ag_recv((2, 3))
    ag_start((10, 11))

    for copy in local_w[:3]:
        copy.wait()
    for copy in remote_w[:3]:
        copy.wait_recv()
    src_col = lax.broadcasted_iota(jnp.int32, (HEAD, HEAD), 0)
    out_col = lax.broadcasted_iota(jnp.int32, (HEAD, HEAD), 1)
    wanted = jnp.where(out_col < HEAD // 2, 2 * out_col, 2 * out_col - HEAD + 1)
    permute = jnp.where(src_col == wanted, 1.0, 0.0).astype(BF16)

    gain = gain_ref[...]
    gain_sum = jnp.zeros((2, HEAD), F32)
    for _ in range(3):
        part = gain.astype(BF16)
        gain_sum = gain_sum + dot_f32(part, permute)
        gain = gain - part.astype(F32)
    GAIN[...] = gain_sum

    def permute_step(i, carry):
        rows = pl.ds(pl.multiple_of(i * 512, 512), 512)
        for j in range(2):
            cols = pl.ds(j * HEAD, HEAD)
            WQKV[rows, cols] = dot_f32(WQKV[rows, cols], permute).astype(BF16)
        return carry

    lax.fori_loop(0, D // 512, permute_step, 0)

    span2 = remote(
        G.at[pl.ds(0, TOKS - 1)], G.at[pl.ds(0, TOKS - 1)], m_s.at[1], m_r.at[1], tok=(t + 1) % TOKS
    )
    span2.wait_recv()
    lane = lax.broadcasted_iota(jnp.int32, (PROMPTS, 128), 1)

    def mod_step(i, carry):
        base = pl.multiple_of(i * (MLPS * MOD_COLS), 128)
        for j in range(15):
            shift = (8 * j) % MOD_COLS
            first = G[i, j].astype(F32)
            if shift:
                first = pltpu.roll(first, 128 - shift, 1)
            second = pltpu.roll(G[i, j + 1].astype(F32), MOD_COLS - shift, 1)
            index = i * 15 + j
            is_scale = jnp.where(((index >= 24) & (index < 48)) | (index >= 96), 1.0, 0.0)
            both = jnp.where(lane < MOD_COLS - shift, first, second) + is_scale
            MOD[:, pl.ds(base + j * 128, 128)] = jnp.concatenate([both, both], axis=0)
        return carry

    lax.fori_loop(0, TOKS, mod_step, 0)

    for i in range(3, 4):
        local_w[i].wait()
        remote_w[i].wait_recv()

    batches = [[(k, 0, j) for k in range(2) for j in range(RING)]]
    batches += [[(k, dv, j) for k in range(2) for dv in (1, 3)] for j in range(RING)]
    batches += [[(k, 2, j) for k in range(2) for j in (2 * half, 2 * half + 1)] for half in range(2)]
    starts = (0, 192, 288, 384, 480, 576, 672)
    width = 768

    def modulate(b):
        blocks = batches[b]

        def step(i, carry):
            cols = pl.ds(pl.multiple_of(i * width, width), width)
            scale = MOD[:, pl.ds(pl.multiple_of(D + i * width, width), width)]
            shift = MOD[:, cols]
            for pair in range(0, len(blocks), 2):
                pieces = [
                    X[k, (uv[k][1] + dv) % RING, order_u(uv[k][0], j), :, cols].astype(F32).reshape(3, 8, width)
                    for k, dv, j in blocks[pair : pair + 2]
                ]
                both = jnp.concatenate(pieces, axis=0) * scale[None] + shift[None]
                first = starts[b] + pair * PIECE
                N[first : first + 48, cols] = both.reshape(48, width).astype(BF16)
            return carry

        lax.fori_loop(0, D // width, step, 0)

    soft_scale = math.log2(math.e) / math.sqrt(HEAD)

    def groups_of(b):
        return len(batches[b]) // RING, starts[b] // CHUNK

    def qkv(b):
        count, g0 = groups_of(b)
        rows_b = count * CHUNK
        pre = dot_f32(N[starts[b] : starts[b] + rows_b, :], WQKV[...])
        for j in range(3):
            QF[j, 0:rows_b] = pre[:, j * HEAD : (j + 1) * HEAD]
        for p in range(PROMPTS):
            rows = pl.ds(p, count * PIECE, stride=PROMPTS)
            cosine = COS[p, g0 : g0 + count].reshape(count * PIECE, HEAD)
            sine = SIN[p, g0 : g0 + count].reshape(count * PIECE, HEAD)
            outs = []
            for j in range(2):
                val = QF.at[j][rows, :]
                val = val * lax.rsqrt(jnp.mean(val * val, axis=-1, keepdims=True) + EPSILON) * GAIN[j : j + 1, :]
                outs.append((val * cosine + pltpu.roll(val, HEAD // 2, 1) * sine).astype(BF16))
            outs.append(QF.at[2][rows, :].astype(BF16))
            for place, val in ((0, outs[1]), (1, outs[2]), (2, outs[0])):
                for g in range(count):
                    ST[p, g0 + g, place] = val[g * PIECE : (g + 1) * PIECE]

    def job(i):
        p = (t // 2 + i) % PROMPTS
        rel = (t - 2 * p + TOKS) % TOKS
        half = 1 - ((rel + 7) % TOKS) // RING
        return p, 2 * p + half

    sign = 1 - 2 * (t % 2)
    partner = t + sign
    kv = pl.ds(0, 2)

    def tile(o):
        return (t + TOKS - sign * o) % TOKS

    def z_local(b):
        count, g0 = groups_of(b)
        gs = pl.ds(g0, count)
        return pltpu.make_async_copy(ST.at[t // 2, gs], R.at[t, gs], z_l.at[b])

    def z_send(b, i):
        count, g0 = groups_of(b)
        gs = pl.ds(g0, count)
        p, z_query = job(i)
        return remote(ST.at[p, gs], R.at[t, gs], z_s.at[i, b], z_r.at[t, b], tok=z_query)

    def z_near(b, o):
        count, g0 = groups_of(b)
        block = R.at[tile(o), pl.ds(g0, count)]
        return remote(block, block, z_s.at[0, b], z_r.at[tile(o), b], tok=partner)

    def z_hand(b, o):
        count, g0 = groups_of(b)
        gs = pl.ds(g0, count)
        src = ST.at[t // 2, gs, kv] if o == 0 else R.at[tile(o), gs, kv]
        return remote(src, R.at[tile(o), gs, kv], f_s.at[o, b], f_r.at[tile(o), b], tok=partner)

    def z_far(b, o):
        count, g0 = groups_of(b)
        block = R.at[tile(o), pl.ds(g0, count), kv]
        return remote(block, block, f_s.at[0, b], f_r.at[tile(o), b], tok=partner)

    def send_batch(b):
        for i in (2, 1, 3):
            z_send(b, i).start()
        z_local(b).start()
        z_hand(b, 0).start()

    def z_both(b, i):
        count, g0 = groups_of(b)
        gs = pl.ds(g0, count)
        p, z_query = job(i)
        other = 4 * p + 1 - z_query
        return remote(ST.at[p, gs, kv], R.at[t, gs, kv], f_s.at[i, b], f_r.at[t, b], tok=other)

    def hand_on(b):
        for o in range(1, RING):
            z_near(b, o).wait_recv()
            z_hand(b, o).start()

    def units(first, count):
        ACT[first : first + count, :] = jax.nn.gelu(
            dot_f32(N[first : first + count, :], WMI[...]), approximate=True
        ).astype(BF16)

    def units_out(first, count):
        def step(i, carry):
            cols = pl.ds(pl.multiple_of(i * 512, 512), 512)
            for h in range(2):
                ACC[h, first : first + count, cols] = dot_f32(ACT[first : first + count, :], WMO[h, :, cols])
            return carry

        lax.fori_loop(0, HALF // 512, step, 0)

    def take(b):
        modulate(b)
        qkv(b)
        send_batch(b)

    take(0)
    ag_recv((4, 5))
    ag_start((12, 13))
    ag_recv((6, 7))
    ag_start((14, 15))
    take(1)
    take(2)
    units(0, 192)
    ag_recv((8, 9))
    ag_start((16, 17))
    take(3)
    for b in range(3):
        hand_on(b)
    for i in range(4, 6):
        local_w[i].wait()
        remote_w[i].wait_recv()
    units_out(0, 192)
    ag_recv((10, 11))
    ag_start((18, 19))
    take(4)
    hand_on(3)
    units(192, 384)
    ag_recv(range(12, 16))
    take(5)
    hand_on(4)
    ag_recv(range(16, 20))
    take(6)
    for i in (2, 1, 3):
        z_both(6, i).start()
    hand_on(5)
    units(576, 192)
    units_out(192, 384)
    units_out(576, 192)
    for o in range(1, RING):
        z_near(6, o).wait_recv()

    for b in range(len(batches)):
        z_local(b).wait()
        for o in range(RING, TOKS):
            z_far(b, o).wait_recv()
    own_p = t // 2

    def attend(o):
        keys = R[:, :, 0].reshape(TOKS * SLOTS, HEAD)
        vals = R[:, :, 1].reshape(TOKS * SLOTS, HEAD)
        query = R[tile(o), :, 2].reshape(SLOTS, HEAD)
        soft = jnp.exp2(dot_t(query, keys) * soft_scale) * MASK[...]
        total = jnp.sum(soft, axis=-1, keepdims=True)
        return (dot_f32(soft.astype(BF16), vals) / total).astype(BF16)

    def send_out(o):
        remote(OS.at[o], OR.at[own_p], o_s.at[o], o_r.at[own_p], tok=tile(o)).start()

    third, second = attend(3), attend(2)
    OS[3] = third
    OS[2] = second
    send_out(3)
    send_out(2)
    first, own = attend(1), attend(0)
    OS[1] = first
    send_out(1)
    OR[own_p] = own

    for i in range(1, PROMPTS):
        p, z_query = job(i)
        remote(OS.at[0], OR.at[p], o_s.at[0], o_r.at[p], tok=z_query).wait_recv()
    for p in range(PROMPTS):
        ATT[pl.ds(p, SLOTS, stride=PROMPTS), :] = OR[p].astype(F32)

    rel_v = {0: 0, 1: 1, 3: 2, 2: 3}

    def out_rows(first, blocks):
        count = len(blocks) * PIECE
        att = ATT[first : first + count, :].astype(BF16)
        for h in range(2):
            for n in range(HALF // 512):
                cols = slice(n * 512, (n + 1) * 512)
                part = dot_f32(att, WAO[h, :, cols]) + ACC[h, first : first + count, cols]
                for i, (k, dv, j) in enumerate(blocks):
                    PS[k, rel_v[dv], j, :, h * HALF + n * 512 : h * HALF + (n + 1) * 512] = part[
                        i * PIECE : (i + 1) * PIECE
                    ].astype(BF16)

    def rs(k, i):
        u, v = uv[k]
        sems = (rs_s.at[k, i], rs_r.at[k, i])
        up, um = {"mlp": at_uv(k, (u + 1) % RING, v)}, {"mlp": at_uv(k, (u + 3) % RING, v)}
        vp, vm = {"mlp": at_uv(k, u, (v + 1) % RING)}, {"mlp": at_uv(k, u, (v + 3) % RING)}
        if i < 16:
            j, d = 3 - (i % 8) // 2, i % 2
            where = vp if d == 0 else vm
            if i < 8:
                block = PS.at[k, 3, j, :, lo if d == 0 else hi]
                return remote(block, RB.at[k, d, j], *sems, **where)
            block = PS.at[k, 1 + d, j]
            return remote(block, RC.at[k, d, j], *sems, **where)
        d = i % 2
        where = up if d == 0 else um
        if i < 18:
            return remote(PS2.at[k, 0, :, lo if d == 0 else hi], RB2.at[k, d], *sems, **where)
        return remote(PS2.at[k, 1 + d], RC2.at[k, d], *sems, **where)

    for half in (1, 0):
        out_rows(starts[5 + half], batches[5 + half])
        for i in range(4 * (1 - half), 4 * (1 - half) + 4):
            for k in range(2):
                rs(k, i).start()
    for step in range(RING):
        j = 3 - step
        out_rows(starts[1 + j], batches[1 + j])
        for d in range(2):
            for k in range(2):
                rs(k, 2 * step + d).wait_recv()
                cols = slice(0, HALF) if d == 0 else slice(HALF, D)
                PS[k, 1 + d, j, :, cols] = (
                    PS[k, 1 + d, j, :, cols].astype(F32) + RB[k, d, j].astype(F32)
                ).astype(BF16)
                rs(k, 8 + 2 * step + d).start()
    out_rows(0, batches[0])

    def own_sum(k, j):
        for d in range(2):
            rs(k, 8 + 2 * (3 - j) + d).wait_recv()
        return PS[k, 0, j].astype(F32) + RC[k, 0, j].astype(F32) + RC[k, 1, j].astype(F32)

    for k in range(2):
        PS2[k, 0] = own_sum(k, 3).astype(BF16)
        rs(k, 16).start()
        rs(k, 17).start()
    for d in range(2):
        for k in range(2):
            total = own_sum(k, 2 - d)
            rs(k, 16 + d).wait_recv()
            cols = slice(0, HALF) if d == 0 else slice(HALF, D)
            PS2[k, 1 + d] = total.astype(BF16)
            PS2[k, 1 + d, :, cols] = (total[:, cols] + RB2[k, d].astype(F32)).astype(BF16)
            rs(k, 18 + d).start()
    fin_copy.wait()
    finals = []
    stream_copy = pltpu.make_async_copy(stream_ref, stream_hbm, out_l)
    for k in range(2):
        branch = own_sum(k, 0)
        for d in range(2):
            rs(k, 18 + d).wait_recv()
        branch = branch + RC2[k, 0].astype(F32) + RC2[k, 1].astype(F32)
        rows = slice(k * PIECE, (k + 1) * PIECE)
        gated = branch.reshape(3, 8, D) * MOD[:, 2 * D : 3 * D][None]
        stream = (HID[rows, :] + gated.reshape(PIECE, D)).astype(BF16)
        stream32 = stream.astype(F32)
        for i in range(PIECE // PROMPTS):
            stream_ref[k * (PIECE // PROMPTS) + i] = stream32[i * PROMPTS : (i + 1) * PROMPTS].astype(BF16)
        shaped = layer_norm(stream32).reshape(3, 8, D)
        shaped = shaped * MOD[:, 4 * D : 5 * D][None] + MOD[:, 3 * D : 4 * D][None]
        finals.append(shaped.reshape(PIECE, D).astype(BF16).astype(F32))
    stream_copy.start()
    final_normed = jnp.concatenate(finals, axis=0).astype(BF16)
    half_velocity = dot_t(final_normed, WFIN[...])
    parts = (half_velocity[:, :CH_HALF] * IMAGE[...], half_velocity[:, CH_HALF:] * IMAGE[...])
    first = c == 0
    VS[...] = jnp.where(first, parts[1], parts[0])
    swap = remote(VS, VR, v_s, v_r, cfg=1 - c)
    swap.start()
    own = jnp.where(first, parts[0], parts[1])
    swap.wait_recv()
    other = VR[...]
    cond = jnp.where(first, own, other)
    uncond = jnp.where(first, other, own)
    for i in range(ROWS_OWN // PROMPTS):
        rows = slice(i * PROMPTS, (i + 1) * PROMPTS)
        cond_ref[i] = cond[rows]
        uncond_ref[i] = uncond[rows]

    stream_copy.wait()
    swap.wait_send()
    for copy in remote_w:
        copy.wait_send()
    span1.wait_send()
    span2.wait_send()
    for k in range(2):
        for i in range(20):
            ag(k, i).wait_send()
            rs(k, i).wait_send()
    for b in range(len(batches)):
        for i in range(1, PROMPTS):
            z_send(b, i).wait_send()
        for o in range(RING):
            (z_both(b, o) if b == 6 and o else z_hand(b, o)).wait_send()
    for o in range(1, RING):
        remote(OS.at[o], OR.at[own_p], o_s.at[o], o_r.at[own_p], tok=tile(o)).wait_send()


def call_kernel(*operands):
    vmem = pl.BlockSpec(memory_space=pltpu.VMEM)
    hbm = pl.BlockSpec(memory_space=pl.ANY)
    dma = pltpu.SemaphoreType.DMA
    scratch = [
        pltpu.VMEM((ROWS_OWN // PROMPTS, PROMPTS, D), BF16),
        pltpu.VMEM((PROMPTS, D), F32),
        pltpu.VMEM((PROMPTS, TOKS * SLOTS), jnp.int32),
        pltpu.VMEM((1, PROMPTS), jnp.int32),
        pltpu.VMEM((2, HEAD), F32),
        pltpu.VMEM((SLOTS, 3), jnp.int32),
        pltpu.VMEM((SLOTS, 2 * HEAD), BF16),
        pltpu.VMEM((ROWS_OWN // PROMPTS, PROMPTS, D), BF16),
        pltpu.VMEM((ROWS_OWN, D), F32),
        pltpu.VMEM((16, TOKS * SLOTS), F32),
        pltpu.VMEM((PROMPTS, 2 * RING, PIECE, HEAD), F32),
        pltpu.VMEM((PROMPTS, 2 * RING, PIECE, HEAD), F32),
        pltpu.VMEM((1, TOKS * SLOTS), F32),
        pltpu.VMEM((ROWS_OWN, CH_HALF), F32),
        pltpu.VMEM((2, HEAD), F32),
        pltpu.VMEM((2, RING, RING, PIECE, D), BF16),
        pltpu.VMEM((PROMPTS * SLOTS, D), BF16),
        pltpu.VMEM((MOD_COLS, D), BF16),
        pltpu.VMEM((D, 3 * HEAD), BF16),
        pltpu.VMEM((D, UNITS), BF16),
        pltpu.VMEM((2, HEAD, HALF), BF16),
        pltpu.VMEM((2, UNITS, HALF), BF16),
        pltpu.VMEM((2 * CH_HALF, D), BF16),
        pltpu.VMEM((TOKS, MLPS, PROMPTS, 128), BF16),
        pltpu.VMEM((8, 5 * D), F32),
        pltpu.VMEM((3, STAGE, HEAD), F32),
        pltpu.VMEM((PROMPTS, 2 * RING, 3, PIECE, HEAD), BF16),
        pltpu.VMEM((TOKS, 2 * RING, 3, PIECE, HEAD), BF16),
        pltpu.VMEM((RING, SLOTS, HEAD), BF16),
        pltpu.VMEM((PROMPTS, SLOTS, HEAD), BF16),
        pltpu.VMEM((PROMPTS * SLOTS, HEAD), F32),
        pltpu.VMEM((PROMPTS * SLOTS, UNITS), BF16),
        pltpu.VMEM((2, PROMPTS * SLOTS, HALF), F32),
        pltpu.VMEM((2, RING, RING, PIECE, D), BF16),
        pltpu.VMEM((2, 2, RING, PIECE, HALF), BF16),
        pltpu.VMEM((2, 2, RING, PIECE, D), BF16),
        pltpu.VMEM((2, 3, PIECE, D), BF16),
        pltpu.VMEM((2, 2, PIECE, HALF), BF16),
        pltpu.VMEM((2, 2, PIECE, D), BF16),
        pltpu.VMEM((ROWS_OWN, CH_HALF), F32),
        pltpu.VMEM((ROWS_OWN, CH_HALF), F32),
        dma((2, 20)), dma((2, 20)), dma((2, 20)), dma((2, 20)),
        dma((8,)), dma((6,)), dma((6,)), dma((2,)), dma((2,)),
        dma((7,)), dma((PROMPTS, 7)), dma((TOKS, 7)), dma((RING, 7)), dma((TOKS, 7)),
        dma((RING,)), dma((PROMPTS,)), dma, dma, dma((7,)), dma,
    ]
    return pl.pallas_call(
        kernel,
        out_shape=(
            jax.ShapeDtypeStruct((ROWS_OWN // PROMPTS, PROMPTS, CH_HALF), F32),
            jax.ShapeDtypeStruct((ROWS_OWN // PROMPTS, PROMPTS, CH_HALF), F32),
            jax.ShapeDtypeStruct((ROWS_OWN // PROMPTS, PROMPTS, D), BF16),
        ),
        in_specs=[hbm] * 13,
        out_specs=(vmem, vmem, hbm),
        scratch_shapes=scratch,
        compiler_params=pltpu.CompilerParams(
            collective_id=0, has_side_effects=True, vmem_limit_bytes=60000000
        ),
    )(*operands)


def slot_places():
    blocks = [(k, 0, j) for k in range(2) for j in range(RING)]
    blocks += [(k, dv, j) for j in range(RING) for k in range(2) for dv in (1, 3)]
    blocks += [(k, 2, j) for half in range(2) for k in range(2) for j in (2 * half, 2 * half + 1)]
    rows = []
    for k, dv, j in blocks:
        du = (0, 3, 1, 2)[j]
        dx, dy = (du, dv) if k == 0 else (dv, du)
        rows += [(dx, dy, 6 * k + i) for i in range(6)]
    return np.array(rows, np.int32)


def rope_table():
    pairs = HEAD // 2
    first_pairs = HEAD // 16
    axis_pairs = (HEAD - HEAD // 8) // 4
    index = np.arange(pairs, dtype=np.float32)
    in_rows = (index >= first_pairs) & (index < first_pairs + axis_pairs)
    in_cols = index >= first_pairs + axis_pairs
    log_base = np.float32(math.log(ROPE_BASE))
    table = np.zeros((2 * SIDE, 2 * HEAD), np.float32)
    for pos in range(SIDE):
        for base, inside, start in ((0, in_rows, first_pairs), (SIDE, in_cols, first_pairs + axis_pairs)):
            freq = np.exp(-log_base * (index - np.float32(start)) / np.float32(axis_pairs)).astype(np.float32)
            angle = np.where(inside, np.float32(pos) * freq, 0.0).astype(np.float32)
            still = ~(in_rows | in_cols) if base == 0 else np.zeros_like(inside)
            cosine = np.where(inside, np.cos(angle), np.where(still, 1.0, 0.0))
            sine = np.where(inside, np.sin(angle), 0.0)
            table[base + pos] = np.concatenate([cosine, cosine, -sine, sine])
    parts, left = [], table
    for _ in range(3):
        part = left.astype(jnp.bfloat16)
        parts.append(part)
        left = left - part.astype(np.float32)
    return np.concatenate(parts, axis=0)


def on_device(
    hidden, latents, vec, slot_token, text_len, step_index, guidance,
    w_mod, w_qkv, w_mlp_in, qk_gain, w_attn_out, w_mlp_out, w_final,
):
    cond, uncond, stream = call_kernel(
        hidden[0], vec[0], slot_token, text_len, qk_gain[0], jnp.asarray(slot_places()), jnp.asarray(rope_table()),
        w_mod.T, w_qkv[0].transpose(1, 0, 2), w_mlp_in[0], w_attn_out[0], w_mlp_out[0], w_final.T,
    )
    velocity = uncond + guidance[0] * (cond - uncond)
    current = step_index[0].astype(F32)
    step_size = sigma_at(current + 1.0, STEPS) - sigma_at(current, STEPS)
    return velocity, latents + step_size * velocity, stream[None]


def solution(mesh):
    return jax.shard_map(
        on_device,
        mesh=mesh,
        in_specs=(
            P("cfg", ("tok", "mlp"), None, None),
            P(("tok", "mlp"), None, "cfg"),
            P("cfg", None, None),
            P(),
            P("cfg", None),
            P(),
            P(),
            P(None, ("tok", "mlp")),
            P(None, "cfg", None, "mlp"),
            P(None, "cfg", "mlp"),
            P(),
            P(None, "mlp", "cfg"),
            P(None, "mlp", "cfg"),
            P(),
        ),
        out_specs=(
            P(("tok", "mlp"), None, "cfg"),
            P(("tok", "mlp"), None, "cfg"),
            P("cfg", ("tok", "mlp"), None, None),
        ),
        check_vma=False,
    )
```

```python
import math

import jax
import jax.numpy as jnp
import numpy as np
from jax import lax
from jax.experimental import pallas as pl
from jax.experimental.pallas import tpu as pltpu
from jax.sharding import PartitionSpec as P

SIDE = 32
TXT = 512
STEPS = 28
EPSILON = 1e-06
ROPE_BASE = 10000.0
TIME_SHIFT = 3.0

MESH = pl.DeviceIdType.MESH
F32 = jnp.float32
BF16 = jnp.bfloat16

D = 3072
HALF = D // 2
HEAD = 128
UNITS = 768
PROMPTS = 4
RING = 4
TOKS = 8
MLPS = 16
PIECE = 24
CHUNK = RING * PIECE
STAGE = 2 * CHUNK
SLOTS = 192
ROWS_OWN = 2 * PIECE
MOD_COLS = 120
CH_HALF = 32


def sigma_at(position, steps_total):
    remain = 1.0 - position / steps_total
    return TIME_SHIFT * remain / (1.0 + (TIME_SHIFT - 1.0) * remain)


def layer_norm(values):
    average = jnp.mean(values, axis=-1, keepdims=True)
    centred = values - average
    spread = jnp.mean(centred * centred, axis=-1, keepdims=True)
    return centred * lax.rsqrt(spread + EPSILON)


def dot_f32(a, b):
    return jnp.dot(a, b, preferred_element_type=F32)


def dot_t(a, b):
    return lax.dot_general(a, b, (((1,), (1,)), ((), ())), preferred_element_type=F32)


def kernel(
    hid_hbm, vec_hbm, token_hbm, len_hbm, gain_hbm, place_hbm, tab_hbm,
    wmod_hbm, wqkv_hbm, wmi_hbm, wao_hbm, wmo_hbm, wfin_hbm,
    cond_ref, uncond_ref, stream_hbm,
    hid_ref, vec_ref, token_ref, len_ref, gain_ref, place_ref, tab_ref, stream_ref, HID, TT, COS, SIN, MASK, IMAGE, GAIN, X, N, WMOD, WQKV, WMI, WAO, WMO, WFIN, G, MOD, QF, ST, R, OS, OR, ATT,
    ACT, ACC, PS, RB, RC, PS2, RB2, RC2, VS, VR,
    ag_s, ag_r, rs_s, rs_r, w_l, w_s, w_r, m_s, m_r, z_l, z_s, z_r, f_s, f_r, o_s, o_r, v_s, v_r, in_l, out_l,
):
    c = lax.axis_index("cfg")
    t = lax.axis_index("tok")
    m = lax.axis_index("mlp")
    x, y = m // RING, m % RING
    uv = ((x, y), (y, x))

    def at_uv(k, u, v):
        return u * RING + v if k == 0 else v * RING + u

    def remote(src, dst, ssem, rsem, **where):
        return pltpu.make_async_remote_copy(
            src_ref=src, dst_ref=dst, send_sem=ssem, recv_sem=rsem,
            device_id=where, device_id_type=MESH,
        )

    barrier = pltpu.get_barrier_semaphore()
    for d in range(1, MLPS):
        pl.semaphore_signal(barrier, inc=1, device_id={"mlp": (m + d) % MLPS}, device_id_type=MESH)
    for d in range(1, TOKS):
        pl.semaphore_signal(barrier, inc=1, device_id={"tok": (t + d) % TOKS}, device_id_type=MESH)
    pl.semaphore_signal(barrier, inc=1, device_id={"cfg": 1 - c}, device_id_type=MESH)

    inputs = [
        pltpu.make_async_copy(src, dst, in_l.at[i])
        for i, (src, dst) in enumerate((
            (hid_hbm, hid_ref), (vec_hbm, vec_ref), (token_hbm, token_ref), (len_hbm, len_ref),
            (gain_hbm, gain_ref), (place_hbm, place_ref), (tab_hbm, tab_ref),
        ))
    ]
    for copy in inputs:
        copy.start()

    wmod_copy = pltpu.make_async_copy(wmod_hbm, WMOD, w_l.at[0])
    wmod_copy.start()
    k_rows = pl.ds(pl.multiple_of(c * HALF, HALF), HALF)
    weights = (
        [(wqkv_hbm.at[j], WQKV.at[k_rows, pl.ds(j * HEAD, HEAD)]) for j in range(3)]
        + [(wmi_hbm, WMI.at[k_rows]), (wao_hbm, WAO.at[c]), (wmo_hbm, WMO.at[c])]
    )
    local_w = [pltpu.make_async_copy(s, d, w_l.at[1 + i]) for i, (s, d) in enumerate(weights)]
    remote_w = [remote(s, d, w_s.at[i], w_r.at[i], cfg=1 - c) for i, (s, d) in enumerate(weights)]
    fin_copy = pltpu.make_async_copy(wfin_hbm, WFIN, w_l.at[7])

    inputs[0].wait()
    for i in range(ROWS_OWN // PROMPTS):
        HID[i * PROMPTS : (i + 1) * PROMPTS, :] = hid_ref[i].astype(F32)
    normed = layer_norm(HID[...]).astype(BF16)
    X[0, y, x] = normed[:PIECE]
    X[1, x, y] = normed[PIECE:]

    inputs[1].wait()
    vec = vec_ref[...]
    silu_vec = (vec * (1.0 / (1.0 + jnp.exp(-vec)))).astype(BF16)
    wmod_copy.wait()
    G[t, m, :, 0:MOD_COLS] = dot_t(silu_vec, WMOD[...]).astype(BF16)
    pl.semaphore_wait(barrier, MLPS - 1 + TOKS - 1 + 1)
    mod1 = [
        remote(G.at[t, m], G.at[t, m], m_s.at[0], m_r.at[0], mlp=(m + d) % MLPS) for d in range(1, MLPS)
    ]
    for copy in mod1:
        copy.start()

    lo, hi = pl.ds(0, HALF), pl.ds(HALF, HALF)

    def order_u(u, j):
        return (u, (u + 3) % RING, (u + 1) % RING, (u + 2) % RING)[j]

    def ag(k, i):
        u, v = uv[k]
        sems = (ag_s.at[k, i], ag_r.at[k, i])
        up, um = {"mlp": at_uv(k, (u + 1) % RING, v)}, {"mlp": at_uv(k, (u + 3) % RING, v)}
        vp, vm = {"mlp": at_uv(k, u, (v + 1) % RING)}, {"mlp": at_uv(k, u, (v + 3) % RING)}
        if i < 2:
            block = X.at[k, v, u]
            return remote(block, block, *sems, **(up if i == 0 else um))
        if i < 4:
            block = X.at[k, v, (u + (3 if i == 2 else 1)) % RING, :, lo if i == 2 else hi]
            return remote(block, block, *sems, **(up if i == 2 else um))
        if i < 12:
            j, d = (i - 4) // 2, (i - 4) % 2
            block = X.at[k, v, order_u(u, j)]
            return remote(block, block, *sems, **(vp if d == 0 else vm))
        j, d = (i - 12) // 2, (i - 12) % 2
        block = X.at[k, (v + (3 if d == 0 else 1)) % RING, order_u(u, j), :, lo if d == 0 else hi]
        return remote(block, block, *sems, **(vp if d == 0 else vm))

    def ag_start(ids):
        for i in ids:
            for k in range(2):
                ag(k, i).start()

    def ag_recv(ids):
        for i in ids:
            for k in range(2):
                ag(k, i).wait_recv()

    ag_start((0, 1, 4, 5))

    for copy in local_w[:3]:
        copy.start()
    for copy in remote_w[:3]:
        copy.start()
    for i in range(3, 6):
        local_w[i].start()
        remote_w[i].start()
    fin_copy.start()

    for copy in inputs[2:]:
        copy.wait()
    tokens = token_ref[...]
    is_image = tokens >= TXT
    place = jnp.where(is_image, tokens - TXT, 0)
    TT[0:4, :] = (place // SIDE).astype(F32)
    TT[4:8, :] = (place % SIDE).astype(F32)
    TT[8:12, :] = jnp.where(is_image, 1.0, 0.0)
    TT[12:16, :] = jnp.zeros((4, TOKS * SLOTS), F32)
    kinds = TT[...].astype(BF16)

    def lanes(shape):
        return lax.broadcasted_iota(jnp.int32, shape, 1)

    place_x = (place_ref[:, 0:1] + x) % RING
    place_y = (place_ref[:, 1:2] + y) % RING
    natural = (RING * place_x + place_y) * (ROWS_OWN // PROMPTS) + place_ref[:, 2:3]
    chosen = jnp.where(lanes((SLOTS, TOKS * SLOTS)) == natural + t * SLOTS, 1.0, 0.0).astype(BF16)
    picked = dot_t(chosen, kinds)
    lane192 = lanes((SLOTS, SLOTS))
    for p in range(PROMPTS):
        wanted_pos = jnp.where(lane192 % 64 < 32, picked[:, p : p + 1], picked[:, 4 + p : 5 + p])
        hot = jnp.where((lane192 % 32).astype(F32) == wanted_pos, 1.0, 0.0).astype(BF16)
        both = dot_f32(hot, tab_ref[...])
        COS[p] = both[:, :HEAD].reshape(2 * RING, PIECE, HEAD)
        SIN[p] = both[:, HEAD:].reshape(2 * RING, PIECE, HEAD)
    sub = lax.broadcasted_iota(jnp.int32, (ROWS_OWN, TOKS * SLOTS), 0)
    chosen = jnp.where(
        lanes((ROWS_OWN, TOKS * SLOTS)) == sub // PROMPTS + (t * MLPS + m) * (ROWS_OWN // PROMPTS), 1.0, 0.0
    ).astype(BF16)
    sub16 = lax.broadcasted_iota(jnp.int32, (ROWS_OWN, 16), 0)
    own_image = jnp.where(lanes((ROWS_OWN, 16)) == 8 + sub16 % PROMPTS, dot_t(chosen, kinds), 0.0)
    IMAGE[...] = jnp.broadcast_to(jnp.sum(own_image, axis=-1, keepdims=True), (ROWS_OWN, CH_HALF))
    this = lax.broadcasted_iota(jnp.int32, (PROMPTS, TOKS * SLOTS), 0) == t // 2
    job_tokens = jnp.sum(jnp.where(this, tokens.astype(F32), 0.0), axis=0, keepdims=True)
    job_len = jnp.sum(
        jnp.where(lanes((1, PROMPTS)) == t // 2, len_ref[...].astype(F32), 0.0), axis=-1, keepdims=True
    )
    valid = jnp.where((job_tokens >= TXT) | (job_tokens < job_len), 1.0, 0.0)
    valid = jnp.concatenate([valid[:, i * SLOTS : (i + 1) * SLOTS] for i in range(TOKS)], axis=0)
    valid = dot_t(valid.astype(BF16), jnp.where(lane192 == natural, 1.0, 0.0).astype(BF16))
    MASK[...] = jnp.concatenate([valid[i : i + 1, :] for i in range(TOKS)], axis=1)

    ag_recv((0, 1))
    ag_start((2, 3, 6, 7, 8, 9))

    span1 = remote(G.at[t, pl.ds(0, MLPS - 1)], G.at[t, pl.ds(0, MLPS - 1)], m_s.at[0], m_r.at[0], mlp=(m + 1) % MLPS)
    span1.wait_recv()
    mod2 = [remote(G.at[t], G.at[t], m_s.at[1], m_r.at[1], tok=(t + d) % TOKS) for d in range(1, TOKS)]
    for copy in mod2:
        copy.start()

    ag_recv((2, 3))
    ag_start((10, 11))

    for copy in local_w[:3]:
        copy.wait()
    for copy in remote_w[:3]:
        copy.wait_recv()
    src_col = lax.broadcasted_iota(jnp.int32, (HEAD, HEAD), 0)
    out_col = lax.broadcasted_iota(jnp.int32, (HEAD, HEAD), 1)
    wanted = jnp.where(out_col < HEAD // 2, 2 * out_col, 2 * out_col - HEAD + 1)
    permute = jnp.where(src_col == wanted, 1.0, 0.0).astype(BF16)

    gain = gain_ref[...]
    gain_sum = jnp.zeros((2, HEAD), F32)
    for _ in range(3):
        part = gain.astype(BF16)
        gain_sum = gain_sum + dot_f32(part, permute)
        gain = gain - part.astype(F32)
    GAIN[...] = gain_sum

    def permute_step(i, carry):
        rows = pl.ds(pl.multiple_of(i * 512, 512), 512)
        for j in range(2):
            cols = pl.ds(j * HEAD, HEAD)
            WQKV[rows, cols] = dot_f32(WQKV[rows, cols], permute).astype(BF16)
        return carry

    lax.fori_loop(0, D // 512, permute_step, 0)

    span2 = remote(
        G.at[pl.ds(0, TOKS - 1)], G.at[pl.ds(0, TOKS - 1)], m_s.at[1], m_r.at[1], tok=(t + 1) % TOKS
    )
    span2.wait_recv()
    lane = lax.broadcasted_iota(jnp.int32, (PROMPTS, 128), 1)

    def mod_step(i, carry):
        base = pl.multiple_of(i * (MLPS * MOD_COLS), 128)
        for j in range(15):
            shift = (8 * j) % MOD_COLS
            first = G[i, j].astype(F32)
            if shift:
                first = pltpu.roll(first, 128 - shift, 1)
            second = pltpu.roll(G[i, j + 1].astype(F32), MOD_COLS - shift, 1)
            index = i * 15 + j
            is_scale = jnp.where(((index >= 24) & (index < 48)) | (index >= 96), 1.0, 0.0)
            both = jnp.where(lane < MOD_COLS - shift, first, second) + is_scale
            MOD[:, pl.ds(base + j * 128, 128)] = jnp.concatenate([both, both], axis=0)
        return carry

    lax.fori_loop(0, TOKS, mod_step, 0)

    for i in range(3, 4):
        local_w[i].wait()
        remote_w[i].wait_recv()

    batches = [[(k, 0, j) for k in range(2) for j in range(RING)]]
    batches += [[(k, dv, j) for k in range(2) for dv in (1, 3)] for j in range(RING)]
    batches += [[(k, 2, j) for k in range(2) for j in (2 * half, 2 * half + 1)] for half in range(2)]
    starts = (0, 192, 288, 384, 480, 576, 672)
    width = 768

    def modulate(b):
        blocks = batches[b]

        def step(i, carry):
            cols = pl.ds(pl.multiple_of(i * width, width), width)
            scale = MOD[:, pl.ds(pl.multiple_of(D + i * width, width), width)]
            shift = MOD[:, cols]
            for pair in range(0, len(blocks), 2):
                pieces = [
                    X[k, (uv[k][1] + dv) % RING, order_u(uv[k][0], j), :, cols].astype(F32).reshape(3, 8, width)
                    for k, dv, j in blocks[pair : pair + 2]
                ]
                both = jnp.concatenate(pieces, axis=0) * scale[None] + shift[None]
                first = starts[b] + pair * PIECE
                N[first : first + 48, cols] = both.reshape(48, width).astype(BF16)
            return carry

        lax.fori_loop(0, D // width, step, 0)

    soft_scale = math.log2(math.e) / math.sqrt(HEAD)

    def groups_of(b):
        return len(batches[b]) // RING, starts[b] // CHUNK

    def qkv(b):
        count, g0 = groups_of(b)
        rows_b = count * CHUNK
        pre = dot_f32(N[starts[b] : starts[b] + rows_b, :], WQKV[...])
        for j in range(3):
            QF[j, 0:rows_b] = pre[:, j * HEAD : (j + 1) * HEAD]
        for p in range(PROMPTS):
            rows = pl.ds(p, count * PIECE, stride=PROMPTS)
            cosine = COS[p, g0 : g0 + count].reshape(count * PIECE, HEAD)
            sine = SIN[p, g0 : g0 + count].reshape(count * PIECE, HEAD)
            outs = []
            for j in range(2):
                val = QF.at[j][rows, :]
                val = val * lax.rsqrt(jnp.mean(val * val, axis=-1, keepdims=True) + EPSILON) * GAIN[j : j + 1, :]
                outs.append((val * cosine + pltpu.roll(val, HEAD // 2, 1) * sine).astype(BF16))
            outs.append(QF.at[2][rows, :].astype(BF16))
            for place, val in ((0, outs[1]), (1, outs[2]), (2, outs[0])):
                for g in range(count):
                    ST[p, g0 + g, place] = val[g * PIECE : (g + 1) * PIECE]

    def job(i):
        p = (t // 2 + i) % PROMPTS
        rel = (t - 2 * p + TOKS) % TOKS
        half = 1 - ((rel + 7) % TOKS) // RING
        return p, 2 * p + half

    sign = 1 - 2 * (t % 2)
    partner = t + sign
    kv = pl.ds(0, 2)

    def tile(o):
        return (t + TOKS - sign * o) % TOKS

    def z_local(b):
        count, g0 = groups_of(b)
        gs = pl.ds(g0, count)
        return pltpu.make_async_copy(ST.at[t // 2, gs], R.at[t, gs], z_l.at[b])

    def z_send(b, i):
        count, g0 = groups_of(b)
        gs = pl.ds(g0, count)
        p, z_query = job(i)
        return remote(ST.at[p, gs], R.at[t, gs], z_s.at[i, b], z_r.at[t, b], tok=z_query)

    def z_near(b, o):
        count, g0 = groups_of(b)
        block = R.at[tile(o), pl.ds(g0, count)]
        return remote(block, block, z_s.at[0, b], z_r.at[tile(o), b], tok=partner)

    def z_hand(b, o):
        count, g0 = groups_of(b)
        gs = pl.ds(g0, count)
        src = ST.at[t // 2, gs, kv] if o == 0 else R.at[tile(o), gs, kv]
        return remote(src, R.at[tile(o), gs, kv], f_s.at[o, b], f_r.at[tile(o), b], tok=partner)

    def z_far(b, o):
        count, g0 = groups_of(b)
        block = R.at[tile(o), pl.ds(g0, count), kv]
        return remote(block, block, f_s.at[0, b], f_r.at[tile(o), b], tok=partner)

    def send_batch(b):
        for i in (2, 1, 3):
            z_send(b, i).start()
        z_local(b).start()
        z_hand(b, 0).start()

    def z_both(b, i):
        count, g0 = groups_of(b)
        gs = pl.ds(g0, count)
        p, z_query = job(i)
        other = 4 * p + 1 - z_query
        return remote(ST.at[p, gs, kv], R.at[t, gs, kv], f_s.at[i, b], f_r.at[t, b], tok=other)

    def hand_on(b):
        for o in range(1, RING):
            z_near(b, o).wait_recv()
            z_hand(b, o).start()

    def units(first, count):
        ACT[first : first + count, :] = jax.nn.gelu(
            dot_f32(N[first : first + count, :], WMI[...]), approximate=True
        ).astype(BF16)

    def units_out(first, count):
        def step(i, carry):
            cols = pl.ds(pl.multiple_of(i * 512, 512), 512)
            for h in range(2):
                ACC[h, first : first + count, cols] = dot_f32(ACT[first : first + count, :], WMO[h, :, cols])
            return carry

        lax.fori_loop(0, HALF // 512, step, 0)

    def take(b):
        modulate(b)
        qkv(b)
        send_batch(b)

    take(0)
    ag_recv((4, 5))
    ag_start((12, 13))
    ag_recv((6, 7))
    ag_start((14, 15))
    take(1)
    take(2)
    units(0, 192)
    ag_recv((8, 9))
    ag_start((16, 17))
    take(3)
    for b in range(3):
        hand_on(b)
    for i in range(4, 6):
        local_w[i].wait()
        remote_w[i].wait_recv()
    units_out(0, 192)
    ag_recv((10, 11))
    ag_start((18, 19))
    take(4)
    hand_on(3)
    units(192, 192)
    ag_recv(range(12, 16))
    take(5)
    hand_on(4)
    ag_recv(range(16, 20))
    take(6)
    for i in (2, 1, 3):
        z_both(6, i).start()
    hand_on(5)
    units(384, 192)
    units(576, 192)
    units_out(192, 384)
    units_out(576, 192)
    for o in range(1, RING):
        z_near(6, o).wait_recv()

    for b in range(len(batches)):
        z_local(b).wait()
        for o in range(RING, TOKS):
            z_far(b, o).wait_recv()
    own_p = t // 2

    def attend(o):
        keys = R[:, :, 0].reshape(TOKS * SLOTS, HEAD)
        vals = R[:, :, 1].reshape(TOKS * SLOTS, HEAD)
        query = R[tile(o), :, 2].reshape(SLOTS, HEAD)
        soft = jnp.exp2(dot_t(query, keys) * soft_scale) * MASK[...]
        total = jnp.sum(soft, axis=-1, keepdims=True)
        return (dot_f32(soft.astype(BF16), vals) / total).astype(BF16)

    def send_out(o):
        remote(OS.at[o], OR.at[own_p], o_s.at[o], o_r.at[own_p], tok=tile(o)).start()

    third, second = attend(3), attend(2)
    OS[3] = third
    OS[2] = second
    send_out(3)
    send_out(2)
    first, own = attend(1), attend(0)
    OS[1] = first
    send_out(1)
    OR[own_p] = own

    for i in range(1, PROMPTS):
        p, z_query = job(i)
        remote(OS.at[0], OR.at[p], o_s.at[0], o_r.at[p], tok=z_query).wait_recv()
    for p in range(PROMPTS):
        ATT[pl.ds(p, SLOTS, stride=PROMPTS), :] = OR[p].astype(F32)

    rel_v = {0: 0, 1: 1, 3: 2, 2: 3}

    def out_rows(first, blocks):
        count = len(blocks) * PIECE
        att = ATT[first : first + count, :].astype(BF16)
        for h in range(2):
            for n in range(HALF // 512):
                cols = slice(n * 512, (n + 1) * 512)
                part = dot_f32(att, WAO[h, :, cols]) + ACC[h, first : first + count, cols]
                for i, (k, dv, j) in enumerate(blocks):
                    PS[k, rel_v[dv], j, :, h * HALF + n * 512 : h * HALF + (n + 1) * 512] = part[
                        i * PIECE : (i + 1) * PIECE
                    ].astype(BF16)

    def rs(k, i):
        u, v = uv[k]
        sems = (rs_s.at[k, i], rs_r.at[k, i])
        up, um = {"mlp": at_uv(k, (u + 1) % RING, v)}, {"mlp": at_uv(k, (u + 3) % RING, v)}
        vp, vm = {"mlp": at_uv(k, u, (v + 1) % RING)}, {"mlp": at_uv(k, u, (v + 3) % RING)}
        if i < 16:
            j, d = 3 - (i % 8) // 2, i % 2
            where = vp if d == 0 else vm
            if i < 8:
                block = PS.at[k, 3, j, :, lo if d == 0 else hi]
                return remote(block, RB.at[k, d, j], *sems, **where)
            block = PS.at[k, 1 + d, j]
            return remote(block, RC.at[k, d, j], *sems, **where)
        d = i % 2
        where = up if d == 0 else um
        if i < 18:
            return remote(PS2.at[k, 0, :, lo if d == 0 else hi], RB2.at[k, d], *sems, **where)
        return remote(PS2.at[k, 1 + d], RC2.at[k, d], *sems, **where)

    for half in (1, 0):
        out_rows(starts[5 + half], batches[5 + half])
        for i in range(4 * (1 - half), 4 * (1 - half) + 4):
            for k in range(2):
                rs(k, i).start()
    for step in range(RING):
        j = 3 - step
        out_rows(starts[1 + j], batches[1 + j])
        for d in range(2):
            for k in range(2):
                rs(k, 2 * step + d).wait_recv()
                cols = slice(0, HALF) if d == 0 else slice(HALF, D)
                PS[k, 1 + d, j, :, cols] = (
                    PS[k, 1 + d, j, :, cols].astype(F32) + RB[k, d, j].astype(F32)
                ).astype(BF16)
                rs(k, 8 + 2 * step + d).start()
    out_rows(0, batches[0])

    def own_sum(k, j):
        for d in range(2):
            rs(k, 8 + 2 * (3 - j) + d).wait_recv()
        return PS[k, 0, j].astype(F32) + RC[k, 0, j].astype(F32) + RC[k, 1, j].astype(F32)

    for k in range(2):
        PS2[k, 0] = own_sum(k, 3).astype(BF16)
        rs(k, 16).start()
        rs(k, 17).start()
    for d in range(2):
        for k in range(2):
            total = own_sum(k, 2 - d)
            rs(k, 16 + d).wait_recv()
            cols = slice(0, HALF) if d == 0 else slice(HALF, D)
            PS2[k, 1 + d] = total.astype(BF16)
            PS2[k, 1 + d, :, cols] = (total[:, cols] + RB2[k, d].astype(F32)).astype(BF16)
            rs(k, 18 + d).start()
    fin_copy.wait()
    finals = []
    stream_copy = pltpu.make_async_copy(stream_ref, stream_hbm, out_l)
    for k in range(2):
        branch = own_sum(k, 0)
        for d in range(2):
            rs(k, 18 + d).wait_recv()
        branch = branch + RC2[k, 0].astype(F32) + RC2[k, 1].astype(F32)
        rows = slice(k * PIECE, (k + 1) * PIECE)
        gated = branch.reshape(3, 8, D) * MOD[:, 2 * D : 3 * D][None]
        stream = (HID[rows, :] + gated.reshape(PIECE, D)).astype(BF16)
        stream32 = stream.astype(F32)
        for i in range(PIECE // PROMPTS):
            stream_ref[k * (PIECE // PROMPTS) + i] = stream32[i * PROMPTS : (i + 1) * PROMPTS].astype(BF16)
        shaped = layer_norm(stream32).reshape(3, 8, D)
        shaped = shaped * MOD[:, 4 * D : 5 * D][None] + MOD[:, 3 * D : 4 * D][None]
        finals.append(shaped.reshape(PIECE, D).astype(BF16).astype(F32))
    stream_copy.start()
    final_normed = jnp.concatenate(finals, axis=0).astype(BF16)
    half_velocity = dot_t(final_normed, WFIN[...])
    parts = (half_velocity[:, :CH_HALF] * IMAGE[...], half_velocity[:, CH_HALF:] * IMAGE[...])
    first = c == 0
    VS[...] = jnp.where(first, parts[1], parts[0])
    swap = remote(VS, VR, v_s, v_r, cfg=1 - c)
    swap.start()
    own = jnp.where(first, parts[0], parts[1])
    swap.wait_recv()
    other = VR[...]
    cond = jnp.where(first, own, other)
    uncond = jnp.where(first, other, own)
    for i in range(ROWS_OWN // PROMPTS):
        rows = slice(i * PROMPTS, (i + 1) * PROMPTS)
        cond_ref[i] = cond[rows]
        uncond_ref[i] = uncond[rows]

    stream_copy.wait()
    swap.wait_send()
    for copy in remote_w:
        copy.wait_send()
    span1.wait_send()
    span2.wait_send()
    for k in range(2):
        for i in range(20):
            ag(k, i).wait_send()
            rs(k, i).wait_send()
    for b in range(len(batches)):
        for i in range(1, PROMPTS):
            z_send(b, i).wait_send()
        for o in range(RING):
            (z_both(b, o) if b == 6 and o else z_hand(b, o)).wait_send()
    for o in range(1, RING):
        remote(OS.at[o], OR.at[own_p], o_s.at[o], o_r.at[own_p], tok=tile(o)).wait_send()


def call_kernel(*operands):
    vmem = pl.BlockSpec(memory_space=pltpu.VMEM)
    hbm = pl.BlockSpec(memory_space=pl.ANY)
    dma = pltpu.SemaphoreType.DMA
    scratch = [
        pltpu.VMEM((ROWS_OWN // PROMPTS, PROMPTS, D), BF16),
        pltpu.VMEM((PROMPTS, D), F32),
        pltpu.VMEM((PROMPTS, TOKS * SLOTS), jnp.int32),
        pltpu.VMEM((1, PROMPTS), jnp.int32),
        pltpu.VMEM((2, HEAD), F32),
        pltpu.VMEM((SLOTS, 3), jnp.int32),
        pltpu.VMEM((SLOTS, 2 * HEAD), BF16),
        pltpu.VMEM((ROWS_OWN // PROMPTS, PROMPTS, D), BF16),
        pltpu.VMEM((ROWS_OWN, D), F32),
        pltpu.VMEM((16, TOKS * SLOTS), F32),
        pltpu.VMEM((PROMPTS, 2 * RING, PIECE, HEAD), F32),
        pltpu.VMEM((PROMPTS, 2 * RING, PIECE, HEAD), F32),
        pltpu.VMEM((1, TOKS * SLOTS), F32),
        pltpu.VMEM((ROWS_OWN, CH_HALF), F32),
        pltpu.VMEM((2, HEAD), F32),
        pltpu.VMEM((2, RING, RING, PIECE, D), BF16),
        pltpu.VMEM((PROMPTS * SLOTS, D), BF16),
        pltpu.VMEM((MOD_COLS, D), BF16),
        pltpu.VMEM((D, 3 * HEAD), BF16),
        pltpu.VMEM((D, UNITS), BF16),
        pltpu.VMEM((2, HEAD, HALF), BF16),
        pltpu.VMEM((2, UNITS, HALF), BF16),
        pltpu.VMEM((2 * CH_HALF, D), BF16),
        pltpu.VMEM((TOKS, MLPS, PROMPTS, 128), BF16),
        pltpu.VMEM((8, 5 * D), F32),
        pltpu.VMEM((3, STAGE, HEAD), F32),
        pltpu.VMEM((PROMPTS, 2 * RING, 3, PIECE, HEAD), BF16),
        pltpu.VMEM((TOKS, 2 * RING, 3, PIECE, HEAD), BF16),
        pltpu.VMEM((RING, SLOTS, HEAD), BF16),
        pltpu.VMEM((PROMPTS, SLOTS, HEAD), BF16),
        pltpu.VMEM((PROMPTS * SLOTS, HEAD), F32),
        pltpu.VMEM((PROMPTS * SLOTS, UNITS), BF16),
        pltpu.VMEM((2, PROMPTS * SLOTS, HALF), F32),
        pltpu.VMEM((2, RING, RING, PIECE, D), BF16),
        pltpu.VMEM((2, 2, RING, PIECE, HALF), BF16),
        pltpu.VMEM((2, 2, RING, PIECE, D), BF16),
        pltpu.VMEM((2, 3, PIECE, D), BF16),
        pltpu.VMEM((2, 2, PIECE, HALF), BF16),
        pltpu.VMEM((2, 2, PIECE, D), BF16),
        pltpu.VMEM((ROWS_OWN, CH_HALF), F32),
        pltpu.VMEM((ROWS_OWN, CH_HALF), F32),
        dma((2, 20)), dma((2, 20)), dma((2, 20)), dma((2, 20)),
        dma((8,)), dma((6,)), dma((6,)), dma((2,)), dma((2,)),
        dma((7,)), dma((PROMPTS, 7)), dma((TOKS, 7)), dma((RING, 7)), dma((TOKS, 7)),
        dma((RING,)), dma((PROMPTS,)), dma, dma, dma((7,)), dma,
    ]
    return pl.pallas_call(
        kernel,
        out_shape=(
            jax.ShapeDtypeStruct((ROWS_OWN // PROMPTS, PROMPTS, CH_HALF), F32),
            jax.ShapeDtypeStruct((ROWS_OWN // PROMPTS, PROMPTS, CH_HALF), F32),
            jax.ShapeDtypeStruct((ROWS_OWN // PROMPTS, PROMPTS, D), BF16),
        ),
        in_specs=[hbm] * 13,
        out_specs=(vmem, vmem, hbm),
        scratch_shapes=scratch,
        compiler_params=pltpu.CompilerParams(
            collective_id=0, has_side_effects=True, vmem_limit_bytes=60000000
        ),
    )(*operands)


def slot_places():
    blocks = [(k, 0, j) for k in range(2) for j in range(RING)]
    blocks += [(k, dv, j) for j in range(RING) for k in range(2) for dv in (1, 3)]
    blocks += [(k, 2, j) for half in range(2) for k in range(2) for j in (2 * half, 2 * half + 1)]
    rows = []
    for k, dv, j in blocks:
        du = (0, 3, 1, 2)[j]
        dx, dy = (du, dv) if k == 0 else (dv, du)
        rows += [(dx, dy, 6 * k + i) for i in range(6)]
    return np.array(rows, np.int32)


def rope_table():
    pairs = HEAD // 2
    first_pairs = HEAD // 16
    axis_pairs = (HEAD - HEAD // 8) // 4
    index = np.arange(pairs, dtype=np.float32)
    in_rows = (index >= first_pairs) & (index < first_pairs + axis_pairs)
    in_cols = index >= first_pairs + axis_pairs
    log_base = np.float32(math.log(ROPE_BASE))
    table = np.zeros((2 * SIDE, 2 * HEAD), np.float32)
    for pos in range(SIDE):
        for base, inside, start in ((0, in_rows, first_pairs), (SIDE, in_cols, first_pairs + axis_pairs)):
            freq = np.exp(-log_base * (index - np.float32(start)) / np.float32(axis_pairs)).astype(np.float32)
            angle = np.where(inside, np.float32(pos) * freq, 0.0).astype(np.float32)
            still = ~(in_rows | in_cols) if base == 0 else np.zeros_like(inside)
            cosine = np.where(inside, np.cos(angle), np.where(still, 1.0, 0.0))
            sine = np.where(inside, np.sin(angle), 0.0)
            table[base + pos] = np.concatenate([cosine, cosine, -sine, sine])
    parts, left = [], table
    for _ in range(3):
        part = left.astype(jnp.bfloat16)
        parts.append(part)
        left = left - part.astype(np.float32)
    return np.concatenate(parts, axis=0)


def on_device(
    hidden, latents, vec, slot_token, text_len, step_index, guidance,
    w_mod, w_qkv, w_mlp_in, qk_gain, w_attn_out, w_mlp_out, w_final,
):
    cond, uncond, stream = call_kernel(
        hidden[0], vec[0], slot_token, text_len, qk_gain[0], jnp.asarray(slot_places()), jnp.asarray(rope_table()),
        w_mod.T, w_qkv[0].transpose(1, 0, 2), w_mlp_in[0], w_attn_out[0], w_mlp_out[0], w_final.T,
    )
    velocity = uncond + guidance[0] * (cond - uncond)
    current = step_index[0].astype(F32)
    step_size = sigma_at(current + 1.0, STEPS) - sigma_at(current, STEPS)
    return velocity, latents + step_size * velocity, stream[None]


def solution(mesh):
    return jax.shard_map(
        on_device,
        mesh=mesh,
        in_specs=(
            P("cfg", ("tok", "mlp"), None, None),
            P(("tok", "mlp"), None, "cfg"),
            P("cfg", None, None),
            P(),
            P("cfg", None),
            P(),
            P(),
            P(None, ("tok", "mlp")),
            P(None, "cfg", None, "mlp"),
            P(None, "cfg", "mlp"),
            P(),
            P(None, "mlp", "cfg"),
            P(None, "mlp", "cfg"),
            P(),
        ),
        out_specs=(
            P(("tok", "mlp"), None, "cfg"),
            P(("tok", "mlp"), None, "cfg"),
            P("cfg", ("tok", "mlp"), None, None),
        ),
        check_vma=False,
    )
```
